32 devices in a mesh: ens: 4 (over x, core), space: 8 (over z, y).
Axes of the slice: x: 2, y: 2, z: 4, core: 2. Of those that a mesh axis runs over, the one named last changes fastest.
Arguments:
- checkpoints: bfloat16 [32, 2, 3, 256, 2048], P('ens', None, None, 'space'), may hold values from -6 to 6
- section_index: int32 [32], P('ens'), may hold values from 0 to 1
- targets: bfloat16 [32, 256, 2048], P('ens', 'space'), may hold values from -6 to 6
- sea_mask: int32 [256, 2048], P('space'), may hold values 0 or 1
- basis_rows: bfloat16 [256, 1024], P('space'), may hold values from -0.25 to 0.25
- basis_cols: bfloat16 [2048, 1024], replicated, may hold values from -0.1875 to 0.1875
- control: float32 [1024, 1024], P('space'), may hold values from -6 to 6
Outputs:
- control_next: float32 [1024, 1024], P('space')
The draws below stay inside these ranges and needn't reach their ends.
Inputs may be any that keep to these rules, and one draw needn't show every extreme that they name: `section_index`: selects one of the 2 slots.
All inputs are finite; a program needn't handle non-finite values. No bound on the sum of `sea_mask` on one device may be relied on, other than what follows from the above.
Results may differ from the reference program's by a relative error of at most 0.0014.
The reference program's roundings to bfloat16 on the way (of `coeffs` and `projected`) count: a program that leaves them out, or rounds other values in their place, can miss the bound.
Values may be sent and summed in bfloat16 or wider, within the bound.
No kernel may reach another device: no remote copies, remote signals or barrier semaphores. Data moves between devices by JAX's collectives and lax.ppermute only.
A program may use at most 128 MiB of HBM per device.

```python
import jax
import jax.numpy as jnp
from jax import lax

COLS = 2048
BASIS = 1024
SLOTS = 2
STATES = 32
NX = 256


def set_ends(result, stream_key, least, high):
    extent = result.shape
    index_at = [jax.random.randint(jax.random.fold_in(stream_key, axis), (), 0, extent[axis]) for axis in range(len(extent))]
    result = result.at[tuple(index_at)].set(least)
    longest = extent.index(max(extent))
    index_at[longest] = (index_at[longest] + 1) % extent[longest]
    return result.at[tuple(index_at)].set(high)


def strengthened(result, own_key, source, target, blocks, factor):
    owner, partner = [(jnp.arange(result.shape[axis_at]) // (result.shape[axis_at] // blocks)).reshape([-1 if axis == axis_at else 1 for axis in range(result.ndim)]) for axis_at in (source, target)]
    chosen = jax.random.permutation(own_key, blocks)[partner]
    strong = (owner == chosen) | (owner == (partner + blocks // 2) % blocks)
    return jnp.where(strong, factor * result, result)


def block_levels(rng, extent, shards, low, largest):
    def one(position, blocks):
        heights = jax.random.uniform(jax.random.fold_in(jax.random.fold_in(rng, 6), position), (blocks,), jnp.float32, low / len(shards), largest / len(shards))
        return jnp.repeat(jnp.exp(heights), extent[position] // blocks).reshape((-1,) + (1,) * (len(extent) - position - 1))

    factor_of = one(*shards[0])
    for cut in shards[1:]:
        factor_of = factor_of * one(*cut)
    return factor_of


def noise(key, dims, width, most, pieces=(), held_as=jnp.bfloat16):
    values = jax.random.normal(key, dims, jnp.float32) * width
    if len(pieces) > 0:
        values = block_levels(key, dims, pieces, -0.22, 0.18) * values
    return jnp.clip(values, min=-most, max=most).astype(held_as)


def noise_with(rng, dims, width, reach, cuts, heavy, kind=jnp.bfloat16):
    values = width * jax.random.normal(rng, dims, jnp.float32)
    if cuts:
        values = values * block_levels(rng, dims, cuts, -0.22, 0.18)
    return jnp.clip(strengthened(values, jax.random.fold_in(rng, 3), *heavy), -reach, reach).astype(kind)


def setup_inputs(seed: int = 0) -> dict:
    arg_keys = jax.random.split(jax.random.key(seed), 8)
    return {
        "checkpoints": noise(arg_keys[0], (STATES, SLOTS, 3, NX, COLS), 1.0, 6.0, ((0, 4), (3, 8))),
        "section_index": set_ends(jax.random.randint(arg_keys[1], (STATES,), 0, SLOTS), jax.random.fold_in(arg_keys[1], 1), 0, SLOTS - 1).astype(jnp.int32),
        "targets": noise(arg_keys[2], (STATES, NX, COLS), 1.0, 6.0, ((0, 4), (1, 8))),
        "sea_mask": set_ends((jax.random.randint(arg_keys[3], (NX, COLS), 0, 4) < 3).astype(jnp.int32), jax.random.fold_in(arg_keys[3], 1), 0, 1),
        "basis_rows": noise_with(arg_keys[4], (NX, BASIS), BASIS ** -0.5, 0.25, ((0, 8),), (0, 1, 8, 2.0)),
        "basis_cols": noise(arg_keys[5], (COLS, BASIS), BASIS ** -0.5, 0.1875),
        "control": noise(arg_keys[6], (BASIS, BASIS), 1.0, 6.0, ((0, 8),), jnp.float32),
    }


DEPTH = 1.0
GRAVITY = 1.0
CORIOLIS = 0.5
FRICTION = 0.1
TIME_STEP = 0.3
STEP_SIZE = 1.0
EPSILON = 1e-06

def across_columns(field):
    widths = [(0, 0)] * (field.ndim - 1) + [(1, 1)]
    padded = jnp.pad(field, widths)
    return 0.5 * (padded[..., 2:] - padded[..., :-2])

def across_rows(field):
    widths = [(0, 0)] * (field.ndim - 2) + [(1, 1), (0, 0)]
    padded = jnp.pad(field, widths)
    return 0.5 * (padded[..., 2:, :] - padded[..., :-2, :])

def height_change(height, east, north):
    return -(across_columns((DEPTH + height) * east) + across_rows((DEPTH + height) * north))

def reference(checkpoints, section_index, targets, sea_mask, basis_rows, basis_cols, control):
    coeffs = jnp.dot(basis_rows, control.astype(jnp.bfloat16), preferred_element_type=jnp.float32).astype(jnp.bfloat16)
    potential = lax.dot_general(coeffs, basis_cols, (((1,), (1,)), ((), ())), preferred_element_type=jnp.float32)
    sea = sea_mask.astype(jnp.float32)

    def one_state(total, item):
        stored, slot, observed = item
        chosen = slot == jnp.arange(SLOTS, dtype=jnp.int32)[:, None, None, None]
        start = lax.optimization_barrier(jnp.sum(jnp.where(chosen, stored, jnp.zeros_like(stored)), axis=0, dtype=jnp.float32))
        observed = observed.astype(jnp.float32)

        def misfit(field):
            stress_x = -across_rows(field)
            stress_y = across_columns(field)
            height_start, east_start, north_start = (start[0], start[1], start[2])
            change_height = height_change(height_start, east_start, north_start)
            change_east = CORIOLIS * north_start - GRAVITY * across_columns(height_start) - FRICTION * east_start + stress_x
            change_north = -CORIOLIS * east_start - GRAVITY * across_rows(height_start) - FRICTION * north_start + stress_y
            height_mid = sea * (height_start + TIME_STEP * change_height)
            east_mid = sea * (east_start + TIME_STEP * change_east)
            north_mid = sea * (north_start + TIME_STEP * change_north)
            change_mid = height_change(height_mid, east_mid, north_mid)
            height_end = sea * (0.5 * height_start + 0.5 * (height_mid + TIME_STEP * change_mid))
            differ = height_end - observed
            return 0.5 * jnp.sum(sea * differ * differ)
        value, pull = jax.vjp(misfit, potential)
        return (total + pull(jnp.ones_like(value))[0], None)
    zeros = jnp.zeros(potential.shape, jnp.float32)
    summed, _ = lax.scan(one_state, zeros, (checkpoints, section_index, targets))
    projected = jnp.dot(summed.astype(jnp.bfloat16), basis_cols, preferred_element_type=jnp.float32).astype(jnp.bfloat16)
    gradient = lax.dot_general(basis_rows, projected, (((0,), (0,)), ((), ())), preferred_element_type=jnp.float32)
    meansq = jnp.mean(gradient * gradient)
    return control - STEP_SIZE * gradient / jnp.sqrt(meansq + EPSILON)
```

```python
import jax
import jax.numpy as jnp
from jax import lax
from jax.sharding import PartitionSpec as P

DEPTH = 1.0
GRAVITY = 1.0
CORIOLIS = 0.5
FRICTION = 0.1
TIME_STEP = 0.3
STEP_SIZE = 1.0
EPSILON = 1e-06

F32 = jnp.float32
BF16 = jnp.bfloat16


def across_columns(field):
    widths = [(0, 0)] * (field.ndim - 1) + [(1, 1)]
    padded = jnp.pad(field, widths)
    return 0.5 * (padded[..., 2:] - padded[..., :-2])


def across_rows(field):
    return 0.5 * (field[..., 2:, :] - field[..., :-2, :])


def partner(value, bit):
    count = lax.axis_size("ens")
    return lax.ppermute(value, "ens", [(i, i ^ bit) for i in range(count)])


def edge_rows(pieces):
    count = lax.axis_size("space")
    up = [(i, i + 1) for i in range(count - 1)]
    down = [(i + 1, i) for i in range(count - 1)]
    last, first = [], []
    for value, width in pieces:
        rows = value.shape[-2]
        tail = value[..., rows - width :, :]
        head = value[..., :width, :]
        last.append(tail.reshape(-1))
        first.append(head.reshape(-1))
    before = lax.ppermute(jnp.concatenate(last), "space", up)
    after = lax.ppermute(jnp.concatenate(first), "space", down)
    out, at = [], 0
    for value, width in pieces:
        shape = value.shape[:-2] + (width, value.shape[-1])
        size = 1
        for n in shape:
            size *= n
        top = before[at : at + size].reshape(shape)
        bottom = after[at : at + size].reshape(shape)
        at += size
        out.append(jnp.concatenate([top, value, bottom], axis=-2))
    return out


def flux_change(height, east, north):
    flux_x = (DEPTH + height) * east
    flux_y = (DEPTH + height) * north
    return -(across_columns(flux_x[..., 1:-1, :]) + across_rows(flux_y))


def local_gradient(height, east, north, targets, sea, potential):
    stress_x = -across_rows(potential)
    stress_y = across_columns(potential)
    inner = height[..., 1:-1, :]
    change_height = -(
        across_columns((DEPTH + inner) * east) + across_rows((DEPTH + height) * north)
    )
    height_mid = sea * (inner + TIME_STEP * change_height)
    north_inner = north[..., 1:-1, :]
    change_north = (
        -CORIOLIS * east - GRAVITY * across_rows(height) - FRICTION * north_inner + stress_y
    )
    north_mid = sea * (north_inner + TIME_STEP * change_north)
    sea1 = sea[1:-1]
    east1 = east[..., 1:-1, :]
    change_east = (
        CORIOLIS * north_inner[..., 1:-1, :]
        - GRAVITY * across_columns(inner[..., 1:-1, :])
        - FRICTION * east1
        + stress_x
    )
    east_mid = sea1 * (east1 + TIME_STEP * change_east)
    mid1 = height_mid[..., 1:-1, :]
    change_mid = -(
        across_columns((DEPTH + mid1) * east_mid)
        + across_rows((DEPTH + height_mid) * north_mid)
    )
    height_end = sea1 * (0.5 * inner[..., 1:-1, :] + 0.5 * (mid1 + TIME_STEP * change_mid))
    adjoint = 0.5 * sea1 * (height_end - targets)
    weight = TIME_STEP * TIME_STEP * sea1 * (DEPTH + mid1)
    push_east = jnp.sum(weight * across_columns(adjoint), axis=0)
    push_north = jnp.sum(weight[..., 1:-1, :] * across_rows(adjoint), axis=0)
    return across_rows(push_east) - across_columns(push_north)


def on_device(checkpoints, section_index, targets, sea_mask, basis_rows, basis_cols, control):
    members = lax.axis_size("ens")
    slabs = lax.axis_size("space")
    member = lax.axis_index("ens")
    slab = lax.axis_index("space")
    core = member % 2
    rows_out, width = control.shape
    rows = basis_rows.shape[0]
    quarter = width // members

    own = lax.dynamic_slice_in_dim(control, member * quarter, quarter, 1).astype(BF16)
    spread = jnp.broadcast_to(own[None], (slabs, rows_out, quarter))
    control_part = lax.all_to_all(spread, "space", 0, 0).reshape(slabs * rows_out, quarter)

    half = width // 2
    own_basis = lax.dynamic_slice_in_dim(basis_rows, core * half, half, 1)
    spread = jnp.broadcast_to(own_basis[None], (slabs, rows, half))
    basis_half = lax.all_to_all(spread, "space", 0, 0).reshape(slabs * rows, half)
    other_half = partner(basis_half, 1)
    first_half = jnp.where(core == 0, basis_half, other_half)
    second_half = jnp.where(core == 0, other_half, basis_half)
    basis_all = jnp.concatenate([first_half, second_half], axis=1)

    slots = checkpoints.shape[1]
    chosen = section_index[:, None, None, None, None] == lax.broadcasted_iota(
        jnp.int32, (1, slots, 1, 1, 1), 1
    )
    start = jnp.sum(jnp.where(chosen, checkpoints, jnp.zeros_like(checkpoints)), axis=1)
    height, east, north, seen, sea, basis_ext = edge_rows(
        [
            (start[:, 0], 3),
            (start[:, 1], 2),
            (start[:, 2], 3),
            (targets, 1),
            (sea_mask.astype(BF16), 2),
            (basis_rows, 2),
        ]
    )

    coeffs_part = jnp.dot(basis_ext, control_part, preferred_element_type=F32).astype(BF16)
    near = partner(coeffs_part, 1)
    far = partner(coeffs_part, 2)
    both = partner(coeffs_part, 3)
    mine = jnp.stack([coeffs_part, near, far, both])
    coeffs = jnp.concatenate([mine[member ^ k] for k in range(members)], axis=1)
    potential = lax.dot_general(
        coeffs, basis_cols, (((1,), (1,)), ((), ())), preferred_element_type=F32
    )
    grad = local_gradient(
        height.astype(F32),
        east.astype(F32),
        north.astype(F32),
        seen.astype(F32),
        sea.astype(F32),
        potential,
    )

    pair = rows // 2
    single = rows // 4
    keep = lax.dynamic_slice_in_dim(grad, core * pair, pair, 0)
    give = lax.dynamic_slice_in_dim(grad, (1 - core) * pair, pair, 0)
    keep = keep + partner(give, 1)
    chip = member // 2
    own_sum = lax.dynamic_slice_in_dim(keep, chip * single, single, 0)
    give = lax.dynamic_slice_in_dim(keep, (1 - chip) * single, single, 0)
    own_sum = own_sum + partner(give, 2)

    projected = jnp.dot(own_sum.astype(BF16), basis_cols, preferred_element_type=F32).astype(BF16)
    halves = projected.reshape(single, 2, half).transpose(1, 0, 2)
    send = jnp.broadcast_to(
        halves[None, :, None], (members // 2, 2, slabs, single, half)
    ).reshape(members * slabs, single, half)
    got = lax.all_to_all(send, ("ens", "space"), 0, 0)
    got = got.reshape(members // 2, 2, slabs, single, half).transpose(2, 1, 0, 3, 4)
    projected_half = got.reshape(slabs * rows, half)

    gradient_half = lax.dot_general(
        basis_all, projected_half, (((0,), (0,)), ((), ())), preferred_element_type=F32
    )
    squares = jnp.sum(gradient_half * gradient_half)
    gradient_own = lax.dynamic_slice_in_dim(gradient_half, slab * rows_out, rows_out, 0)
    total = squares + partner(squares, 1)
    gradient_other = partner(gradient_own, 1)
    left = jnp.where(core == 0, gradient_own, gradient_other)
    right = jnp.where(core == 0, gradient_other, gradient_own)
    gradient_rows = jnp.concatenate([left, right], axis=1)
    return control - STEP_SIZE * gradient_rows / jnp.sqrt(total / (width * width) + EPSILON)


def solution(mesh):
    return jax.shard_map(
        on_device,
        mesh=mesh,
        in_specs=(
            P("ens", None, None, "space", None),
            P("ens"),
            P("ens", "space", None),
            P("space", None),
            P("space", None),
            P(),
            P("space", None),
        ),
        out_specs=P("space", None),
        check_vma=False,
    )
```

```python
import functools

import jax
import jax.numpy as jnp
from jax import lax
from jax.experimental import pallas as pl
from jax.experimental.pallas import tpu as pltpu
from jax.sharding import PartitionSpec as P

DEPTH = 1.0
GRAVITY = 1.0
CORIOLIS = 0.5
FRICTION = 0.1
TIME_STEP = 0.3
STEP_SIZE = 1.0
EPSILON = 1e-06

F32 = jnp.float32
BF16 = jnp.bfloat16
TILE = 8
LANES = 128
MIB = 1 << 20


VMEM = pl.BlockSpec(memory_space=pltpu.VMEM)
SMEM = pl.BlockSpec(memory_space=pltpu.SMEM)
HBM = pl.BlockSpec(memory_space=pl.ANY)


def limit(mib):
    return pltpu.CompilerParams(vmem_limit_bytes=mib * MIB)


def tile_rows(shape):
    return lax.broadcasted_iota(jnp.int32, shape, 0)


def shift_cols(field, step):
    count = field.shape[1]
    turned = pltpu.roll(field, (-step) % count, 1)
    lane = lax.broadcasted_iota(jnp.int32, (field.shape[0], LANES), 1)
    if step > 0:
        edge = jnp.where(lane >= LANES - step, 0.0, turned[:, count - LANES :])
        return jnp.concatenate([turned[:, : count - LANES], edge], axis=1)
    edge = jnp.where(lane < -step, 0.0, turned[:, :LANES])
    return jnp.concatenate([edge, turned[:, LANES:]], axis=1)


def shift_rows(field, step):
    return pltpu.roll(field, (-step) % field.shape[0], 0)


def dx(field):
    return shift_cols(field, 1) - shift_cols(field, -1)


def dy(field):
    return shift_rows(field, 1) - shift_rows(field, -1)


def pack_edges(index_ref, states_ref, targets_ref, sea_ref, basis_ref, up_ref, down_ref, last, first, seen, sems):
    count, _, _, rows, cols = states_ref.shape
    copies = []
    for s in range(count):
        slot = index_ref[s]
        for side, (buffer, row) in enumerate(((last, rows - TILE), (first, 0))):
            copy = pltpu.make_async_copy(
                states_ref.at[s, slot, :, pl.ds(row, TILE), :], buffer.at[s], sems.at[side, s]
            )
            copy.start()
            copies.append(copy)
    for side, row in enumerate((rows - TILE, 0)):
        copy = pltpu.make_async_copy(
            targets_ref.at[:, pl.ds(row, TILE), :], seen.at[side], sems.at[side, count]
        )
        copy.start()
        copies.append(copy)
    row = tile_rows((TILE, cols))
    width = basis_ref.shape[1]
    sea_last = sea_ref[rows - TILE :, :].astype(F32)
    sea_first = sea_ref[:TILE, :].astype(F32)
    basis_last = pltpu.roll(basis_ref[rows - TILE :, :].astype(F32), 4, 0)
    basis_first = pltpu.roll(basis_ref[:TILE, :].astype(F32), 2, 0)
    rest = jnp.zeros((TILE, cols - width), F32)
    up_ref[count + 1] = jnp.where(
        row >= 6, sea_last, jnp.concatenate([basis_last, rest], axis=1)
    ).astype(BF16)
    down_ref[count + 1] = jnp.where(
        row < 2, sea_first, jnp.concatenate([basis_first, rest], axis=1)
    ).astype(BF16)
    for copy in copies:
        copy.wait()
    targets_up = jnp.zeros((TILE, cols), F32)
    targets_down = jnp.zeros((TILE, cols), F32)
    for s in range(count):
        height, east, north = (last[s, f].astype(F32) for f in range(3))
        up_ref[s] = jnp.where(
            row >= 5, height, jnp.where(row >= 2, pltpu.roll(north, 5, 0), pltpu.roll(east, 2, 0))
        ).astype(BF16)
        height, east, north = (first[s, f].astype(F32) for f in range(3))
        down_ref[s] = jnp.where(
            row < 3, height, jnp.where(row < 6, pltpu.roll(north, 3, 0), pltpu.roll(east, 6, 0))
        ).astype(BF16)
        edge = seen[0, s].astype(F32)[TILE - 1 :, :]
        targets_up = jnp.where(row == s, edge, targets_up)
        edge = seen[1, s].astype(F32)[:1, :]
        targets_down = jnp.where(row == s, edge, targets_down)
    up_ref[count] = targets_up.astype(BF16)
    down_ref[count] = targets_down.astype(BF16)


def edge_messages(section_index, checkpoints, targets, sea_mask, basis_rows):
    count, _, fields, _, cols = checkpoints.shape
    shape = jax.ShapeDtypeStruct((count + 2, TILE, cols), BF16)
    return pl.pallas_call(
        pack_edges,
        name="pack_edges",
        out_shape=(shape, shape),
        in_specs=[SMEM, HBM, HBM, VMEM, VMEM],
        out_specs=(VMEM, VMEM),
        scratch_shapes=[
            pltpu.VMEM((count, fields, TILE, cols), BF16),
            pltpu.VMEM((count, fields, TILE, cols), BF16),
            pltpu.VMEM((2, count, TILE, cols), BF16),
            pltpu.SemaphoreType.DMA((2, count + 1)),
        ],
        compiler_params=limit(12),
    )(section_index, checkpoints, targets, sea_mask, basis_rows)


def pack_pieces(member_ref, control_ref, basis_ref, out_ref):
    quarter = out_ref.shape[2]
    at = pl.multiple_of(member_ref[0] * quarter, quarter)
    rows_out = control_ref.shape[0]
    own = control_ref[:, pl.ds(at, quarter)].astype(BF16)
    basis = basis_ref[:, pl.ds(at, quarter)]
    for k in range(out_ref.shape[0]):
        out_ref[k, :rows_out] = own
        out_ref[k, rows_out:] = basis


def pieces_for(member, control, basis_rows, slabs, quarter):
    rows = control.shape[0] + basis_rows.shape[0]
    return pl.pallas_call(
        pack_pieces,
        name="pack_pieces",
        out_shape=jax.ShapeDtypeStruct((slabs, rows, quarter), BF16),
        in_specs=[SMEM, VMEM, VMEM],
        out_specs=VMEM,
        compiler_params=limit(8),
    )(member.reshape(1), control, basis_rows)


def run_states(index_ref, state_ref, before_ref, after_ref, seen_before_ref, seen_after_ref, targets_ref, sea_ref, base_ref, pairs_ref, mask_ref, gx, gy, seen_edge):
    s = pl.program_id(0)
    rows, cols = sea_ref.shape
    row = tile_rows((TILE, cols))

    @pl.when(s == 0)
    def _():
        edge = jnp.where(
            row < 2,
            seen_after_ref[1].astype(F32),
            jnp.where(row >= 6, seen_before_ref[1].astype(F32), 0.0),
        )
        mask_ref[...] = jnp.concatenate([sea_ref[...].astype(F32), edge], axis=0)
        seen_edge[0] = seen_before_ref[0].astype(F32)
        seen_edge[1] = seen_after_ref[0].astype(F32)
        gx[...] = jnp.zeros_like(gx)
        gy[...] = jnp.zeros_like(gy)
        pairs_ref[...] = jnp.zeros_like(pairs_ref)

    mask = mask_ref[...]
    before = before_ref[0].astype(F32)
    after = after_ref[0].astype(F32)
    top = row < 4

    def extended(field, forward, back):
        edge = jnp.where(top, pltpu.roll(after, forward, 0), pltpu.roll(before, back, 0))
        return jnp.concatenate([state_ref[0, 0, field].astype(F32), edge], axis=0)

    height = jnp.concatenate(
        [state_ref[0, 0, 0].astype(F32), jnp.where(top, after, before)], axis=0
    )
    east = extended(1, 2, 6)
    north = extended(2, 5, 3)
    seen = jnp.concatenate(
        [
            targets_ref[0].astype(F32),
            jnp.where(top, seen_edge[1, pl.ds(s, 1), :], seen_edge[0, pl.ds(s, 1), :]),
        ],
        axis=0,
    )
    half = 0.5 * TIME_STEP
    keep = 1.0 - TIME_STEP * FRICTION
    deep = DEPTH + height
    height_mid = mask * (height - half * (dx(deep * east) + dy(deep * north)))
    east_mid = mask * (
        keep * east + TIME_STEP * CORIOLIS * north - half * GRAVITY * dx(height)
    )
    north_mid = mask * (
        keep * north - TIME_STEP * CORIOLIS * east - half * GRAVITY * dy(height)
    )
    deep = DEPTH + height_mid
    height_end = 0.5 * (height + height_mid) - 0.5 * half * (
        dx(deep * east_mid) + dy(deep * north_mid)
    )
    misfit = mask * (height_end - seen)
    weight = mask * deep
    gx[...] += weight * dx(misfit)
    gy[...] += weight * dy(misfit)
    beside = shift_cols(weight, 1)
    pairs_ref[0] += weight * weight
    pairs_ref[1] += weight * shift_cols(weight, 2)
    pairs_ref[2] += weight * shift_rows(weight, 2)
    pairs_ref[3] += weight * shift_rows(beside, 1)
    pairs_ref[4] += weight * shift_rows(beside, -1)

    @pl.when(s == pl.num_programs(0) - 1)
    def _():
        scale = 0.125 * TIME_STEP * TIME_STEP
        base_ref[...] = scale * (dy(gx[...]) - dx(gy[...]))


def states_pass(section_index, checkpoints, before, after, targets, sea_mask):
    count, _, fields, rows, cols = checkpoints.shape
    ring = rows + TILE
    field = jax.ShapeDtypeStruct((ring, cols), F32)
    edge = pl.BlockSpec((1, TILE, cols), lambda s, index: (s, 0, 0))
    shared = pl.BlockSpec((2, TILE, cols), lambda s, index: (count // 2, 0, 0))
    return pl.pallas_call(
        run_states,
        name="run_states",
        out_shape=(field, jax.ShapeDtypeStruct((5, ring, cols), F32), field),
        grid_spec=pltpu.PrefetchScalarGridSpec(
            num_scalar_prefetch=1,
            grid=(count,),
            in_specs=[
                pl.BlockSpec((1, 1, fields, rows, cols), lambda s, index: (s, index[s], 0, 0, 0)),
                edge,
                edge,
                shared,
                shared,
                pl.BlockSpec((1, rows, cols), lambda s, index: (s, 0, 0)),
                pl.BlockSpec((rows, cols), lambda s, index: (0, 0)),
            ],
            out_specs=(
                pl.BlockSpec((ring, cols), lambda s, index: (0, 0)),
                pl.BlockSpec((5, ring, cols), lambda s, index: (0, 0, 0)),
                pl.BlockSpec((ring, cols), lambda s, index: (0, 0)),
            ),
            scratch_shapes=[
                pltpu.VMEM((ring, cols), F32),
                pltpu.VMEM((ring, cols), F32),
                pltpu.VMEM((2, TILE, cols), F32),
            ],
        ),
        compiler_params=limit(32),
    )(section_index, checkpoints, before, after, before, after, targets, sea_mask)


def make_coeffs(basis_ref, before_ref, after_ref, pieces_ref, out_ref):
    slabs, both, quarter = pieces_ref.shape
    rows, width = basis_ref.shape
    rows_out = width // slabs
    row = tile_rows((TILE, width))
    after = pltpu.roll(after_ref[0, :, :width].astype(F32), 6, 0)
    before = pltpu.roll(before_ref[0, :, :width].astype(F32), 4, 0)
    edge = jnp.where(row < 2, after, jnp.where(row >= 6, before, 0.0))
    basis = jnp.concatenate([basis_ref[...].astype(F32), edge], axis=0).astype(BF16)
    part = pieces_ref[:, :rows_out, :].reshape(slabs * rows_out, quarter)
    out_ref[...] = jnp.dot(basis, part, preferred_element_type=F32).astype(BF16)


def coeffs_part(basis_rows, before, after, pieces):
    rows, width = basis_rows.shape
    last = before.shape[0] - 1
    edge = pl.BlockSpec((1, TILE, before.shape[2]), lambda i: (last, 0, 0))
    return pl.pallas_call(
        make_coeffs,
        name="make_coeffs",
        out_shape=jax.ShapeDtypeStruct((rows + TILE, pieces.shape[2]), BF16),
        grid=(1,),
        in_specs=[
            pl.BlockSpec((rows, width), lambda i: (0, 0)),
            edge,
            edge,
            pl.BlockSpec(pieces.shape, lambda i: (0, 0, 0)),
        ],
        out_specs=pl.BlockSpec((rows + TILE, pieces.shape[2]), lambda i: (0, 0)),
        compiler_params=limit(12),
    )(basis_rows, before, after, pieces)


def apply_potential(member_ref, own_ref, near_ref, far_ref, both_ref, cols_ref, base_ref, pairs_ref, mask_ref, keep_ref, give_ref, coeffs, total):
    member = member_ref[0]
    quarter = own_ref.shape[1]
    for bits, ref in enumerate((own_ref, near_ref, far_ref, both_ref)):
        at = pl.multiple_of((member ^ bits) * quarter, quarter)
        coeffs[:, pl.ds(at, quarter)] = ref[...]
    potential = lax.dot_general(
        coeffs[...], cols_ref[...], (((1,), (1,)), ((), ())), preferred_element_type=F32
    )
    sx = -dy(potential)
    sy = dx(potential)
    mask = mask_ref[...]
    same, two_x, two_y, up, down = (pairs_ref[k] for k in range(5))
    same_x = same * sx
    same_y = same * sy
    up_x = up * shift_rows(shift_cols(sx, 1), 1)
    up_y = up * shift_rows(shift_cols(sy, 1), 1)
    down_x = down * shift_rows(shift_cols(sx, 1), -1)
    down_y = down * shift_rows(shift_cols(sy, 1), -1)
    back_up_x = shift_rows(shift_cols(up * sx, -1), -1)
    back_up_y = shift_rows(shift_cols(up * sy, -1), -1)
    back_down_x = shift_rows(shift_cols(down * sx, -1), 1)
    back_down_y = shift_rows(shift_cols(down * sy, -1), 1)
    gx = shift_cols(mask, 1) * (
        two_x * shift_cols(sx, 2) - same_x + up_y - down_y
    ) - shift_cols(mask, -1) * (same_x - shift_cols(two_x * sx, -2) + back_down_y - back_up_y)
    gy = shift_rows(mask, 1) * (
        up_x - back_down_x + two_y * shift_rows(sy, 2) - same_y
    ) - shift_rows(mask, -1) * (down_x - back_up_x + same_y - shift_rows(two_y * sy, -2))
    scale = -(TIME_STEP**4) / 64.0
    grad = base_ref[...] + scale * (dy(gx) - dx(gy))
    pair = keep_ref.shape[0]
    total[...] = grad[: 2 * pair]
    core = member % 2
    keep_ref[...] = total[pl.ds(pl.multiple_of(core * pair, pair), pair), :]
    give_ref[...] = total[pl.ds(pl.multiple_of((1 - core) * pair, pair), pair), :]


def gradient_halves(member, parts, basis_cols, base, pairs, mask):
    ring, cols = base.shape
    pair = (ring - TILE) // 2
    half = jax.ShapeDtypeStruct((pair, cols), F32)
    return pl.pallas_call(
        apply_potential,
        name="apply_potential",
        out_shape=(half, half),
        in_specs=[SMEM] + [VMEM] * 8,
        out_specs=(VMEM, VMEM),
        scratch_shapes=[
            pltpu.VMEM((ring, basis_cols.shape[1]), BF16),
            pltpu.VMEM((2 * pair, cols), F32),
        ],
        compiler_params=limit(24),
    )(member.reshape(1), *parts, basis_cols, base, pairs, mask)


def project(own_ref, other_ref, cols_ref, out_ref):
    total = (own_ref[...] + other_ref[...]).astype(BF16)
    projected = jnp.dot(total, cols_ref[...], preferred_element_type=F32).astype(BF16)
    half = out_ref.shape[3]
    for core in range(2):
        part = projected[:, core * half : (core + 1) * half]
        for chip in range(out_ref.shape[0] // 2):
            for k in range(out_ref.shape[1]):
                out_ref[2 * chip + core, k] = part


def projected_pieces(own, other, basis_cols, members, slabs):
    single = own.shape[0]
    half = basis_cols.shape[1] // 2
    return pl.pallas_call(
        project,
        name="project",
        out_shape=jax.ShapeDtypeStruct((members, slabs, single, half), BF16),
        in_specs=[VMEM] * 3,
        out_specs=VMEM,
        compiler_params=limit(16),
    )(own, other, basis_cols)


def partner(value, bit):
    count = lax.axis_size("ens")
    return lax.ppermute(value, "ens", [(i, i ^ bit) for i in range(count)])


def on_device(checkpoints, section_index, targets, sea_mask, basis_rows, basis_cols, control):
    members = lax.axis_size("ens")
    slabs = lax.axis_size("space")
    member = lax.axis_index("ens").astype(jnp.int32)
    slab = lax.axis_index("space")
    core = member % 2
    chip = member // 2
    rows_out, width = control.shape
    rows = basis_rows.shape[0]
    quarter = width // members
    half = width // 2

    pieces = pieces_for(member, control, basis_rows, slabs, quarter)
    pieces = lax.all_to_all(pieces, "space", 0, 0)

    up, down = edge_messages(section_index, checkpoints, targets, sea_mask, basis_rows)
    before = lax.ppermute(up, "space", [(i, i + 1) for i in range(slabs - 1)])
    after = lax.ppermute(down, "space", [(i + 1, i) for i in range(slabs - 1)])
    base, pairs, mask = states_pass(
        section_index, checkpoints, before, after, targets, sea_mask
    )

    own = coeffs_part(basis_rows, before, after, pieces)
    parts = [own] + [partner(own, bits) for bits in (1, 2, 3)]
    keep, give = gradient_halves(member, parts, basis_cols, base, pairs, mask)

    keep = keep + partner(give, 1)
    single = rows // 4
    own_rows = lax.dynamic_slice_in_dim(keep, chip * single, single, 0)
    give = lax.dynamic_slice_in_dim(keep, (1 - chip) * single, single, 0)
    send = projected_pieces(own_rows, partner(give, 2), basis_cols, members, slabs)
    send = send.reshape(members * slabs, single, half)
    got = lax.all_to_all(send, ("ens", "space"), 0, 0)

    part = pieces[:, rows_out:, :].reshape(slabs * rows, quarter)
    part, _ = lax.optimization_barrier((part, send))
    far = partner(part, 2)
    low = jnp.where(chip == 0, part, far)
    high = jnp.where(chip == 0, far, part)
    near = partner(jnp.stack([low, high]), 1)
    columns = [
        jnp.where(core == 0, low, near[0]),
        jnp.where(core == 0, near[0], low),
        jnp.where(core == 0, high, near[1]),
        jnp.where(core == 0, near[1], high),
    ]
    basis_all = jnp.concatenate(columns, axis=1)

    got = got.reshape(members // 2, 2, slabs, single, half).transpose(2, 1, 0, 3, 4)
    projected_half = got.reshape(slabs * rows, half)
    gradient_half = lax.dot_general(
        basis_all, projected_half, (((0,), (0,)), ((), ())), preferred_element_type=F32
    )
    squares = jnp.sum(gradient_half * gradient_half)
    gradient_own = lax.dynamic_slice_in_dim(gradient_half, slab * rows_out, rows_out, 0)
    total = squares + partner(squares, 1)
    gradient_other = partner(gradient_own, 1)
    left = jnp.where(core == 0, gradient_own, gradient_other)
    right = jnp.where(core == 0, gradient_other, gradient_own)
    gradient_rows = jnp.concatenate([left, right], axis=1)
    return control - STEP_SIZE * gradient_rows / jnp.sqrt(total / (width * width) + EPSILON)


def solution(mesh):
    return jax.shard_map(
        on_device,
        mesh=mesh,
        in_specs=(
            P("ens", None, None, "space", None),
            P("ens"),
            P("ens", "space", None),
            P("space", None),
            P("space", None),
            P(),
            P("space", None),
        ),
        out_specs=P("space", None),
        check_vma=False,
    )
```

```python
import jax
import jax.numpy as jnp
from jax import lax
from jax.experimental import pallas as pl
from jax.experimental.pallas import tpu as pltpu
from jax.sharding import PartitionSpec as P


DEPTH = 1.0
GRAVITY = 1.0
CORIOLIS = 0.5
FRICTION = 0.1
TIME_STEP = 0.3
STEP_SIZE = 1.0
EPSILON = 1e-06

F32 = jnp.float32
BF16 = jnp.bfloat16
TILE = 8
LANES = 128
MIB = 1 << 20


VMEM = pl.BlockSpec(memory_space=pltpu.VMEM)
SMEM = pl.BlockSpec(memory_space=pltpu.SMEM)
HBM = pl.BlockSpec(memory_space=pltpu.HBM)


def limit(mib):
    return pltpu.CompilerParams(vmem_limit_bytes=mib * MIB)


def tile_rows(shape):
    return lax.broadcasted_iota(jnp.int32, shape, 0)


def shift_cols(field, step):
    count = field.shape[1]
    turned = pltpu.roll(field, (-step) % count, 1)
    lane = lax.broadcasted_iota(jnp.int32, (field.shape[0], LANES), 1)
    if step > 0:
        edge = jnp.where(lane >= LANES - step, 0.0, turned[:, count - LANES :])
        return jnp.concatenate([turned[:, : count - LANES], edge], axis=1)
    edge = jnp.where(lane < -step, 0.0, turned[:, :LANES])
    return jnp.concatenate([edge, turned[:, LANES:]], axis=1)


def shift_rows(field, step):
    return pltpu.roll(field, (-step) % field.shape[0], 0)


def dx(field):
    return shift_cols(field, 1) - shift_cols(field, -1)


def dy(field):
    return shift_rows(field, 1) - shift_rows(field, -1)


def pack(index_ref, member_ref, states_ref, targets_ref, sea_ref, basis_ref, control_ref, up_ref, down_ref, out_ref, rows_ref, last, first, seen, sea, basis, own, sems):
    count, _, _, rows, cols = states_ref.shape
    width = basis_ref.shape[1]
    rows_out = control_ref.shape[0]
    quarter = out_ref.shape[2]
    at = pl.multiple_of(member_ref[0] * quarter, quarter)

    def fetch(source, target, sem):
        copy = pltpu.make_async_copy(source, target, sem)
        copy.start()
        return copy

    states = []
    for s in range(count):
        slot = index_ref[s]
        for side, (buffer, row) in enumerate(((last, rows - TILE), (first, 0))):
            source = states_ref.at[s, slot, :, pl.ds(row, TILE), :]
            states.append(fetch(source, buffer.at[s], sems.at[side, s]))
    others = [
        fetch(targets_ref.at[:, pl.ds(rows - TILE, TILE), :], seen.at[0], sems.at[0, count]),
        fetch(targets_ref.at[:, pl.ds(0, TILE), :], seen.at[1], sems.at[1, count]),
        fetch(sea_ref.at[pl.ds(rows - TILE, TILE), :], sea.at[0], sems.at[0, count + 1]),
        fetch(sea_ref.at[pl.ds(0, TILE), :], sea.at[1], sems.at[1, count + 1]),
        fetch(basis_ref, basis, sems.at[0, count + 2]),
        fetch(control_ref.at[:, pl.ds(at, quarter)], own, sems.at[1, count + 2]),
    ]
    row = tile_rows((TILE, cols))
    for s in range(count):
        states[2 * s].wait()
        height, east, north = (last[s, f].astype(F32) for f in range(3))
        up_ref[s] = jnp.where(
            row >= 5, height, jnp.where(row >= 2, pltpu.roll(north, 5, 0), pltpu.roll(east, 2, 0))
        ).astype(BF16)
        states[2 * s + 1].wait()
        height, east, north = (first[s, f].astype(F32) for f in range(3))
        down_ref[s] = jnp.where(
            row < 3, height, jnp.where(row < 6, pltpu.roll(north, 3, 0), pltpu.roll(east, 6, 0))
        ).astype(BF16)
    for copy in others:
        copy.wait()
    targets_up = jnp.zeros((TILE, cols), F32)
    targets_down = jnp.zeros((TILE, cols), F32)
    for s in range(count):
        targets_up = jnp.where(row == s, seen[0, s].astype(F32)[TILE - 1 :, :], targets_up)
        targets_down = jnp.where(row == s, seen[1, s].astype(F32)[:1, :], targets_down)
    up_ref[count] = targets_up.astype(BF16)
    down_ref[count] = targets_down.astype(BF16)
    basis_last = pltpu.roll(basis[rows - TILE :, :].astype(F32), 4, 0)
    basis_first = pltpu.roll(basis[:TILE, :].astype(F32), 2, 0)
    rest = jnp.zeros((TILE, cols - width), F32)
    up_ref[count + 1] = jnp.where(
        row >= 6, sea[0].astype(F32), jnp.concatenate([basis_last, rest], axis=1)
    ).astype(BF16)
    down_ref[count + 1] = jnp.where(
        row < 2, sea[1].astype(F32), jnp.concatenate([basis_first, rest], axis=1)
    ).astype(BF16)
    part = own[...].astype(BF16)
    part_basis = basis[:, pl.ds(at, quarter)]
    rows_ref[...] = basis[...]
    for k in range(out_ref.shape[0]):
        out_ref[k, :rows_out] = part
        out_ref[k, rows_out:] = part_basis


def packed(section_index, member, checkpoints, targets, sea_mask, basis_rows, control, slabs, quarter):
    count, _, fields, rows, cols = checkpoints.shape
    rows_out, width = control.shape
    edges = jax.ShapeDtypeStruct((count + 2, TILE, cols), BF16)
    return pl.pallas_call(
        pack,
        name="pack",
        out_shape=(
            edges,
            edges,
            jax.ShapeDtypeStruct((slabs, rows_out + rows, quarter), BF16),
            jax.ShapeDtypeStruct((rows, width), BF16),
        ),
        in_specs=[SMEM, SMEM] + [HBM] * 5,
        out_specs=(VMEM, VMEM, VMEM, VMEM),
        scratch_shapes=[
            pltpu.VMEM((count, fields, TILE, cols), BF16),
            pltpu.VMEM((count, fields, TILE, cols), BF16),
            pltpu.VMEM((2, count, TILE, cols), BF16),
            pltpu.VMEM((2, TILE, cols), jnp.int32),
            pltpu.VMEM((rows, width), BF16),
            pltpu.VMEM((rows_out, quarter), F32),
            pltpu.SemaphoreType.DMA((2, count + 3)),
        ],
        compiler_params=limit(14),
    )(
        section_index,
        member.reshape(1),
        *map(in_hbm, (checkpoints, targets, sea_mask, basis_rows, control)),
    )


def hold(source_ref, out_ref, sem):
    copy = pltpu.make_async_copy(source_ref, out_ref, sem)
    copy.start()
    copy.wait()


def in_hbm(array):
    return pltpu.with_memory_space_constraint(array, pltpu.HBM)


def held(array):
    size = array.size * array.dtype.itemsize
    return pl.pallas_call(
        hold,
        name="hold",
        out_shape=jax.ShapeDtypeStruct(array.shape, array.dtype),
        in_specs=[HBM],
        out_specs=VMEM,
        scratch_shapes=[pltpu.SemaphoreType.DMA],
        compiler_params=limit(size // MIB + 2),
    )(in_hbm(array))


def run_states(index_ref, state_ref, before_ref, after_ref, seen_before_ref, seen_after_ref, targets_ref, sea_ref, base_ref, pairs_ref, out_mask_ref, mask_ref, gx, gy, seen_edge):
    s = pl.program_id(0)
    _, cols = sea_ref.shape
    row = tile_rows((TILE, cols))

    @pl.when(s == 0)
    def _():
        edge = jnp.where(
            row < 2,
            seen_after_ref[1].astype(F32),
            jnp.where(row >= 6, seen_before_ref[1].astype(F32), 0.0),
        )
        mask_ref[...] = jnp.concatenate([sea_ref[...].astype(F32), edge], axis=0)
        out_mask_ref[...] = mask_ref[...].astype(BF16)
        seen_edge[0] = seen_before_ref[0].astype(F32)
        seen_edge[1] = seen_after_ref[0].astype(F32)
        gx[...] = jnp.zeros_like(gx)
        gy[...] = jnp.zeros_like(gy)
        pairs_ref[...] = jnp.zeros_like(pairs_ref)

    mask = mask_ref[...]
    before = before_ref[0].astype(F32)
    after = after_ref[0].astype(F32)
    top = row < 4

    def extended(field, forward, back):
        edge = jnp.where(top, pltpu.roll(after, forward, 0), pltpu.roll(before, back, 0))
        return jnp.concatenate([state_ref[0, 0, field].astype(F32), edge], axis=0)

    height = jnp.concatenate(
        [state_ref[0, 0, 0].astype(F32), jnp.where(top, after, before)], axis=0
    )
    east = extended(1, 2, 6)
    north = extended(2, 5, 3)
    seen = jnp.concatenate(
        [
            targets_ref[0].astype(F32),
            jnp.where(top, seen_edge[1, pl.ds(s, 1), :], seen_edge[0, pl.ds(s, 1), :]),
        ],
        axis=0,
    )
    half = 0.5 * TIME_STEP
    keep = 1.0 - TIME_STEP * FRICTION
    deep = DEPTH + height
    height_mid = mask * (height - half * (dx(deep * east) + dy(deep * north)))
    east_mid = mask * (
        keep * east + TIME_STEP * CORIOLIS * north - half * GRAVITY * dx(height)
    )
    north_mid = mask * (
        keep * north - TIME_STEP * CORIOLIS * east - half * GRAVITY * dy(height)
    )
    deep = DEPTH + height_mid
    height_end = 0.5 * (height + height_mid) - 0.5 * half * (
        dx(deep * east_mid) + dy(deep * north_mid)
    )
    misfit = mask * (height_end - seen)
    weight = mask * deep
    gx[...] += weight * dx(misfit)
    gy[...] += weight * dy(misfit)
    beside = shift_cols(weight, 1)
    pairs_ref[0] += weight * weight
    pairs_ref[1] += weight * shift_cols(weight, 2)
    pairs_ref[2] += weight * shift_rows(weight, 2)
    pairs_ref[3] += weight * shift_rows(beside, 1)
    pairs_ref[4] += weight * shift_rows(beside, -1)

    @pl.when(s == pl.num_programs(0) - 1)
    def _():
        scale = 0.125 * TIME_STEP * TIME_STEP
        base_ref[...] = scale * (dy(gx[...]) - dx(gy[...]))


def states_pass(section_index, checkpoints, before, after, targets, sea_mask):
    count, _, fields, rows, cols = checkpoints.shape
    ring = rows + TILE
    field = jax.ShapeDtypeStruct((ring, cols), F32)
    edge = pl.BlockSpec((1, TILE, cols), lambda s, index: (s, 0, 0))
    shared = pl.BlockSpec((2, TILE, cols), lambda s, index: (count // 2, 0, 0))
    return pl.pallas_call(
        run_states,
        name="run_states",
        out_shape=(
            field,
            jax.ShapeDtypeStruct((5, ring, cols), F32),
            jax.ShapeDtypeStruct((ring, cols), BF16),
        ),
        grid_spec=pltpu.PrefetchScalarGridSpec(
            num_scalar_prefetch=1,
            grid=(count,),
            in_specs=[
                pl.BlockSpec((1, 1, fields, rows, cols), lambda s, index: (s, index[s], 0, 0, 0)),
                edge,
                edge,
                shared,
                shared,
                pl.BlockSpec((1, rows, cols), lambda s, index: (s, 0, 0)),
                pl.BlockSpec((rows, cols), lambda s, index: (0, 0)),
            ],
            out_specs=(
                pl.BlockSpec((ring, cols), lambda s, index: (0, 0)),
                pl.BlockSpec((5, ring, cols), lambda s, index: (0, 0, 0)),
                pl.BlockSpec((ring, cols), lambda s, index: (0, 0)),
            ),
            scratch_shapes=[
                pltpu.VMEM((ring, cols), F32),
                pltpu.VMEM((ring, cols), F32),
                pltpu.VMEM((ring, cols), F32),
                pltpu.VMEM((2, TILE, cols), F32),
            ],
        ),
        compiler_params=limit(32),
    )(
        section_index,
        in_hbm(checkpoints),
        before,
        after,
        before,
        after,
        in_hbm(targets),
        sea_mask,
    )


def make_coeffs(basis_ref, before_ref, after_ref, pieces_ref, out_ref):
    slabs, _, quarter = pieces_ref.shape
    _, width = basis_ref.shape
    rows_out = width // slabs
    row = tile_rows((TILE, width))
    after = pltpu.roll(after_ref[0, :, :width].astype(F32), 6, 0)
    before = pltpu.roll(before_ref[0, :, :width].astype(F32), 4, 0)
    edge = jnp.where(row < 2, after, jnp.where(row >= 6, before, 0.0))
    basis = jnp.concatenate([basis_ref[...].astype(F32), edge], axis=0).astype(BF16)
    part = pieces_ref[:, :rows_out, :].reshape(slabs * rows_out, quarter)
    out_ref[...] = jnp.dot(basis, part, preferred_element_type=F32).astype(BF16)


def coeffs_part(basis_rows, before, after, pieces):
    rows, width = basis_rows.shape
    last = before.shape[0] - 1
    edge = pl.BlockSpec((1, TILE, before.shape[2]), lambda i: (last, 0, 0))
    return pl.pallas_call(
        make_coeffs,
        name="make_coeffs",
        out_shape=jax.ShapeDtypeStruct((rows + TILE, pieces.shape[2]), BF16),
        grid=(1,),
        in_specs=[
            pl.BlockSpec((rows, width), lambda i: (0, 0)),
            edge,
            edge,
            pl.BlockSpec(pieces.shape, lambda i: (0, 0, 0)),
        ],
        out_specs=pl.BlockSpec((rows + TILE, pieces.shape[2]), lambda i: (0, 0)),
        compiler_params=limit(12),
    )(basis_rows, before, after, pieces)


def apply_potential(member_ref, own_ref, near_ref, far_ref, both_ref, cols_ref, base_ref, pairs_ref, mask_ref, keep_ref, give_ref, coeffs, total, held_cols, field, sems):
    member = member_ref[0]
    blocks = held_cols.shape[0]
    block = held_cols.shape[1]
    copies = []
    for k in range(blocks):
        copy = pltpu.make_async_copy(
            cols_ref.at[pl.ds(k * block, block), :], held_cols.at[k], sems.at[k]
        )
        copy.start()
        copies.append(copy)
    quarter = own_ref.shape[1]
    for bits, ref in enumerate((own_ref, near_ref, far_ref, both_ref)):
        at = pl.multiple_of((member ^ bits) * quarter, quarter)
        coeffs[:, pl.ds(at, quarter)] = ref[...]
    for k, copy in enumerate(copies):
        copy.wait()
        field[:, k * block : (k + 1) * block] = lax.dot_general(
            coeffs[...], held_cols[k], (((1,), (1,)), ((), ())), preferred_element_type=F32
        )
    potential = field[...]
    sx = -dy(potential)
    sy = dx(potential)
    mask = mask_ref[...].astype(F32)
    same, two_x, two_y, up, down = (pairs_ref[k] for k in range(5))
    same_x = same * sx
    same_y = same * sy
    up_x = up * shift_rows(shift_cols(sx, 1), 1)
    up_y = up * shift_rows(shift_cols(sy, 1), 1)
    down_x = down * shift_rows(shift_cols(sx, 1), -1)
    down_y = down * shift_rows(shift_cols(sy, 1), -1)
    back_up_x = shift_rows(shift_cols(up * sx, -1), -1)
    back_up_y = shift_rows(shift_cols(up * sy, -1), -1)
    back_down_x = shift_rows(shift_cols(down * sx, -1), 1)
    back_down_y = shift_rows(shift_cols(down * sy, -1), 1)
    gx = shift_cols(mask, 1) * (
        two_x * shift_cols(sx, 2) - same_x + up_y - down_y
    ) - shift_cols(mask, -1) * (same_x - shift_cols(two_x * sx, -2) + back_down_y - back_up_y)
    gy = shift_rows(mask, 1) * (
        up_x - back_down_x + two_y * shift_rows(sy, 2) - same_y
    ) - shift_rows(mask, -1) * (down_x - back_up_x + same_y - shift_rows(two_y * sy, -2))
    scale = -(TIME_STEP**4) / 64.0
    grad = base_ref[...] + scale * (dy(gx) - dx(gy))
    pair = keep_ref.shape[0]
    total[...] = grad[: 2 * pair]
    core = member % 2
    keep_ref[...] = total[pl.ds(pl.multiple_of(core * pair, pair), pair), :]
    give_ref[...] = total[pl.ds(pl.multiple_of((1 - core) * pair, pair), pair), :]


def gradient_halves(member, parts, basis_cols, base, pairs, mask):
    ring, cols = base.shape
    width = basis_cols.shape[1]
    pair = (ring - TILE) // 2
    half = jax.ShapeDtypeStruct((pair, cols), F32)
    return pl.pallas_call(
        apply_potential,
        name="apply_potential",
        out_shape=(half, half),
        in_specs=[SMEM] + [VMEM] * 4 + [HBM] + [VMEM] * 3,
        out_specs=(VMEM, VMEM),
        scratch_shapes=[
            pltpu.VMEM((ring, width), BF16),
            pltpu.VMEM((2 * pair, cols), F32),
            pltpu.VMEM((4, cols // 4, width), BF16),
            pltpu.VMEM((ring, cols), F32),
            pltpu.SemaphoreType.DMA((4,)),
        ],
        compiler_params=limit(24),
    )(member.reshape(1), *parts, in_hbm(basis_cols), base, pairs, mask)


def project(own_ref, other_ref, cols_ref, out_ref):
    total = (own_ref[...] + other_ref[...]).astype(BF16)
    projected = jnp.dot(total, cols_ref[...], preferred_element_type=F32).astype(BF16)
    half = out_ref.shape[3]
    for core in range(2):
        part = projected[:, core * half : (core + 1) * half]
        for chip in range(out_ref.shape[0] // 2):
            for k in range(out_ref.shape[1]):
                out_ref[2 * chip + core, k] = part


def projected_pieces(own, other, basis_cols, members, slabs):
    single = own.shape[0]
    half = basis_cols.shape[1] // 2
    return pl.pallas_call(
        project,
        name="project",
        out_shape=jax.ShapeDtypeStruct((members, slabs, single, half), BF16),
        in_specs=[VMEM] * 3,
        out_specs=VMEM,
        compiler_params=limit(16),
    )(own, other, basis_cols)


def assemble(member_ref, own_ref, far_ref, near_ref, control_ref, basis_ref, kept_ref, sem):
    copy = pltpu.make_async_copy(control_ref, kept_ref, sem)
    copy.start()
    member = member_ref[0]
    quarter = own_ref.shape[1]
    parts = (own_ref[...], near_ref[0], far_ref[...], near_ref[1])
    for bits, part in enumerate(parts):
        at = pl.multiple_of((member ^ bits) * quarter, quarter)
        basis_ref[pl.ds(at, quarter), :] = part.astype(F32).T.astype(BF16)
    copy.wait()


def assembled(member, own, far, near, control):
    rows, _ = own.shape
    width = control.shape[1]
    return pl.pallas_call(
        assemble,
        name="assemble",
        out_shape=(
            jax.ShapeDtypeStruct((width, rows), BF16),
            jax.ShapeDtypeStruct(control.shape, F32),
        ),
        in_specs=[SMEM, VMEM, VMEM, VMEM, HBM],
        out_specs=(VMEM, VMEM),
        scratch_shapes=[pltpu.SemaphoreType.DMA],
        compiler_params=limit(24),
    )(member.reshape(1), own, far, near, in_hbm(control))


def gradient(slab_ref, basis_ref, projected_ref, out_ref):
    rows_out = out_ref.shape[0] - TILE
    width = basis_ref.shape[0]
    half = out_ref.shape[1]
    projected = projected_ref[...]
    block = width // 4
    squares = jnp.zeros((TILE, half), F32)
    for k in range(4):
        part = jnp.dot(
            basis_ref[k * block : (k + 1) * block, :], projected, preferred_element_type=F32
        )
        squares += jnp.sum((part * part).reshape(block // TILE, TILE, half), axis=0)
    at = pl.multiple_of(slab_ref[0] * rows_out, rows_out)
    out_ref[:rows_out] = jnp.dot(
        basis_ref[pl.ds(at, rows_out), :], projected, preferred_element_type=F32
    )
    out_ref[rows_out:] = squares


def gradient_block(slab, basis, projected, rows_out):
    half = projected.shape[1]
    return pl.pallas_call(
        gradient,
        name="gradient",
        out_shape=jax.ShapeDtypeStruct((rows_out + TILE, half), F32),
        in_specs=[SMEM, VMEM, VMEM],
        out_specs=VMEM,
        compiler_params=limit(24),
    )(slab.reshape(1), basis, projected)


def update(core_ref, control_ref, own_ref, other_ref, out_ref):
    rows_out, width = control_ref.shape
    half = width // 2
    total = jnp.sum(own_ref[rows_out:] + other_ref[rows_out:])
    scale = STEP_SIZE * lax.rsqrt(total / (width * width) + EPSILON)
    for turn, ref in enumerate((own_ref, other_ref)):
        at = pl.multiple_of((core_ref[0] ^ turn) * half, half)
        out_ref[:, pl.ds(at, half)] = control_ref[:, pl.ds(at, half)] - ref[:rows_out] * scale


def updated(core, control, own, other):
    return pl.pallas_call(
        update,
        name="update",
        out_shape=jax.ShapeDtypeStruct(control.shape, F32),
        in_specs=[SMEM, VMEM, VMEM, VMEM],
        out_specs=VMEM,
        compiler_params=limit(8),
    )(core.reshape(1), control, own, other)


def partner(value, bit):
    count = lax.axis_size("ens")
    return lax.ppermute(value, "ens", [(i, i ^ bit) for i in range(count)])


def on_device(checkpoints, section_index, targets, sea_mask, basis_rows, basis_cols, control):
    members = lax.axis_size("ens")
    slabs = lax.axis_size("space")
    member = lax.axis_index("ens").astype(jnp.int32)
    slab = lax.axis_index("space").astype(jnp.int32)
    core = member & 1
    chip = member >> 1
    rows_out, width = control.shape
    rows = basis_rows.shape[0]
    quarter = width // members
    half = width // 2
    single = rows // 4

    up, down, pieces, near_rows = packed(
        section_index, member, checkpoints, targets, sea_mask, basis_rows, control, slabs, quarter
    )
    before = lax.ppermute(up, "space", [(i, i + 1) for i in range(slabs - 1)])
    after = lax.ppermute(down, "space", [(i + 1, i) for i in range(slabs - 1)])
    pieces = lax.all_to_all(pieces, "space", 0, 0)
    base, pairs, mask = states_pass(section_index, checkpoints, before, after, targets, sea_mask)
    own = coeffs_part(near_rows, before, after, pieces)
    parts = [own] + [partner(own, bits) for bits in (1, 2, 3)]
    keep, give = gradient_halves(member, parts, basis_cols, base, pairs, mask)

    keep = keep + partner(give, 1)
    own_rows = lax.dynamic_slice_in_dim(keep, chip * single, single, 0)
    give = lax.dynamic_slice_in_dim(keep, (1 - chip) * single, single, 0)
    arriving = partner(give, 2)
    cols = held(basis_cols)
    send = projected_pieces(own_rows, arriving, cols, members, slabs)
    got = lax.all_to_all(send.reshape(members * slabs, single, half), ("ens", "space"), 0, 0)
    projected_half = got.reshape(slabs * rows, half)

    part = pieces[:, rows_out:, :].reshape(slabs, 2, members // 2, single, quarter)
    part = part.transpose(2, 1, 0, 3, 4).reshape(slabs * rows, quarter)
    far = partner(part, 2)
    near = partner(jnp.stack([part, far]), 1)
    basis, kept = assembled(member, part, far, near, control)
    block = gradient_block(slab, basis, projected_half, rows_out)
    other = partner(block, 1)
    return updated(core, kept, block, other)


def solution(mesh):
    return jax.shard_map(
        on_device,
        mesh=mesh,
        in_specs=(
            P("ens", None, None, "space", None),
            P("ens"),
            P("ens", "space", None),
            P("space", None),
            P("space", None),
            P(),
            P("space", None),
        ),
        out_specs=P("space", None),
        check_vma=False,
    )
```

```python
import jax
import jax.numpy as jnp
from jax import lax
from jax.experimental import pallas as pl
from jax.experimental.pallas import tpu as pltpu
from jax.sharding import PartitionSpec as P


DEPTH = 1.0
GRAVITY = 1.0
CORIOLIS = 0.5
FRICTION = 0.1
TIME_STEP = 0.3
STEP_SIZE = 1.0
EPSILON = 1e-06

F32 = jnp.float32
BF16 = jnp.bfloat16
TILE = 8
LANES = 128
MIB = 1 << 20


VMEM = pl.BlockSpec(memory_space=pltpu.VMEM)
SMEM = pl.BlockSpec(memory_space=pltpu.SMEM)
HBM = pl.BlockSpec(memory_space=pltpu.HBM)


def limit(mib):
    return pltpu.CompilerParams(vmem_limit_bytes=mib * MIB)


def tile_rows(shape):
    return lax.broadcasted_iota(jnp.int32, shape, 0)


def split_lanes(field):
    return jnp.stack([field[:, k : k + LANES] for k in range(0, field.shape[1], LANES)])


def join_lanes(field):
    return jnp.concatenate([field[k] for k in range(field.shape[0])], axis=1)


def shift_cols(field, step):
    turned = pltpu.roll(field, (-step) % LANES, 2)
    lane = lax.broadcasted_iota(jnp.int32, field.shape, 2)
    outside = jnp.zeros_like(turned[:1])
    if step > 0:
        beside = jnp.concatenate([turned[1:], outside], axis=0)
        return jnp.where(lane >= LANES - step, beside, turned)
    beside = jnp.concatenate([outside, turned[:-1]], axis=0)
    return jnp.where(lane < -step, beside, turned)


def shift_rows(field, step):
    return pltpu.roll(field, (-step) % field.shape[1], 1)


def dx(field):
    return shift_cols(field, 1) - shift_cols(field, -1)


def dy(field):
    return shift_rows(field, 1) - shift_rows(field, -1)


def pack(index_ref, member_ref, states_ref, targets_ref, sea_ref, basis_ref, control_ref, up_ref, down_ref, out_ref, last, first, seen, sea, basis, own, sems):
    count, _, _, rows, cols = states_ref.shape
    width = basis_ref.shape[1]
    rows_out = control_ref.shape[0]
    quarter = out_ref.shape[2]
    at = pl.multiple_of(member_ref[0] * quarter, quarter)

    def fetch(source, target, sem):
        copy = pltpu.make_async_copy(source, target, sem)
        copy.start()
        return copy

    states = []
    for s in range(count):
        slot = index_ref[s]
        for side, (buffer, row) in enumerate(((last, rows - TILE), (first, 0))):
            source = states_ref.at[s, slot, :, pl.ds(row, TILE), :]
            states.append(fetch(source, buffer.at[s], sems.at[side, s]))
    others = [
        fetch(targets_ref.at[:, pl.ds(rows - TILE, TILE), :], seen.at[0], sems.at[0, count]),
        fetch(targets_ref.at[:, pl.ds(0, TILE), :], seen.at[1], sems.at[1, count]),
        fetch(sea_ref.at[pl.ds(rows - TILE, TILE), :], sea.at[0], sems.at[0, count + 1]),
        fetch(sea_ref.at[pl.ds(0, TILE), :], sea.at[1], sems.at[1, count + 1]),
        fetch(basis_ref, basis, sems.at[0, count + 2]),
        fetch(control_ref.at[:, pl.ds(at, quarter)], own, sems.at[1, count + 2]),
    ]
    row = tile_rows((TILE, cols))
    for s in range(count):
        states[2 * s].wait()
        height, east, north = (last[s, f].astype(F32) for f in range(3))
        up_ref[s] = jnp.where(
            row >= 5, height, jnp.where(row >= 2, pltpu.roll(north, 5, 0), pltpu.roll(east, 2, 0))
        ).astype(BF16)
        states[2 * s + 1].wait()
        height, east, north = (first[s, f].astype(F32) for f in range(3))
        down_ref[s] = jnp.where(
            row < 3, height, jnp.where(row < 6, pltpu.roll(north, 3, 0), pltpu.roll(east, 6, 0))
        ).astype(BF16)
    for copy in others:
        copy.wait()
    targets_up = jnp.zeros((TILE, cols), F32)
    targets_down = jnp.zeros((TILE, cols), F32)
    for s in range(count):
        targets_up = jnp.where(row == s, seen[0, s].astype(F32)[TILE - 1 :, :], targets_up)
        targets_down = jnp.where(row == s, seen[1, s].astype(F32)[:1, :], targets_down)
    up_ref[count] = targets_up.astype(BF16)
    down_ref[count] = targets_down.astype(BF16)
    basis_last = pltpu.roll(basis[rows - TILE :, :].astype(F32), 4, 0)
    basis_first = pltpu.roll(basis[:TILE, :].astype(F32), 2, 0)
    rest = jnp.zeros((TILE, cols - width), F32)
    up_ref[count + 1] = jnp.where(
        row >= 6, sea[0].astype(F32), jnp.concatenate([basis_last, rest], axis=1)
    ).astype(BF16)
    down_ref[count + 1] = jnp.where(
        row < 2, sea[1].astype(F32), jnp.concatenate([basis_first, rest], axis=1)
    ).astype(BF16)
    part = own[...].astype(BF16)
    part_basis = basis[:, pl.ds(at, quarter)]
    for k in range(out_ref.shape[0]):
        out_ref[k, :rows_out] = part
        out_ref[k, rows_out:] = part_basis


def packed(section_index, member, checkpoints, targets, sea_mask, basis_rows, control, slabs, quarter):
    count, _, fields, rows, cols = checkpoints.shape
    rows_out, width = control.shape
    edges = jax.ShapeDtypeStruct((count + 2, TILE, cols), BF16)
    return pl.pallas_call(
        pack,
        name="pack",
        out_shape=(
            edges,
            edges,
            jax.ShapeDtypeStruct((slabs, rows_out + rows, quarter), BF16),
        ),
        in_specs=[SMEM, SMEM] + [HBM] * 5,
        out_specs=(VMEM, VMEM, VMEM),
        scratch_shapes=[
            pltpu.VMEM((count, fields, TILE, cols), BF16),
            pltpu.VMEM((count, fields, TILE, cols), BF16),
            pltpu.VMEM((2, count, TILE, cols), BF16),
            pltpu.VMEM((2, TILE, cols), jnp.int32),
            pltpu.VMEM((rows, width), BF16),
            pltpu.VMEM((rows_out, quarter), F32),
            pltpu.SemaphoreType.DMA((2, count + 3)),
        ],
        compiler_params=limit(14),
    )(
        in_hbm(section_index),
        member.reshape(1),
        *map(in_hbm, (checkpoints, targets, sea_mask, basis_rows, control)),
    )


def hold(source_ref, out_ref, sem):
    copy = pltpu.make_async_copy(source_ref, out_ref, sem)
    copy.start()
    copy.wait()


def in_hbm(array):
    return pltpu.with_memory_space_constraint(array, pltpu.HBM)


def held(array):
    size = array.size * array.dtype.itemsize
    return pl.pallas_call(
        hold,
        out_shape=jax.ShapeDtypeStruct(array.shape, array.dtype),
        in_specs=[HBM],
        out_specs=VMEM,
        scratch_shapes=[pltpu.SemaphoreType.DMA],
        compiler_params=limit(size // MIB + 2),
    )(in_hbm(array))


def run_states(index_ref, state_ref, before_ref, after_ref, shared_before_ref, shared_after_ref, targets_ref, sea_ref, basis_ref, base_ref, pairs_ref, mask_ref, rows_ref, mask, seen_edge, heights, fluxes, mid_fluxes, weights, besides, misfits, partial, gx, gy):
    s = pl.program_id(0)
    rows, cols = sea_ref.shape
    width = basis_ref.shape[1]
    tiles = rows // TILE + 1
    row = tile_rows((TILE, cols))
    top = row < 4

    def put(ref, tile, value):
        ref[:, TILE * (tile + 1) : TILE * (tile + 2), :] = value
        if tile == tiles - 1:
            ref[:, :TILE, :] = value
        if tile == 0:
            ref[:, TILE * (tiles + 1) :, :] = value

    def get(ref, tile, step=0):
        start = TILE * (tile + 1) + step
        return ref[:, start : start + TILE, :]

    def rows_of(tile):
        return slice(TILE * tile, TILE * (tile + 1))

    @pl.when(s == 0)
    def _():
        after = shared_after_ref[1].astype(F32)
        before = shared_before_ref[1].astype(F32)
        edge = jnp.where(row < 2, after, jnp.where(row >= 6, before, 0.0))
        for tile in range(tiles - 1):
            mask[:, rows_of(tile), :] = split_lanes(sea_ref[rows_of(tile), :].astype(F32))
        mask[:, rows:, :] = split_lanes(edge)
        mask_ref[...] = mask[...].astype(BF16)
        seen_edge[0] = shared_before_ref[0].astype(F32)
        seen_edge[1] = shared_after_ref[0].astype(F32)
        gx[...] = jnp.zeros_like(gx)
        gy[...] = jnp.zeros_like(gy)
        pairs_ref[...] = jnp.zeros_like(pairs_ref)
        after = pltpu.roll(after[:, :width], 6, 0)
        before = pltpu.roll(before[:, :width], 4, 0)
        edge = jnp.where(row[:, :width] < 2, after, jnp.where(row[:, :width] >= 6, before, 0.0))
        rows_ref[...] = jnp.concatenate(
            [basis_ref[...].astype(F32), edge], axis=0
        ).astype(BF16)

    after = after_ref[0].astype(F32)
    before = before_ref[0].astype(F32)
    edges = (
        jnp.where(top, after, before),
        jnp.where(top, pltpu.roll(after, 2, 0), pltpu.roll(before, 6, 0)),
        jnp.where(top, pltpu.roll(after, 5, 0), pltpu.roll(before, 3, 0)),
    )

    def load(field, tile):
        if tile == tiles - 1:
            return split_lanes(edges[field])
        return split_lanes(state_ref[0, 0, field, rows_of(tile), :].astype(F32))

    half = 0.5 * TIME_STEP
    keep = 1.0 - TIME_STEP * FRICTION
    turn = TIME_STEP * CORIOLIS / keep
    slope = half * GRAVITY / keep

    for tile in range(tiles):
        height = load(0, tile)
        put(heights, tile, height)
        put(fluxes, tile, (DEPTH + height) * load(2, tile))

    for tile in range(tiles):
        height = get(heights, tile)
        east = load(1, tile)
        north = load(2, tile)
        flux = dx((DEPTH + height) * east) + (get(fluxes, tile, 1) - get(fluxes, tile, -1))
        sea = mask[:, rows_of(tile), :]
        height_mid = sea * (height - half * flux)
        weight = DEPTH * sea + height_mid
        east_mid = east + turn * north - slope * dx(height)
        north_mid = (
            north - turn * east - slope * (get(heights, tile, 1) - get(heights, tile, -1))
        )
        if tile == tiles - 1:
            seen = split_lanes(
                jnp.where(top, seen_edge[1, pl.ds(s, 1), :], seen_edge[0, pl.ds(s, 1), :])
            )
        else:
            seen = split_lanes(targets_ref[0, rows_of(tile), :].astype(F32))
        put(mid_fluxes, tile, weight * north_mid)
        put(weights, tile, weight)
        put(besides, tile, shift_cols(weight, 1))
        partial[:, rows_of(tile), :] = (
            height + height_mid - 2.0 * seen - half * keep * dx(weight * east_mid)
        )

    for tile in range(tiles):
        change = get(mid_fluxes, tile, 1) - get(mid_fluxes, tile, -1)
        misfit = mask[:, rows_of(tile), :] * (
            partial[:, rows_of(tile), :] - half * keep * change
        )
        put(misfits, tile, misfit)
        gx[:, rows_of(tile), :] += get(weights, tile) * dx(misfit)

    for tile in range(tiles):
        here = rows_of(tile)
        weight = get(weights, tile)
        gy[:, here, :] += weight * (get(misfits, tile, 1) - get(misfits, tile, -1))
        pairs_ref[0, :, here, :] += weight * weight
        pairs_ref[1, :, here, :] += weight * shift_cols(weight, 2)
        pairs_ref[2, :, here, :] += weight * get(weights, tile, 2)
        pairs_ref[3, :, here, :] += weight * get(besides, tile, 1)
        pairs_ref[4, :, here, :] += weight * get(besides, tile, -1)

    @pl.when(s == pl.num_programs(0) - 1)
    def _():
        scale = 0.0625 * TIME_STEP * TIME_STEP
        base_ref[...] = scale * (dy(gx[...]) - dx(gy[...]))


def states_pass(section_index, checkpoints, before, after, targets, sea_mask, basis_rows):
    count, _, fields, rows, cols = checkpoints.shape
    width = basis_rows.shape[1]
    ring = rows + TILE
    lanes = cols // LANES
    padded = pltpu.VMEM((lanes, ring + 2 * TILE, LANES), F32)
    plain = pltpu.VMEM((lanes, ring, LANES), F32)
    edge = pl.BlockSpec((1, TILE, cols), lambda s, index: (s, 0, 0))
    shared = pl.BlockSpec((2, TILE, cols), lambda s, index: (count // 2, 0, 0))
    outs = (
        jax.ShapeDtypeStruct((lanes, ring, LANES), F32),
        jax.ShapeDtypeStruct((5, lanes, ring, LANES), F32),
        jax.ShapeDtypeStruct((lanes, ring, LANES), BF16),
        jax.ShapeDtypeStruct((ring, width), BF16),
    )
    return pl.pallas_call(
        run_states,
        name="run_states",
        out_shape=outs,
        grid_spec=pltpu.PrefetchScalarGridSpec(
            num_scalar_prefetch=1,
            grid=(count,),
            in_specs=[
                pl.BlockSpec((1, 1, fields, rows, cols), lambda s, index: (s, index[s], 0, 0, 0)),
                edge,
                edge,
                shared,
                shared,
                pl.BlockSpec((1, rows, cols), lambda s, index: (s, 0, 0)),
                pl.BlockSpec((rows, cols), lambda s, index: (0, 0)),
                pl.BlockSpec((rows, width), lambda s, index: (0, 0)),
            ],
            out_specs=tuple(
                pl.BlockSpec(out.shape, lambda s, index, n=len(out.shape): (0,) * n) for out in outs
            ),
            scratch_shapes=[plain, pltpu.VMEM((2, TILE, cols), F32)]
            + [padded] * 6
            + [plain] * 3,
        ),
        compiler_params=limit(20),
    )(
        section_index,
        in_hbm(checkpoints),
        before,
        after,
        before,
        after,
        in_hbm(targets),
        in_hbm(sea_mask),
        in_hbm(basis_rows),
    )


def make_coeffs(basis_ref, pieces_ref, out_ref):
    slabs, _, quarter = pieces_ref.shape
    width = basis_ref.shape[1]
    part = pieces_ref[:, : width // slabs, :].reshape(width, quarter)
    out_ref[...] = jnp.dot(basis_ref[...], part, preferred_element_type=F32).astype(BF16)


def coeffs_part(basis, pieces):
    return pl.pallas_call(
        make_coeffs,
        name="make_coeffs",
        out_shape=jax.ShapeDtypeStruct((basis.shape[0], pieces.shape[2]), BF16),
        in_specs=[VMEM, VMEM],
        out_specs=VMEM,
        compiler_params=limit(12),
    )(basis, pieces)


def apply_potential(member_ref, own_ref, near_ref, far_ref, both_ref, cols_ref, base_ref, pairs_ref, mask_ref, keep_ref, give_ref, coeffs, total):
    member = member_ref[0]
    quarter = own_ref.shape[1]
    for bits, ref in enumerate((own_ref, near_ref, far_ref, both_ref)):
        at = pl.multiple_of((member ^ bits) * quarter, quarter)
        coeffs[:, pl.ds(at, quarter)] = ref[...]
    potential = split_lanes(
        lax.dot_general(
            coeffs[...], cols_ref[...], (((1,), (1,)), ((), ())), preferred_element_type=F32
        )
    )
    sx = -dy(potential)
    sy = dx(potential)
    mask = mask_ref[...].astype(F32)
    same, two_x, two_y, up, down = (pairs_ref[k] for k in range(5))
    same_x = same * sx
    same_y = same * sy
    up_x = up * shift_rows(shift_cols(sx, 1), 1)
    up_y = up * shift_rows(shift_cols(sy, 1), 1)
    down_x = down * shift_rows(shift_cols(sx, 1), -1)
    down_y = down * shift_rows(shift_cols(sy, 1), -1)
    back_up_x = shift_rows(shift_cols(up * sx, -1), -1)
    back_up_y = shift_rows(shift_cols(up * sy, -1), -1)
    back_down_x = shift_rows(shift_cols(down * sx, -1), 1)
    back_down_y = shift_rows(shift_cols(down * sy, -1), 1)
    gx = shift_cols(mask, 1) * (
        two_x * shift_cols(sx, 2) - same_x + up_y - down_y
    ) - shift_cols(mask, -1) * (same_x - shift_cols(two_x * sx, -2) + back_down_y - back_up_y)
    gy = shift_rows(mask, 1) * (
        up_x - back_down_x + two_y * shift_rows(sy, 2) - same_y
    ) - shift_rows(mask, -1) * (down_x - back_up_x + same_y - shift_rows(two_y * sy, -2))
    scale = -(TIME_STEP**4) / 64.0
    grad = base_ref[...] + scale * (dy(gx) - dx(gy))
    pair = keep_ref.shape[0]
    total[...] = join_lanes(grad[:, : 2 * pair, :])
    core = member % 2
    keep_ref[...] = total[pl.ds(pl.multiple_of(core * pair, pair), pair), :]
    give_ref[...] = total[pl.ds(pl.multiple_of((1 - core) * pair, pair), pair), :]


def gradient_halves(member, parts, basis_cols, base, pairs, mask):
    _, ring, _ = base.shape
    cols, width = basis_cols.shape
    pair = (ring - TILE) // 2
    half = jax.ShapeDtypeStruct((pair, cols), F32)
    return pl.pallas_call(
        apply_potential,
        name="apply_potential",
        out_shape=(half, half),
        in_specs=[SMEM] + [VMEM] * 8,
        out_specs=(VMEM, VMEM),
        scratch_shapes=[
            pltpu.VMEM((ring, width), BF16),
            pltpu.VMEM((2 * pair, cols), F32),
        ],
        compiler_params=limit(24),
    )(member.reshape(1), *parts, basis_cols, base, pairs, mask)


def project(own_ref, other_ref, cols_ref, out_ref):
    total = (own_ref[...] + other_ref[...]).astype(BF16)
    projected = jnp.dot(total, cols_ref[...], preferred_element_type=F32).astype(BF16)
    half = out_ref.shape[3]
    for core in range(2):
        part = projected[:, core * half : (core + 1) * half]
        for chip in range(out_ref.shape[0] // 2):
            for k in range(out_ref.shape[1]):
                out_ref[2 * chip + core, k] = part


def projected_pieces(own, other, basis_cols, members, slabs):
    single = own.shape[0]
    half = basis_cols.shape[1] // 2
    return pl.pallas_call(
        project,
        name="project",
        out_shape=jax.ShapeDtypeStruct((members, slabs, single, half), BF16),
        in_specs=[VMEM] * 3,
        out_specs=VMEM,
        compiler_params=limit(16),
    )(own, other, basis_cols)


def assemble(member_ref, own_ref, far_ref, near_ref, control_ref, basis_ref, kept_ref, sem):
    copy = pltpu.make_async_copy(control_ref, kept_ref, sem)
    copy.start()
    member = member_ref[0]
    quarter = own_ref.shape[1]
    parts = (own_ref[...], near_ref[0], far_ref[...], near_ref[1])
    for bits, part in enumerate(parts):
        at = pl.multiple_of((member ^ bits) * quarter, quarter)
        basis_ref[pl.ds(at, quarter), :] = part.astype(F32).T.astype(BF16)
    copy.wait()


def assembled(member, own, far, near, control):
    rows, _ = own.shape
    width = control.shape[1]
    return pl.pallas_call(
        assemble,
        name="assemble",
        out_shape=(
            jax.ShapeDtypeStruct((width, rows), BF16),
            jax.ShapeDtypeStruct(control.shape, F32),
        ),
        in_specs=[SMEM, VMEM, VMEM, VMEM, HBM],
        out_specs=(VMEM, VMEM),
        scratch_shapes=[pltpu.SemaphoreType.DMA],
        compiler_params=limit(24),
    )(member.reshape(1), own, far, near, in_hbm(control))


def gradient(slab_ref, basis_ref, projected_ref, out_ref):
    rows_out = out_ref.shape[0] - TILE
    width = basis_ref.shape[0]
    half = out_ref.shape[1]
    projected = projected_ref[...]
    block = width // 4
    squares = jnp.zeros((TILE, half), F32)
    for k in range(4):
        part = jnp.dot(
            basis_ref[k * block : (k + 1) * block, :], projected, preferred_element_type=F32
        )
        squares += jnp.sum((part * part).reshape(block // TILE, TILE, half), axis=0)
    at = pl.multiple_of(slab_ref[0] * rows_out, rows_out)
    out_ref[:rows_out] = jnp.dot(
        basis_ref[pl.ds(at, rows_out), :], projected, preferred_element_type=F32
    )
    out_ref[rows_out:] = squares


def gradient_block(slab, basis, projected, rows_out):
    half = projected.shape[1]
    return pl.pallas_call(
        gradient,
        name="gradient",
        out_shape=jax.ShapeDtypeStruct((rows_out + TILE, half), F32),
        in_specs=[SMEM, VMEM, VMEM],
        out_specs=VMEM,
        compiler_params=limit(24),
    )(slab.reshape(1), basis, projected)


def update(core_ref, control_ref, own_ref, other_ref, out_ref):
    rows_out, width = control_ref.shape
    half = width // 2
    total = jnp.sum(own_ref[rows_out:] + other_ref[rows_out:])
    scale = STEP_SIZE * lax.rsqrt(total / (width * width) + EPSILON)
    for turn, ref in enumerate((own_ref, other_ref)):
        at = pl.multiple_of((core_ref[0] ^ turn) * half, half)
        out_ref[:, pl.ds(at, half)] = control_ref[:, pl.ds(at, half)] - ref[:rows_out] * scale


def updated(core, control, own, other):
    return pl.pallas_call(
        update,
        name="update",
        out_shape=jax.ShapeDtypeStruct(control.shape, F32),
        in_specs=[SMEM, VMEM, VMEM, VMEM],
        out_specs=VMEM,
        compiler_params=limit(8),
    )(core.reshape(1), control, own, other)


def partner(value, bit):
    count = lax.axis_size("ens")
    return lax.ppermute(value, "ens", [(i, i ^ bit) for i in range(count)])


def on_device(checkpoints, section_index, targets, sea_mask, basis_rows, basis_cols, control):
    members = lax.axis_size("ens")
    slabs = lax.axis_size("space")
    member = lax.axis_index("ens").astype(jnp.int32)
    slab = lax.axis_index("space").astype(jnp.int32)
    core = member & 1
    chip = member >> 1
    rows_out, width = control.shape
    rows = basis_rows.shape[0]
    quarter = width // members
    half = width // 2
    single = rows // 4

    up, down, pieces = packed(
        section_index, member, checkpoints, targets, sea_mask, basis_rows, control, slabs, quarter
    )
    before = lax.ppermute(up, "space", [(i, i + 1) for i in range(slabs - 1)])
    after = lax.ppermute(down, "space", [(i + 1, i) for i in range(slabs - 1)])
    pieces = lax.all_to_all(pieces, "space", 0, 0)
    base, pairs, mask, ext_rows = states_pass(
        section_index, checkpoints, before, after, targets, sea_mask, basis_rows
    )
    own = coeffs_part(ext_rows, pieces)
    parts = [own]
    for bits in (1, 2, 3):
        parts.append(partner(own, bits))
    cols = held(basis_cols)
    keep, give = gradient_halves(member, parts, cols, base, pairs, mask)

    keep = keep + partner(give, 1)
    own_rows = lax.dynamic_slice_in_dim(keep, chip * single, single, 0)
    give = lax.dynamic_slice_in_dim(keep, (1 - chip) * single, single, 0)
    arriving = partner(give, 2)
    cols = held(basis_cols)
    send = projected_pieces(own_rows, arriving, cols, members, slabs)
    got = lax.all_to_all(send.reshape(members * slabs, single, half), ("ens", "space"), 0, 0)
    projected_half = got.reshape(slabs * rows, half)

    part = pieces[:, rows_out:, :].reshape(slabs, 2, members // 2, single, quarter)
    part = part.transpose(2, 1, 0, 3, 4).reshape(slabs * rows, quarter)
    far = partner(part, 2)
    near = partner(jnp.stack([part, far]), 1)
    basis, kept = assembled(member, part, far, near, control)
    block = gradient_block(slab, basis, projected_half, rows_out)
    other = partner(block, 1)
    return updated(core, kept, block, other)


def solution(mesh):
    return jax.shard_map(
        on_device,
        mesh=mesh,
        in_specs=(
            P("ens", None, None, "space", None),
            P("ens"),
            P("ens", "space", None),
            P("space", None),
            P("space", None),
            P(),
            P("space", None),
        ),
        out_specs=P("space", None),
        check_vma=False,
    )
```

```python
import jax
import jax.numpy as jnp
from jax import lax
from jax.experimental import pallas as pl
from jax.experimental.pallas import tpu as pltpu
from jax.sharding import PartitionSpec as P


DEPTH = 1.0
GRAVITY = 1.0
CORIOLIS = 0.5
FRICTION = 0.1
TIME_STEP = 0.3
STEP_SIZE = 1.0
EPSILON = 1e-06

F32 = jnp.float32
BF16 = jnp.bfloat16
TILE = 8
LANES = 128
MIB = 1 << 20


VMEM = pl.BlockSpec(memory_space=pltpu.VMEM)
SMEM = pl.BlockSpec(memory_space=pltpu.SMEM)
HBM = pl.BlockSpec(memory_space=pltpu.HBM)


def limit(mib):
    return pltpu.CompilerParams(vmem_limit_bytes=mib * MIB)


def tile_rows(shape):
    return lax.broadcasted_iota(jnp.int32, shape, 0)


def split_lanes(field):
    return jnp.stack([field[:, k : k + LANES] for k in range(0, field.shape[1], LANES)])


def join_lanes(field):
    return jnp.concatenate([field[k] for k in range(field.shape[0])], axis=1)


def shift_cols(field, step):
    turned = pltpu.roll(field, (-step) % LANES, 2)
    lane = lax.broadcasted_iota(jnp.int32, field.shape, 2)
    outside = jnp.zeros_like(turned[:1])
    if step > 0:
        beside = jnp.concatenate([turned[1:], outside], axis=0)
        return jnp.where(lane >= LANES - step, beside, turned)
    beside = jnp.concatenate([outside, turned[:-1]], axis=0)
    return jnp.where(lane < -step, beside, turned)


def shift_rows(field, step):
    return pltpu.roll(field, (-step) % field.shape[1], 1)


def dx(field):
    return shift_cols(field, 1) - shift_cols(field, -1)


def dy(field):
    return shift_rows(field, 1) - shift_rows(field, -1)


def fetch(source, target, sem):
    copy = pltpu.make_async_copy(source, target, sem)
    copy.start()
    return copy


def pack_edges(index_ref, states_ref, targets_ref, sea_ref, up_ref, down_ref, last, first, seen, sea, sems):
    count, _, _, rows, cols = states_ref.shape
    states = []
    for s in range(count):
        slot = index_ref[s]
        for side, (buffer, row) in enumerate(((last, rows - TILE), (first, 0))):
            source = states_ref.at[s, slot, :, pl.ds(row, TILE), :]
            states.append(fetch(source, buffer.at[s], sems.at[side, s]))
    others = [
        fetch(targets_ref.at[:, pl.ds(rows - TILE, TILE), :], seen.at[0], sems.at[0, count]),
        fetch(targets_ref.at[:, pl.ds(0, TILE), :], seen.at[1], sems.at[1, count]),
        fetch(sea_ref.at[pl.ds(rows - TILE, TILE), :], sea.at[0], sems.at[0, count + 1]),
        fetch(sea_ref.at[pl.ds(0, TILE), :], sea.at[1], sems.at[1, count + 1]),
    ]
    row = tile_rows((TILE, cols))
    for s in range(count):
        states[2 * s].wait()
        height, east, north = (last[s, f].astype(F32) for f in range(3))
        height, east, north = (
            pltpu.roll(height, 4, 0), pltpu.roll(east, 1, 0), pltpu.roll(north, 7, 0)
        )
        low = (row >= 1) & (row < 4)
        middle = (row >= 4) & (row < 7)
        up_ref[s] = jnp.where(low, height, jnp.where(middle, north, east)).astype(BF16)
        states[2 * s + 1].wait()
        height, east, north = (first[s, f].astype(F32) for f in range(3))
        height, east, north = (
            pltpu.roll(height, 4, 0), pltpu.roll(east, 2, 0), pltpu.roll(north, 7, 0)
        )
        high = (row >= 2) & (row < 4)
        down_ref[s] = jnp.where(middle, height, jnp.where(high, east, north)).astype(BF16)
    for copy in others:
        copy.wait()
    targets_up = jnp.zeros((TILE, cols), F32)
    targets_down = jnp.zeros((TILE, cols), F32)
    for s in range(count):
        targets_up = jnp.where(row == s, seen[0, s].astype(F32)[TILE - 1 :, :], targets_up)
        targets_down = jnp.where(row == s, seen[1, s].astype(F32)[:1, :], targets_down)
    up_ref[count] = targets_up.astype(BF16)
    down_ref[count] = targets_down.astype(BF16)
    up_ref[count + 1] = pltpu.roll(sea[0].astype(F32), 4, 0).astype(BF16)
    down_ref[count + 1] = pltpu.roll(sea[1].astype(F32), 4, 0).astype(BF16)


def edge_messages(section_index, checkpoints, targets, sea_mask):
    count, _, fields, _, cols = checkpoints.shape
    edges = jax.ShapeDtypeStruct((count + 2, TILE, cols), BF16)
    return pl.pallas_call(
        pack_edges,
        name="pack_edges",
        out_shape=(edges, edges),
        in_specs=[SMEM] + [HBM] * 3,
        out_specs=(VMEM, VMEM),
        scratch_shapes=[
            pltpu.VMEM((count, fields, TILE, cols), BF16),
            pltpu.VMEM((count, fields, TILE, cols), BF16),
            pltpu.VMEM((2, count, TILE, cols), BF16),
            pltpu.VMEM((2, TILE, cols), jnp.int32),
            pltpu.SemaphoreType.DMA((2, count + 2)),
        ],
        compiler_params=limit(12),
    )(*map(in_hbm, (section_index, checkpoints, targets, sea_mask)))


def pack_pieces(member_ref, basis_ref, control_ref, out_ref, basis, own, sems):
    rows, width = basis_ref.shape
    rows_out = control_ref.shape[0]
    slabs, _, quarter = out_ref.shape
    at = pl.multiple_of(member_ref[0] * quarter, quarter)
    copies = [
        fetch(control_ref.at[:, pl.ds(at, quarter)], own, sems.at[0]),
        fetch(basis_ref, basis, sems.at[1]),
    ]
    for copy in copies:
        copy.wait()
    part = own[...].astype(BF16)
    part_basis = basis[:, pl.ds(at, quarter)]
    row = tile_rows((TILE, width))
    first = basis[:TILE, :].astype(F32)
    last = pltpu.roll(basis[rows - TILE :, :].astype(F32), 4, 0)
    both = jnp.where(row < 2, first, last)
    tiles = []
    for q in range(0, width // quarter, 2):
        here = both[:, q * quarter : (q + 1) * quarter]
        below = pltpu.roll(both[:, (q + 1) * quarter : (q + 2) * quarter], 4, 0)
        tiles.append(jnp.where(row[:, :quarter] < 4, here, below))
    edges = jnp.concatenate(tiles, axis=0).astype(BF16)
    for k in range(slabs):
        out_ref[k, :rows_out] = part
        out_ref[k, rows_out : rows_out + rows] = part_basis
        out_ref[k, rows_out + rows :] = edges


def pieces_for(member, basis_rows, control, slabs, quarter):
    rows, width = basis_rows.shape
    rows_out = control.shape[0]
    edges = 4 * width // quarter
    return pl.pallas_call(
        pack_pieces,
        name="pack_pieces",
        out_shape=jax.ShapeDtypeStruct((slabs, rows_out + rows + edges, quarter), BF16),
        in_specs=[SMEM, HBM, HBM],
        out_specs=VMEM,
        scratch_shapes=[
            pltpu.VMEM((rows, width), BF16),
            pltpu.VMEM((rows_out, quarter), F32),
            pltpu.SemaphoreType.DMA((2,)),
        ],
        compiler_params=limit(10),
    )(member.reshape(1), in_hbm(basis_rows), in_hbm(control))


def in_hbm(array):
    return pltpu.with_memory_space_constraint(array, pltpu.HBM)


def hold(source_ref, out_ref, sem):
    copy = pltpu.make_async_copy(source_ref, out_ref, sem)
    copy.start()
    copy.wait()


def held(array):
    size = array.size * array.dtype.itemsize
    return pl.pallas_call(
        hold,
        name="hold",
        out_shape=jax.ShapeDtypeStruct(array.shape, array.dtype),
        in_specs=[HBM],
        out_specs=VMEM,
        scratch_shapes=[pltpu.SemaphoreType.DMA],
        compiler_params=limit(size // MIB + 2),
    )(in_hbm(array))


PAIRS = 5


class Rows:
    def __init__(self, ref):
        self.ref = ref

    def put(self, tile, value):
        self.ref[:, TILE * (tile + 1) : TILE * (tile + 2), :] = value

    def get(self, tile, step=0):
        start = TILE * (tile + 1) + step
        return self.ref[:, start : start + TILE, :]


def rows_of(tile):
    return slice(TILE * tile, TILE * (tile + 1))


def clear(*refs):
    for ref in refs:
        ref[...] = jnp.zeros_like(ref)


def add_state(tiles, load, seen, mask, live, padded, partial, gx, gy, pairs_ref):
    heights, fluxes, mid_fluxes, weights, besides, misfits = (Rows(ref) for ref in padded)
    half = 0.5 * TIME_STEP
    keep = 1.0 - TIME_STEP * FRICTION
    turn = TIME_STEP * CORIOLIS / keep
    slope = half * GRAVITY / keep

    for tile in range(tiles):
        height = load(0, tile)
        heights.put(tile, height)
        fluxes.put(tile, (DEPTH + height) * load(2, tile))

    for tile in range(tiles):
        height = heights.get(tile)
        east = load(1, tile)
        north = load(2, tile)
        flux = dx((DEPTH + height) * east) + (fluxes.get(tile, 1) - fluxes.get(tile, -1))
        sea = mask[:, rows_of(tile), :]
        height_mid = sea * (height - half * flux)
        weight = DEPTH * sea + height_mid
        east_mid = east + turn * north - slope * dx(height)
        north_mid = north - turn * east - slope * (heights.get(tile, 1) - heights.get(tile, -1))
        mid_fluxes.put(tile, weight * north_mid)
        weights.put(tile, weight)
        besides.put(tile, shift_cols(weight, 1))
        partial[:, rows_of(tile), :] = (
            height + height_mid - 2.0 * seen(tile) - half * keep * dx(weight * east_mid)
        )

    for tile in range(tiles):
        change = mid_fluxes.get(tile, 1) - mid_fluxes.get(tile, -1)
        misfit = live[:, rows_of(tile), :] * (partial[:, rows_of(tile), :] - half * keep * change)
        misfits.put(tile, misfit)
        gx[:, rows_of(tile), :] += weights.get(tile) * dx(misfit)

    for tile in range(tiles):
        here = rows_of(tile)
        weight = weights.get(tile)
        gy[:, here, :] += weight * (misfits.get(tile, 1) - misfits.get(tile, -1))
        pairs_ref[0, :, here, :] += weight * weight
        pairs_ref[1, :, here, :] += weight * shift_cols(weight, 2)
        pairs_ref[2, :, here, :] += weight * weights.get(tile, 2)
        pairs_ref[3, :, here, :] += weight * besides.get(tile, 1)
        pairs_ref[4, :, here, :] += weight * besides.get(tile, -1)


def inner_states(index_ref, state_ref, targets_ref, sea_ref, basis_ref, gx_ref, gy_ref, pairs_ref, rows_ref, mask, live, partial, *padded):
    rows = sea_ref.shape[0]
    tiles = rows // TILE

    @pl.when(pl.program_id(0) == 0)
    def _():
        clear(gx_ref, gy_ref, pairs_ref, *padded)
        rows_ref[...] = basis_ref[...]
        for tile in range(tiles):
            mask[:, rows_of(tile), :] = split_lanes(sea_ref[rows_of(tile), :].astype(F32))
        row = lax.broadcasted_iota(jnp.int32, live.shape, 1)
        live[...] = jnp.where((row >= 2) & (row < rows - 2), mask[...], 0.0)

    add_state(
        tiles,
        lambda field, tile: split_lanes(state_ref[0, 0, field, rows_of(tile), :].astype(F32)),
        lambda tile: split_lanes(targets_ref[0, rows_of(tile), :].astype(F32)),
        mask, live, padded, partial, gx_ref, gy_ref, pairs_ref,
    )


def inner_pass(section_index, checkpoints, targets, sea_mask, basis_rows):
    count, _, fields, rows, cols = checkpoints.shape
    width = basis_rows.shape[1]
    lanes = cols // LANES
    padded = pltpu.VMEM((lanes, rows + 2 * TILE, LANES), F32)
    plain = pltpu.VMEM((lanes, rows, LANES), F32)
    outs = (
        jax.ShapeDtypeStruct((lanes, rows, LANES), F32),
        jax.ShapeDtypeStruct((lanes, rows, LANES), F32),
        jax.ShapeDtypeStruct((PAIRS, lanes, rows, LANES), F32),
        jax.ShapeDtypeStruct((rows, width), BF16),
    )
    return pl.pallas_call(
        inner_states,
        name="inner_states",
        out_shape=outs,
        grid_spec=pltpu.PrefetchScalarGridSpec(
            num_scalar_prefetch=1,
            grid=(count,),
            in_specs=[
                pl.BlockSpec((1, 1, fields, rows, cols), lambda s, index: (s, index[s], 0, 0, 0)),
                pl.BlockSpec((1, rows, cols), lambda s, index: (s, 0, 0)),
                pl.BlockSpec((rows, cols), lambda s, index: (0, 0)),
                pl.BlockSpec((rows, width), lambda s, index: (0, 0)),
            ],
            out_specs=tuple(
                pl.BlockSpec(out.shape, lambda s, index, n=len(out.shape): (0,) * n) for out in outs
            ),
            scratch_shapes=[plain] * 3 + [padded] * 6,
        ),
        compiler_params=limit(18),
    )(*map(in_hbm, (section_index, checkpoints, targets, sea_mask, basis_rows)))


def seam_states(index_ref, last_ref, first_ref, before_ref, after_ref, shared_before_ref, shared_after_ref, seen_last_ref, seen_first_ref, sea_ref, gx_in_ref, gy_in_ref, pairs_in_ref, base_ref, pairs_ref, mask_ref, seen_edge, mask, live, partial, gx, gy, pairs, ring_x, ring_y, *padded):
    s = pl.program_id(0)
    rows, cols = sea_ref.shape
    row = tile_rows((TILE, cols))
    top = row < 4

    def seam(ends, beyond_after, beyond_before):
        own_last, own_first = (pltpu.roll(end, 4, 0) for end in ends)
        return (
            split_lanes(jnp.where(top, own_last, beyond_after)),
            split_lanes(jnp.where(top, beyond_before, own_first)),
        )

    @pl.when(s == 0)
    def _():
        clear(gx, gy, pairs, *padded)
        seen_edge[0] = shared_before_ref[0].astype(F32)
        seen_edge[1] = shared_after_ref[0].astype(F32)
        after = jnp.where(row < 6, shared_after_ref[1].astype(F32), 0.0)
        before = jnp.where(row >= 2, shared_before_ref[1].astype(F32), 0.0)
        ends = (sea_ref[rows - TILE :, :].astype(F32), sea_ref[:TILE, :].astype(F32))
        for tile, value in enumerate(seam(ends, after, before)):
            mask[:, rows_of(tile), :] = value
        for tile in range(rows // TILE):
            mask_ref[:, rows_of(tile), :] = split_lanes(
                sea_ref[rows_of(tile), :].astype(F32)
            ).astype(BF16)
        beyond = jnp.where(top, pltpu.roll(after, 4, 0), pltpu.roll(before, 4, 0))
        mask_ref[:, rows:, :] = split_lanes(beyond).astype(BF16)
        place = lax.broadcasted_iota(jnp.int32, live.shape, 1)
        counts = ((place >= 2) & (place < 5)) | ((place >= 11) & (place < 14))
        live[...] = jnp.where(counts, mask[...], 0.0)

    after = after_ref[0].astype(F32)
    before = before_ref[0].astype(F32)
    turned = ((0, 0), (2, 3), (5, 5))
    fields = []
    for field, (forward, back) in enumerate(turned):
        ends = (last_ref[0, 0, field].astype(F32), first_ref[0, 0, field].astype(F32))
        fields.append(
            seam(
                ends,
                pltpu.roll(after, forward, 0) if forward else after,
                pltpu.roll(before, back, 0) if back else before,
            )
        )
    ends = (seen_last_ref[0].astype(F32), seen_first_ref[0].astype(F32))
    seen = seam(ends, seen_edge[1, pl.ds(s, 1), :], seen_edge[0, pl.ds(s, 1), :])
    add_state(
        2,
        lambda field, tile: fields[field][tile],
        lambda tile: seen[tile],
        mask, live, padded, partial, gx, gy, pairs,
    )

    @pl.when(s == pl.num_programs(0) - 1)
    def _():
        place = lax.broadcasted_iota(jnp.int32, (gx.shape[0], TILE, LANES), 1)
        top = place < 4
        final = rows // TILE - 1

        def ring(inner, outer, out, low):
            ending = pltpu.roll(outer[:, :TILE, :], 4, 1)
            opening = pltpu.roll(outer[:, TILE:, :], 4, 1)
            for tile in range(1, final):
                out[:, rows_of(tile), :] = inner[:, rows_of(tile), :]
            head = inner[:, :TILE, :]
            tail = inner[:, rows_of(final), :]
            if low is None:
                head = head + jnp.where(top, opening, 0.0)
                tail = tail + jnp.where(top, 0.0, ending)
            else:
                head = jnp.where(place < low, opening, head)
                tail = jnp.where(place > 4, ending, tail)
            out[:, :TILE, :] = head
            out[:, rows_of(final), :] = tail
            out[:, rows:, :] = jnp.where(top, ending, opening)

        ring(gx_in_ref[...], gx[...], ring_x, None)
        ring(gy_in_ref[...], gy[...], ring_y, None)
        for k in range(PAIRS):
            ring(pairs_in_ref[k], pairs[k], pairs_ref.at[k], 2 if k == 4 else 1)
        scale = 0.0625 * TIME_STEP * TIME_STEP
        base_ref[...] = scale * (dy(ring_x[...]) - dx(ring_y[...]))


def seam_pass(section_index, checkpoints, before, after, targets, sea_mask, gx, gy, pairs):
    count, _, fields, rows, cols = checkpoints.shape
    lanes = cols // LANES
    final = rows // TILE - 1
    ring = rows + TILE
    plain = pltpu.VMEM((lanes, 2 * TILE, LANES), F32)
    padded = pltpu.VMEM((lanes, 4 * TILE, LANES), F32)
    whole = pltpu.VMEM((lanes, ring, LANES), F32)
    state = (1, 1, fields, TILE, cols)
    edge = pl.BlockSpec((1, TILE, cols), lambda s, index: (s, 0, 0))
    shared = pl.BlockSpec((2, TILE, cols), lambda s, index: (count // 2, 0, 0))

    def fixed(array):
        return pl.BlockSpec(array.shape, lambda s, index, n=len(array.shape): (0,) * n)

    outs = (
        jax.ShapeDtypeStruct((lanes, ring, LANES), F32),
        jax.ShapeDtypeStruct((PAIRS, lanes, ring, LANES), F32),
        jax.ShapeDtypeStruct((lanes, ring, LANES), BF16),
    )
    return pl.pallas_call(
        seam_states,
        name="seam_states",
        out_shape=outs,
        grid_spec=pltpu.PrefetchScalarGridSpec(
            num_scalar_prefetch=1,
            grid=(count,),
            in_specs=[
                pl.BlockSpec(state, lambda s, index: (s, index[s], 0, final, 0)),
                pl.BlockSpec(state, lambda s, index: (s, index[s], 0, 0, 0)),
                edge,
                edge,
                shared,
                shared,
                pl.BlockSpec((1, TILE, cols), lambda s, index: (s, final, 0)),
                pl.BlockSpec((1, TILE, cols), lambda s, index: (s, 0, 0)),
                fixed(sea_mask),
                fixed(gx),
                fixed(gy),
                fixed(pairs),
            ],
            out_specs=tuple(fixed(out) for out in outs),
            scratch_shapes=[pltpu.VMEM((2, TILE, cols), F32)]
            + [plain] * 5
            + [pltpu.VMEM((PAIRS, lanes, 2 * TILE, LANES), F32)]
            + [whole] * 2
            + [padded] * 6,
        ),
        compiler_params=limit(20),
    )(
        in_hbm(section_index),
        in_hbm(checkpoints),
        in_hbm(checkpoints),
        before,
        after,
        before,
        after,
        in_hbm(targets),
        in_hbm(targets),
        in_hbm(sea_mask),
        gx,
        gy,
        pairs,
    )


def make_coeffs(slab_ref, basis_ref, pieces_ref, out_ref):
    slabs, _, quarter = pieces_ref.shape
    rows, width = basis_ref.shape
    rows_out = width // slabs
    slab = slab_ref[0]

    def edge_of(k):
        parts = []
        for q in range(width // quarter):
            start = rows_out + rows + TILE * (q // 2)
            part = pieces_ref[k, start : start + TILE, :].astype(F32)
            parts.append(pltpu.roll(part, 4, 0) if q % 2 else part)
        return jnp.concatenate(parts, axis=1)

    after = edge_of(jnp.minimum(slab + 1, slabs - 1))
    before = pltpu.roll(edge_of(jnp.maximum(slab - 1, 0)), 4, 0)
    row = tile_rows((TILE, width))
    use_after = (row < 2) & (slab < slabs - 1)
    use_before = (row >= 6) & (slab > 0)
    edge = jnp.where(use_after, after, jnp.where(use_before, before, 0.0))
    basis = jnp.concatenate([basis_ref[...].astype(F32), edge], axis=0).astype(BF16)
    part = pieces_ref[:, :rows_out, :].reshape(width, quarter)
    out_ref[...] = jnp.dot(basis, part, preferred_element_type=F32).astype(BF16)


def coeffs_part(slab, basis_rows, pieces):
    return pl.pallas_call(
        make_coeffs,
        name="make_coeffs",
        out_shape=jax.ShapeDtypeStruct((basis_rows.shape[0] + TILE, pieces.shape[2]), BF16),
        in_specs=[SMEM, VMEM, VMEM],
        out_specs=VMEM,
        compiler_params=limit(12),
    )(slab.reshape(1), basis_rows, pieces)


def apply_potential(member_ref, own_ref, near_ref, far_ref, both_ref, cols_ref, base_ref, pairs_ref, mask_ref, keep_ref, give_ref, coeffs, total):
    member = member_ref[0]
    quarter = own_ref.shape[1]
    for bits, ref in enumerate((own_ref, near_ref, far_ref, both_ref)):
        at = pl.multiple_of((member ^ bits) * quarter, quarter)
        coeffs[:, pl.ds(at, quarter)] = ref[...]
    potential = split_lanes(
        lax.dot_general(
            coeffs[...], cols_ref[...], (((1,), (1,)), ((), ())), preferred_element_type=F32
        )
    )
    sx = -dy(potential)
    sy = dx(potential)
    mask = mask_ref[...].astype(F32)
    same, two_x, two_y, up, down = (pairs_ref[k] for k in range(5))
    same_x = same * sx
    same_y = same * sy
    up_x = up * shift_rows(shift_cols(sx, 1), 1)
    up_y = up * shift_rows(shift_cols(sy, 1), 1)
    down_x = down * shift_rows(shift_cols(sx, 1), -1)
    down_y = down * shift_rows(shift_cols(sy, 1), -1)
    back_up_x = shift_rows(shift_cols(up * sx, -1), -1)
    back_up_y = shift_rows(shift_cols(up * sy, -1), -1)
    back_down_x = shift_rows(shift_cols(down * sx, -1), 1)
    back_down_y = shift_rows(shift_cols(down * sy, -1), 1)
    gx = shift_cols(mask, 1) * (
        two_x * shift_cols(sx, 2) - same_x + up_y - down_y
    ) - shift_cols(mask, -1) * (same_x - shift_cols(two_x * sx, -2) + back_down_y - back_up_y)
    gy = shift_rows(mask, 1) * (
        up_x - back_down_x + two_y * shift_rows(sy, 2) - same_y
    ) - shift_rows(mask, -1) * (down_x - back_up_x + same_y - shift_rows(two_y * sy, -2))
    scale = -(TIME_STEP**4) / 64.0
    grad = base_ref[...] + scale * (dy(gx) - dx(gy))
    pair = keep_ref.shape[0]
    total[...] = join_lanes(grad[:, : 2 * pair, :])
    core = member % 2
    keep_ref[...] = total[pl.ds(pl.multiple_of(core * pair, pair), pair), :]
    give_ref[...] = total[pl.ds(pl.multiple_of((1 - core) * pair, pair), pair), :]


def gradient_halves(member, parts, basis_cols, base, pairs, mask):
    _, ring, _ = base.shape
    cols, width = basis_cols.shape
    pair = (ring - TILE) // 2
    half = jax.ShapeDtypeStruct((pair, cols), F32)
    return pl.pallas_call(
        apply_potential,
        name="apply_potential",
        out_shape=(half, half),
        in_specs=[SMEM] + [VMEM] * 8,
        out_specs=(VMEM, VMEM),
        scratch_shapes=[
            pltpu.VMEM((ring, width), BF16),
            pltpu.VMEM((2 * pair, cols), F32),
        ],
        compiler_params=limit(24),
    )(member.reshape(1), *parts, basis_cols, base, pairs, mask)


def project(own_ref, other_ref, cols_ref, out_ref):
    total = (own_ref[...] + other_ref[...]).astype(BF16)
    projected = jnp.dot(total, cols_ref[...], preferred_element_type=F32).astype(BF16)
    half = out_ref.shape[3]
    for core in range(2):
        part = projected[:, core * half : (core + 1) * half]
        for chip in range(out_ref.shape[0] // 2):
            for k in range(out_ref.shape[1]):
                out_ref[2 * chip + core, k] = part


def projected_pieces(own, other, basis_cols, members, slabs):
    single = own.shape[0]
    half = basis_cols.shape[1] // 2
    return pl.pallas_call(
        project,
        name="project",
        out_shape=jax.ShapeDtypeStruct((members, slabs, single, half), BF16),
        in_specs=[VMEM] * 3,
        out_specs=VMEM,
        compiler_params=limit(16),
    )(own, other, basis_cols)


def assemble(member_ref, own_ref, far_ref, near_ref, control_ref, basis_ref, kept_ref, sem):
    copy = pltpu.make_async_copy(control_ref, kept_ref, sem)
    copy.start()
    member = member_ref[0]
    quarter = own_ref.shape[1]
    parts = (own_ref[...], near_ref[0], far_ref[...], near_ref[1])
    for bits, part in enumerate(parts):
        at = pl.multiple_of((member ^ bits) * quarter, quarter)
        basis_ref[pl.ds(at, quarter), :] = part.astype(F32).T.astype(BF16)
    copy.wait()


def assembled(member, own, far, near, control):
    rows, _ = own.shape
    width = control.shape[1]
    return pl.pallas_call(
        assemble,
        name="assemble",
        out_shape=(
            jax.ShapeDtypeStruct((width, rows), BF16),
            jax.ShapeDtypeStruct(control.shape, F32),
        ),
        in_specs=[SMEM, VMEM, VMEM, VMEM, HBM],
        out_specs=(VMEM, VMEM),
        scratch_shapes=[pltpu.SemaphoreType.DMA],
        compiler_params=limit(24),
    )(member.reshape(1), own, far, near, in_hbm(control))


def gradient(slab_ref, basis_ref, projected_ref, out_ref):
    rows_out = out_ref.shape[0] - TILE
    width = basis_ref.shape[0]
    half = out_ref.shape[1]
    projected = projected_ref[...]
    block = width // 4
    squares = jnp.zeros((TILE, half), F32)
    for k in range(4):
        part = jnp.dot(
            basis_ref[k * block : (k + 1) * block, :], projected, preferred_element_type=F32
        )
        squares += jnp.sum((part * part).reshape(block // TILE, TILE, half), axis=0)
    at = pl.multiple_of(slab_ref[0] * rows_out, rows_out)
    out_ref[:rows_out] = jnp.dot(
        basis_ref[pl.ds(at, rows_out), :], projected, preferred_element_type=F32
    )
    out_ref[rows_out:] = squares


def gradient_block(slab, basis, projected, rows_out):
    half = projected.shape[1]
    return pl.pallas_call(
        gradient,
        name="gradient",
        out_shape=jax.ShapeDtypeStruct((rows_out + TILE, half), F32),
        in_specs=[SMEM, VMEM, VMEM],
        out_specs=VMEM,
        compiler_params=limit(24),
    )(slab.reshape(1), basis, projected)


def update(core_ref, control_ref, own_ref, other_ref, out_ref):
    rows_out, width = control_ref.shape
    half = width // 2
    total = jnp.sum(own_ref[rows_out:] + other_ref[rows_out:])
    scale = STEP_SIZE * lax.rsqrt(total / (width * width) + EPSILON)
    for turn, ref in enumerate((own_ref, other_ref)):
        at = pl.multiple_of((core_ref[0] ^ turn) * half, half)
        out_ref[:, pl.ds(at, half)] = control_ref[:, pl.ds(at, half)] - ref[:rows_out] * scale


def updated(core, control, own, other):
    return pl.pallas_call(
        update,
        name="update",
        out_shape=jax.ShapeDtypeStruct(control.shape, F32),
        in_specs=[SMEM, VMEM, VMEM, VMEM],
        out_specs=VMEM,
        compiler_params=limit(8),
    )(core.reshape(1), control, own, other)


def partner(value, bit):
    count = lax.axis_size("ens")
    return lax.ppermute(value, "ens", [(i, i ^ bit) for i in range(count)])


def on_device(checkpoints, section_index, targets, sea_mask, basis_rows, basis_cols, control):
    members = lax.axis_size("ens")
    slabs = lax.axis_size("space")
    member = lax.axis_index("ens").astype(jnp.int32)
    slab = lax.axis_index("space").astype(jnp.int32)
    core = member & 1
    chip = member >> 1
    rows_out, width = control.shape
    rows = basis_rows.shape[0]
    quarter = width // members
    half = width // 2
    single = rows // 4

    pieces = pieces_for(member, basis_rows, control, slabs, quarter)
    pieces = lax.all_to_all(pieces, "space", 0, 0)
    up, down = edge_messages(section_index, checkpoints, targets, sea_mask)
    before = lax.ppermute(up, "space", [(i, i + 1) for i in range(slabs - 1)])
    after = lax.ppermute(down, "space", [(i + 1, i) for i in range(slabs - 1)])
    gx, gy, pairs, near_rows = inner_pass(section_index, checkpoints, targets, sea_mask, basis_rows)
    own = coeffs_part(slab, near_rows, pieces)
    parts = [own]
    for bits in (1, 2, 3):
        parts.append(partner(own, bits))
    base, pairs, mask = seam_pass(
        section_index, checkpoints, before, after, targets, sea_mask, gx, gy, pairs
    )
    keep, give = gradient_halves(member, parts, basis_cols, base, pairs, mask)

    keep = keep + partner(give, 1)
    own_rows = lax.dynamic_slice_in_dim(keep, chip * single, single, 0)
    give = lax.dynamic_slice_in_dim(keep, (1 - chip) * single, single, 0)
    arriving = partner(give, 2)
    cols = held(basis_cols)
    send = projected_pieces(own_rows, arriving, cols, members, slabs)
    got = lax.all_to_all(send.reshape(members * slabs, single, half), ("ens", "space"), 0, 0)
    projected_half = got.reshape(slabs * rows, half)

    part = pieces[:, rows_out : rows_out + rows, :].reshape(slabs, 2, members // 2, single, quarter)
    part = part.transpose(2, 1, 0, 3, 4).reshape(slabs * rows, quarter)
    far = partner(part, 2)
    near = partner(jnp.stack([part, far]), 1)
    basis, kept = assembled(member, part, far, near, control)
    block = gradient_block(slab, basis, projected_half, rows_out)
    other = partner(block, 1)
    return updated(core, kept, block, other)


def solution(mesh):
    return jax.shard_map(
        on_device,
        mesh=mesh,
        in_specs=(
            P("ens", None, None, "space", None),
            P("ens"),
            P("ens", "space", None),
            P("space", None),
            P("space", None),
            P(),
            P("space", None),
        ),
        out_specs=P("space", None),
        check_vma=False,
    )
```

```python
import jax
import jax.numpy as jnp
from jax import lax
from jax.experimental import pallas as pl
from jax.experimental.pallas import tpu as pltpu
from jax.sharding import PartitionSpec as P


DEPTH = 1.0
GRAVITY = 1.0
CORIOLIS = 0.5
FRICTION = 0.1
TIME_STEP = 0.3
STEP_SIZE = 1.0
EPSILON = 1e-06

F32 = jnp.float32
BF16 = jnp.bfloat16
TILE = 8
LANES = 128
MIB = 1 << 20


VMEM = pl.BlockSpec(memory_space=pltpu.VMEM)
SMEM = pl.BlockSpec(memory_space=pltpu.SMEM)
HBM = pl.BlockSpec(memory_space=pltpu.HBM)


def limit(mib):
    return pltpu.CompilerParams(vmem_limit_bytes=mib * MIB)


def tile_rows(shape):
    return lax.broadcasted_iota(jnp.int32, shape, 0)


def split_lanes(field):
    return jnp.stack([field[:, k : k + LANES] for k in range(0, field.shape[1], LANES)])


def join_lanes(field):
    return jnp.concatenate([field[k] for k in range(field.shape[0])], axis=1)


def shift_cols(field, step):
    turned = pltpu.roll(field, (-step) % LANES, 2)
    lane = lax.broadcasted_iota(jnp.int32, field.shape, 2)
    outside = jnp.zeros_like(turned[:1])
    if step > 0:
        beside = jnp.concatenate([turned[1:], outside], axis=0)
        return jnp.where(lane >= LANES - step, beside, turned)
    beside = jnp.concatenate([outside, turned[:-1]], axis=0)
    return jnp.where(lane < -step, beside, turned)


def shift_rows(field, step):
    return pltpu.roll(field, (-step) % field.shape[1], 1)


def dx(field):
    return shift_cols(field, 1) - shift_cols(field, -1)


def dy(field):
    return shift_rows(field, 1) - shift_rows(field, -1)


def fetch(source, target, sem):
    copy = pltpu.make_async_copy(source, target, sem)
    copy.start()
    return copy


def pack_edges(index_ref, states_ref, targets_ref, sea_ref, up_ref, down_ref, last, first, seen, sea, sems):
    count, _, _, rows, cols = states_ref.shape
    states = []
    for s in range(count):
        slot = index_ref[s]
        for side, (buffer, row) in enumerate(((last, rows - TILE), (first, 0))):
            source = states_ref.at[s, slot, :, pl.ds(row, TILE), :]
            states.append(fetch(source, buffer.at[s], sems.at[side, s]))
    others = [
        fetch(targets_ref.at[:, pl.ds(rows - TILE, TILE), :], seen.at[0], sems.at[0, count]),
        fetch(targets_ref.at[:, pl.ds(0, TILE), :], seen.at[1], sems.at[1, count]),
        fetch(sea_ref.at[pl.ds(rows - TILE, TILE), :], sea.at[0], sems.at[0, count + 1]),
        fetch(sea_ref.at[pl.ds(0, TILE), :], sea.at[1], sems.at[1, count + 1]),
    ]
    row = tile_rows((TILE, cols))
    for s in range(count):
        states[2 * s].wait()
        height, east, north = (last[s, f].astype(F32) for f in range(3))
        height, north = pltpu.roll(height, 3, 0), pltpu.roll(north, 6, 0)
        up_ref[s] = jnp.where(row < 3, height, jnp.where(row < 6, north, east)).astype(BF16)
        states[2 * s + 1].wait()
        height, east, north = (first[s, f].astype(F32) for f in range(3))
        east, north = pltpu.roll(east, 6, 0), pltpu.roll(north, 3, 0)
        down_ref[s] = jnp.where(row < 3, height, jnp.where(row < 6, north, east)).astype(BF16)
    for copy in others:
        copy.wait()
    targets_up = jnp.zeros((TILE, cols), F32)
    targets_down = jnp.zeros((TILE, cols), F32)
    for s in range(count):
        targets_up = jnp.where(row == s, seen[0, s].astype(F32)[TILE - 1 :, :], targets_up)
        targets_down = jnp.where(row == s, seen[1, s].astype(F32)[:1, :], targets_down)
    up_ref[count] = targets_up.astype(BF16)
    down_ref[count] = targets_down.astype(BF16)
    up_ref[count + 1] = sea[0].astype(F32).astype(BF16)
    down_ref[count + 1] = sea[1].astype(F32).astype(BF16)


def edge_messages(section_index, checkpoints, targets, sea_mask):
    count, _, fields, _, cols = checkpoints.shape
    edges = jax.ShapeDtypeStruct((count + 2, TILE, cols), BF16)
    return pl.pallas_call(
        pack_edges,
        name="pack_edges",
        out_shape=(edges, edges),
        in_specs=[SMEM] + [HBM] * 3,
        out_specs=(VMEM, VMEM),
        scratch_shapes=[
            pltpu.VMEM((count, fields, TILE, cols), BF16),
            pltpu.VMEM((count, fields, TILE, cols), BF16),
            pltpu.VMEM((2, count, TILE, cols), BF16),
            pltpu.VMEM((2, TILE, cols), jnp.int32),
            pltpu.SemaphoreType.DMA((2, count + 2)),
        ],
        compiler_params=limit(12),
    )(*map(in_hbm, (section_index, checkpoints, targets, sea_mask)))


def pack_pieces(member_ref, basis_ref, control_ref, out_ref, basis, own, sems):
    rows, width = basis_ref.shape
    rows_out = control_ref.shape[0]
    slabs, _, quarter = out_ref.shape
    at = pl.multiple_of(member_ref[0] * quarter, quarter)
    copies = [
        fetch(control_ref.at[:, pl.ds(at, quarter)], own, sems.at[0]),
        fetch(basis_ref, basis, sems.at[1]),
    ]
    for copy in copies:
        copy.wait()
    part = own[...].astype(BF16)
    part_basis = basis[:, pl.ds(at, quarter)]
    row = tile_rows((TILE, width))
    first = basis[:TILE, :].astype(F32)
    last = pltpu.roll(basis[rows - TILE :, :].astype(F32), 4, 0)
    both = jnp.where(row < 2, first, last)
    tiles = []
    for q in range(0, width // quarter, 2):
        here = both[:, q * quarter : (q + 1) * quarter]
        below = pltpu.roll(both[:, (q + 1) * quarter : (q + 2) * quarter], 4, 0)
        tiles.append(jnp.where(row[:, :quarter] < 4, here, below))
    edges = jnp.concatenate(tiles, axis=0).astype(BF16)
    for k in range(slabs):
        out_ref[k, :rows_out] = part
        out_ref[k, rows_out : rows_out + rows] = part_basis
        out_ref[k, rows_out + rows :] = edges


def pieces_for(member, basis_rows, control, slabs, quarter):
    rows, width = basis_rows.shape
    rows_out = control.shape[0]
    edges = 4 * width // quarter
    return pl.pallas_call(
        pack_pieces,
        name="pack_pieces",
        out_shape=jax.ShapeDtypeStruct((slabs, rows_out + rows + edges, quarter), BF16),
        in_specs=[SMEM, HBM, HBM],
        out_specs=VMEM,
        scratch_shapes=[
            pltpu.VMEM((rows, width), BF16),
            pltpu.VMEM((rows_out, quarter), F32),
            pltpu.SemaphoreType.DMA((2,)),
        ],
        compiler_params=limit(10),
    )(member.reshape(1), in_hbm(basis_rows), in_hbm(control))


def in_hbm(array):
    return pltpu.with_memory_space_constraint(array, pltpu.HBM)


def hold(source_ref, out_ref, sem):
    copy = pltpu.make_async_copy(source_ref, out_ref, sem)
    copy.start()
    copy.wait()


def held(array):
    size = array.size * array.dtype.itemsize
    return pl.pallas_call(
        hold,
        name="hold",
        out_shape=jax.ShapeDtypeStruct(array.shape, array.dtype),
        in_specs=[HBM],
        out_specs=VMEM,
        scratch_shapes=[pltpu.SemaphoreType.DMA],
        compiler_params=limit(size // MIB + 2),
    )(in_hbm(array))


PAIRS = 5


class Rows:
    def __init__(self, ref):
        self.ref = ref

    def put(self, tile, value):
        self.ref[:, TILE * (tile + 1) : TILE * (tile + 2), :] = value

    def put_at(self, start, value):
        self.ref[:, start : start + value.shape[1], :] = value

    def get(self, tile, step=0):
        start = TILE * (tile + 1) + step
        return self.ref[:, start : start + TILE, :]


def rows_of(tile):
    return slice(TILE * tile, TILE * (tile + 1))


def clear(*refs):
    for ref in refs:
        ref[...] = jnp.zeros_like(ref)


def add_state(tiles, state, mask, live, padded, plain, sums):
    heights, easts, norths, seens = state
    fluxes, mid_fluxes, weights, rights, misfits = (Rows(ref) for ref in padded)
    lefts, partial = plain
    push_left, push_right, gy, same, two_x, two_y, up, down = sums
    half = 0.5 * TIME_STEP
    keep = 1.0 - TIME_STEP * FRICTION
    turn = TIME_STEP * CORIOLIS / keep
    slope = half * GRAVITY / keep

    for tile in range(-1, tiles + 1):
        fluxes.put(tile, (DEPTH + heights.get(tile)) * norths.get(tile))

    for tile in range(tiles):
        here = rows_of(tile)
        height = heights.get(tile)
        east = easts.get(tile)
        north = norths.get(tile)
        flux = dx((DEPTH + height) * east) + (fluxes.get(tile, 1) - fluxes.get(tile, -1))
        sea = mask[:, here, :]
        height_mid = sea * (height - half * flux)
        weight = DEPTH * sea + height_mid
        east_mid = east + turn * north - slope * dx(height)
        north_mid = north - turn * east - slope * (heights.get(tile, 1) - heights.get(tile, -1))
        right = shift_cols(weight, 1)
        left = shift_cols(weight, -1)
        mid_fluxes.put(tile, weight * north_mid)
        weights.put(tile, weight)
        rights.put(tile, right)
        lefts[:, here, :] = left
        same[:, here, :] += weight * weight
        two_x[:, here, :] += left * right
        partial[:, here, :] = (
            height + height_mid - 2.0 * seens.get(tile) - half * keep * dx(weight * east_mid)
        )

    for tile in range(tiles):
        here = rows_of(tile)
        change = mid_fluxes.get(tile, 1) - mid_fluxes.get(tile, -1)
        misfit = live[:, here, :] * (partial[:, here, :] - half * keep * change)
        misfits.put(tile, misfit)
        push_left[:, here, :] += lefts[:, here, :] * misfit
        push_right[:, here, :] += rights.get(tile) * misfit

    for tile in range(tiles):
        here = rows_of(tile)
        weight = weights.get(tile)
        gy[:, here, :] += weight * (misfits.get(tile, 1) - misfits.get(tile, -1))
        two_y[:, here, :] += weight * weights.get(tile, 2)
        up[:, here, :] += weight * rights.get(tile, 1)
        down[:, here, :] += weight * rights.get(tile, -1)


def inner_states(index_ref, state_ref, targets_ref, sea_ref, basis_ref, push_ref, pairs_ref, rows_ref, mask, live, *scratch):
    rows = sea_ref.shape[0]
    tiles = rows // TILE
    plain, padded = scratch[:2], scratch[2:]

    @pl.when(pl.program_id(0) == 0)
    def _():
        clear(push_ref, pairs_ref, *padded)
        rows_ref[...] = basis_ref[...]
        for tile in range(tiles):
            mask[:, rows_of(tile), :] = split_lanes(sea_ref[rows_of(tile), :].astype(F32))
        row = lax.broadcasted_iota(jnp.int32, live.shape, 1)
        live[...] = jnp.where((row >= 2) & (row < rows - 2), mask[...], 0.0)

    state = [Rows(ref) for ref in padded[:4]]
    for tile in range(tiles):
        for field in range(3):
            value = state_ref[0, 0, field, rows_of(tile), :].astype(F32)
            state[field].put(tile, split_lanes(value))
        state[3].put(tile, split_lanes(targets_ref[0, rows_of(tile), :].astype(F32)))
    sums = [push_ref.at[k] for k in range(3)] + [pairs_ref.at[k] for k in range(PAIRS)]
    add_state(tiles, state, mask, live, padded[4:], plain, sums)


def inner_pass(section_index, checkpoints, targets, sea_mask, basis_rows):
    count, _, fields, rows, cols = checkpoints.shape
    width = basis_rows.shape[1]
    lanes = cols // LANES
    padded = pltpu.VMEM((lanes, rows + 2 * TILE, LANES), F32)
    plain = pltpu.VMEM((lanes, rows, LANES), F32)
    outs = (
        jax.ShapeDtypeStruct((3, lanes, rows, LANES), F32),
        jax.ShapeDtypeStruct((PAIRS, lanes, rows, LANES), F32),
        jax.ShapeDtypeStruct((rows, width), BF16),
    )
    return pl.pallas_call(
        inner_states,
        name="inner_states",
        out_shape=outs,
        grid_spec=pltpu.PrefetchScalarGridSpec(
            num_scalar_prefetch=1,
            grid=(count,),
            in_specs=[
                pl.BlockSpec((1, 1, fields, rows, cols), lambda s, index: (s, index[s], 0, 0, 0)),
                pl.BlockSpec((1, rows, cols), lambda s, index: (s, 0, 0)),
                pl.BlockSpec((rows, cols), lambda s, index: (0, 0)),
                pl.BlockSpec((rows, width), lambda s, index: (0, 0)),
            ],
            out_specs=tuple(
                pl.BlockSpec(out.shape, lambda s, index, n=len(out.shape): (0,) * n) for out in outs
            ),
            scratch_shapes=[plain] * 4 + [padded] * 9,
        ),
        compiler_params=limit(18),
    )(*map(in_hbm, (section_index, checkpoints, targets, sea_mask, basis_rows)))


def seam_states(index_ref, last_ref, first_ref, before_ref, after_ref, shared_before_ref, shared_after_ref, seen_last_ref, seen_first_ref, sea_ref, push_in_ref, pairs_in_ref, base_ref, pairs_ref, mask_ref, seen_edge, mask, live, lefts, partial, sums_ref, ring_sums, *padded):
    s = pl.program_id(0)
    rows, cols = sea_ref.shape
    row = tile_rows((TILE, cols))
    top = row < 4

    @pl.when(s == 0)
    def _():
        clear(sums_ref, *padded)
        seen_edge[0] = split_lanes(shared_before_ref[0].astype(F32))
        seen_edge[1] = split_lanes(shared_after_ref[0].astype(F32))
        after = jnp.where(row < 2, shared_after_ref[1].astype(F32), 0.0)
        before = jnp.where(row >= 6, shared_before_ref[1].astype(F32), 0.0)
        beyond = after + before
        turned = pltpu.roll(beyond, 4, 0)
        last = pltpu.roll(sea_ref[rows - TILE :, :].astype(F32), 4, 0)
        first = pltpu.roll(sea_ref[:TILE, :].astype(F32), 4, 0)
        mask[:, :TILE, :] = split_lanes(jnp.where(top, last, turned))
        mask[:, TILE:, :] = split_lanes(jnp.where(top, turned, first))
        for tile in range(rows // TILE):
            mask_ref[:, rows_of(tile), :] = split_lanes(
                sea_ref[rows_of(tile), :].astype(F32)
            ).astype(BF16)
        mask_ref[:, rows:, :] = split_lanes(beyond).astype(BF16)
        place = lax.broadcasted_iota(jnp.int32, live.shape, 1)
        counts = ((place >= 2) & (place < 5)) | ((place >= 11) & (place < 14))
        live[...] = jnp.where(counts, mask[...], 0.0)

    state = [Rows(ref) for ref in padded[:4]]
    after = split_lanes(after_ref[0].astype(F32))
    before = split_lanes(before_ref[0].astype(F32))
    state[0].put_at(12, after)
    state[0].put_at(17, before)
    state[1].put_at(12, before)
    state[1].put_at(6, after)
    state[2].put_at(14, before)
    state[2].put_at(9, after)
    state[3].put_at(12, seen_edge[1, :, pl.ds(s, 1), :])
    state[3].put_at(19, seen_edge[0, :, pl.ds(s, 1), :])
    for field in range(3):
        state[field].put_at(4, split_lanes(last_ref[0, 0, field].astype(F32)))
        state[field].put_at(20, split_lanes(first_ref[0, 0, field].astype(F32)))
    state[3].put_at(4, split_lanes(seen_last_ref[0].astype(F32)))
    state[3].put_at(20, split_lanes(seen_first_ref[0].astype(F32)))
    sums = [sums_ref.at[k] for k in range(3 + PAIRS)]
    add_state(2, state, mask, live, padded[4:], (lefts, partial), sums)

    @pl.when(s == pl.num_programs(0) - 1)
    def _():
        place = lax.broadcasted_iota(jnp.int32, (lefts.shape[0], TILE, LANES), 1)
        top = place < 4
        final = rows // TILE - 1

        def ring(inner, outer, out, bounds):
            ending = pltpu.roll(outer[:, :TILE, :], 4, 1)
            opening = pltpu.roll(outer[:, TILE:, :], 4, 1)
            for tile in range(1, final):
                out[:, rows_of(tile), :] = inner[:, rows_of(tile), :]
            head = inner[:, :TILE, :]
            tail = inner[:, rows_of(final), :]
            if bounds is None:
                head = head + jnp.where(top, opening, 0.0)
                tail = tail + jnp.where(top, 0.0, ending)
            else:
                head = jnp.where(place < bounds[0], opening, head)
                tail = jnp.where(place > bounds[1], ending, tail)
            out[:, :TILE, :] = head
            out[:, rows_of(final), :] = tail
            out[:, rows:, :] = jnp.where(top, ending, opening)

        for k in range(3):
            ring(push_in_ref[k], sums_ref[k], ring_sums.at[k], None)
        for k in range(PAIRS):
            bounds = (2, 5) if k == PAIRS - 1 else (1, 4)
            ring(pairs_in_ref[k], sums_ref[3 + k], pairs_ref.at[k], bounds)
        scale = 0.0625 * TIME_STEP * TIME_STEP
        gx = shift_cols(ring_sums[0], 1) - shift_cols(ring_sums[1], -1)
        base_ref[...] = scale * (dy(gx) - dx(ring_sums[2]))


def seam_pass(section_index, checkpoints, before, after, targets, sea_mask, push, pairs):
    count, _, fields, rows, cols = checkpoints.shape
    lanes = cols // LANES
    final = rows // TILE - 1
    ring = rows + TILE
    plain = pltpu.VMEM((lanes, 2 * TILE, LANES), F32)
    padded = pltpu.VMEM((lanes, 4 * TILE, LANES), F32)
    state = (1, 1, fields, TILE, cols)
    edge = pl.BlockSpec((1, TILE, cols), lambda s, index: (s, 0, 0))
    shared = pl.BlockSpec((2, TILE, cols), lambda s, index: (count // 2, 0, 0))

    def fixed(array):
        return pl.BlockSpec(array.shape, lambda s, index, n=len(array.shape): (0,) * n)

    outs = (
        jax.ShapeDtypeStruct((lanes, ring, LANES), F32),
        jax.ShapeDtypeStruct((PAIRS, lanes, ring, LANES), F32),
        jax.ShapeDtypeStruct((lanes, ring, LANES), BF16),
    )
    return pl.pallas_call(
        seam_states,
        name="seam_states",
        out_shape=outs,
        grid_spec=pltpu.PrefetchScalarGridSpec(
            num_scalar_prefetch=1,
            grid=(count,),
            in_specs=[
                pl.BlockSpec(state, lambda s, index: (s, index[s], 0, final, 0)),
                pl.BlockSpec(state, lambda s, index: (s, index[s], 0, 0, 0)),
                edge,
                edge,
                shared,
                shared,
                pl.BlockSpec((1, TILE, cols), lambda s, index: (s, final, 0)),
                pl.BlockSpec((1, TILE, cols), lambda s, index: (s, 0, 0)),
                fixed(sea_mask),
                fixed(push),
                fixed(pairs),
            ],
            out_specs=tuple(fixed(out) for out in outs),
            scratch_shapes=[pltpu.VMEM((2, lanes, TILE, LANES), F32)]
            + [plain] * 4
            + [pltpu.VMEM((3 + PAIRS, lanes, 2 * TILE, LANES), F32)]
            + [pltpu.VMEM((3, lanes, ring, LANES), F32)]
            + [padded] * 9,
        ),
        compiler_params=limit(22),
    )(
        in_hbm(section_index),
        in_hbm(checkpoints),
        in_hbm(checkpoints),
        before,
        after,
        before,
        after,
        in_hbm(targets),
        in_hbm(targets),
        in_hbm(sea_mask),
        push,
        pairs,
    )


def make_coeffs(slab_ref, basis_ref, pieces_ref, out_ref):
    slabs, _, quarter = pieces_ref.shape
    rows, width = basis_ref.shape
    rows_out = width // slabs
    slab = slab_ref[0]

    def edge_of(k):
        parts = []
        for q in range(width // quarter):
            start = rows_out + rows + TILE * (q // 2)
            part = pieces_ref[k, start : start + TILE, :].astype(F32)
            parts.append(pltpu.roll(part, 4, 0) if q % 2 else part)
        return jnp.concatenate(parts, axis=1)

    after = edge_of(jnp.minimum(slab + 1, slabs - 1))
    before = pltpu.roll(edge_of(jnp.maximum(slab - 1, 0)), 4, 0)
    row = tile_rows((TILE, width))
    use_after = (row < 2) & (slab < slabs - 1)
    use_before = (row >= 6) & (slab > 0)
    edge = jnp.where(use_after, after, jnp.where(use_before, before, 0.0))
    basis = jnp.concatenate([basis_ref[...].astype(F32), edge], axis=0).astype(BF16)
    part = pieces_ref[:, :rows_out, :].reshape(width, quarter)
    out_ref[...] = jnp.dot(basis, part, preferred_element_type=F32).astype(BF16)


def coeffs_part(slab, basis_rows, pieces):
    return pl.pallas_call(
        make_coeffs,
        name="make_coeffs",
        out_shape=jax.ShapeDtypeStruct((basis_rows.shape[0] + TILE, pieces.shape[2]), BF16),
        in_specs=[SMEM, VMEM, VMEM],
        out_specs=VMEM,
        compiler_params=limit(12),
    )(slab.reshape(1), basis_rows, pieces)


def apply_potential(member_ref, own_ref, near_ref, far_ref, both_ref, cols_ref, base_ref, pairs_ref, mask_ref, keep_ref, give_ref, coeffs, total):
    member = member_ref[0]
    quarter = own_ref.shape[1]
    for bits, ref in enumerate((own_ref, near_ref, far_ref, both_ref)):
        at = pl.multiple_of((member ^ bits) * quarter, quarter)
        coeffs[:, pl.ds(at, quarter)] = ref[...]
    potential = split_lanes(
        lax.dot_general(
            coeffs[...], cols_ref[...], (((1,), (1,)), ((), ())), preferred_element_type=F32
        )
    )
    sx = -dy(potential)
    sy = dx(potential)
    mask = mask_ref[...].astype(F32)
    same, two_x, two_y, up, down = (pairs_ref[k] for k in range(5))
    same_x = same * sx
    same_y = same * sy
    right_x = shift_cols(sx, 1)
    right_y = shift_cols(sy, 1)
    up_x = up * shift_rows(right_x, 1)
    up_y = up * shift_rows(right_y, 1)
    down_x = down * shift_rows(right_x, -1)
    down_y = down * shift_rows(right_y, -1)
    back_up_x = shift_rows(shift_cols(up * sx, -1), -1)
    back_up_y = shift_rows(shift_cols(up * sy, -1), -1)
    back_down_x = shift_rows(shift_cols(down * sx, -1), 1)
    back_down_y = shift_rows(shift_cols(down * sy, -1), 1)
    beside = mask * two_x
    gx = (
        shift_cols(mask, 1) * (up_y - same_x - down_y)
        + shift_cols(beside * right_x, 1)
        - shift_cols(mask, -1) * (same_x + back_down_y - back_up_y)
        + shift_cols(beside * shift_cols(sx, -1), -1)
    )
    gy = shift_rows(mask, 1) * (
        up_x - back_down_x + two_y * shift_rows(sy, 2) - same_y
    ) - shift_rows(mask, -1) * (down_x - back_up_x + same_y - shift_rows(two_y * sy, -2))
    scale = -(TIME_STEP**4) / 64.0
    grad = base_ref[...] + scale * (dy(gx) - dx(gy))
    pair = keep_ref.shape[0]
    total[...] = join_lanes(grad[:, : 2 * pair, :])
    core = member % 2
    keep_ref[...] = total[pl.ds(pl.multiple_of(core * pair, pair), pair), :]
    give_ref[...] = total[pl.ds(pl.multiple_of((1 - core) * pair, pair), pair), :]


def gradient_halves(member, parts, basis_cols, base, pairs, mask):
    _, ring, _ = base.shape
    cols, width = basis_cols.shape
    pair = (ring - TILE) // 2
    half = jax.ShapeDtypeStruct((pair, cols), F32)
    return pl.pallas_call(
        apply_potential,
        name="apply_potential",
        out_shape=(half, half),
        in_specs=[SMEM] + [VMEM] * 8,
        out_specs=(VMEM, VMEM),
        scratch_shapes=[
            pltpu.VMEM((ring, width), BF16),
            pltpu.VMEM((2 * pair, cols), F32),
        ],
        compiler_params=limit(24),
    )(member.reshape(1), *parts, basis_cols, base, pairs, mask)


def project(own_ref, other_ref, cols_ref, out_ref):
    total = (own_ref[...] + other_ref[...]).astype(BF16)
    projected = jnp.dot(total, cols_ref[...], preferred_element_type=F32).astype(BF16)
    half = out_ref.shape[3]
    for core in range(2):
        part = projected[:, core * half : (core + 1) * half]
        for chip in range(out_ref.shape[0] // 2):
            for k in range(out_ref.shape[1]):
                out_ref[2 * chip + core, k] = part


def projected_pieces(own, other, basis_cols, members, slabs):
    single = own.shape[0]
    half = basis_cols.shape[1] // 2
    return pl.pallas_call(
        project,
        name="project",
        out_shape=jax.ShapeDtypeStruct((members, slabs, single, half), BF16),
        in_specs=[VMEM] * 3,
        out_specs=VMEM,
        compiler_params=limit(16),
    )(own, other, basis_cols)


def assemble(member_ref, own_ref, far_ref, near_ref, control_ref, basis_ref, kept_ref, sem):
    copy = pltpu.make_async_copy(control_ref, kept_ref, sem)
    copy.start()
    member = member_ref[0]
    quarter = own_ref.shape[1]
    parts = (own_ref[...], near_ref[0], far_ref[...], near_ref[1])
    for bits, part in enumerate(parts):
        at = pl.multiple_of((member ^ bits) * quarter, quarter)
        basis_ref[pl.ds(at, quarter), :] = part.astype(F32).T.astype(BF16)
    copy.wait()


def assembled(member, own, far, near, control):
    rows, _ = own.shape
    width = control.shape[1]
    return pl.pallas_call(
        assemble,
        name="assemble",
        out_shape=(
            jax.ShapeDtypeStruct((width, rows), BF16),
            jax.ShapeDtypeStruct(control.shape, F32),
        ),
        in_specs=[SMEM, VMEM, VMEM, VMEM, HBM],
        out_specs=(VMEM, VMEM),
        scratch_shapes=[pltpu.SemaphoreType.DMA],
        compiler_params=limit(24),
    )(member.reshape(1), own, far, near, in_hbm(control))


def gradient(slab_ref, basis_ref, projected_ref, out_ref):
    rows_out = out_ref.shape[0] - TILE
    width = basis_ref.shape[0]
    half = out_ref.shape[1]
    projected = projected_ref[...]
    block = width // 4
    squares = jnp.zeros((TILE, half), F32)
    for k in range(4):
        part = jnp.dot(
            basis_ref[k * block : (k + 1) * block, :], projected, preferred_element_type=F32
        )
        squares += jnp.sum((part * part).reshape(block // TILE, TILE, half), axis=0)
    at = pl.multiple_of(slab_ref[0] * rows_out, rows_out)
    out_ref[:rows_out] = jnp.dot(
        basis_ref[pl.ds(at, rows_out), :], projected, preferred_element_type=F32
    )
    out_ref[rows_out:] = squares


def gradient_block(slab, basis, projected, rows_out):
    half = projected.shape[1]
    return pl.pallas_call(
        gradient,
        name="gradient",
        out_shape=jax.ShapeDtypeStruct((rows_out + TILE, half), F32),
        in_specs=[SMEM, VMEM, VMEM],
        out_specs=VMEM,
        compiler_params=limit(24),
    )(slab.reshape(1), basis, projected)


def update(core_ref, control_ref, own_ref, other_ref, out_ref):
    rows_out, width = control_ref.shape
    half = width // 2
    total = jnp.sum(own_ref[rows_out:] + other_ref[rows_out:])
    scale = STEP_SIZE * lax.rsqrt(total / (width * width) + EPSILON)
    for turn, ref in enumerate((own_ref, other_ref)):
        at = pl.multiple_of((core_ref[0] ^ turn) * half, half)
        out_ref[:, pl.ds(at, half)] = control_ref[:, pl.ds(at, half)] - ref[:rows_out] * scale


def updated(core, control, own, other):
    return pl.pallas_call(
        update,
        name="update",
        out_shape=jax.ShapeDtypeStruct(control.shape, F32),
        in_specs=[SMEM, VMEM, VMEM, VMEM],
        out_specs=VMEM,
        compiler_params=limit(8),
    )(core.reshape(1), control, own, other)


def partner(value, bit):
    count = lax.axis_size("ens")
    return lax.ppermute(value, "ens", [(i, i ^ bit) for i in range(count)])


def on_device(checkpoints, section_index, targets, sea_mask, basis_rows, basis_cols, control):
    members = lax.axis_size("ens")
    slabs = lax.axis_size("space")
    member = lax.axis_index("ens").astype(jnp.int32)
    slab = lax.axis_index("space").astype(jnp.int32)
    core = member & 1
    chip = member >> 1
    rows_out, width = control.shape
    rows = basis_rows.shape[0]
    quarter = width // members
    half = width // 2
    single = rows // 4

    pieces = pieces_for(member, basis_rows, control, slabs, quarter)
    pieces = lax.all_to_all(pieces, "space", 0, 0)
    up, down = edge_messages(section_index, checkpoints, targets, sea_mask)
    before = lax.ppermute(up, "space", [(i, i + 1) for i in range(slabs - 1)])
    after = lax.ppermute(down, "space", [(i + 1, i) for i in range(slabs - 1)])
    push, pairs, near_rows = inner_pass(section_index, checkpoints, targets, sea_mask, basis_rows)
    own = coeffs_part(slab, near_rows, pieces)
    parts = [own]
    for bits in (1, 2, 3):
        parts.append(partner(own, bits))
    base, pairs, mask = seam_pass(
        section_index, checkpoints, before, after, targets, sea_mask, push, pairs
    )
    keep, give = gradient_halves(member, parts, basis_cols, base, pairs, mask)

    keep = keep + partner(give, 1)
    own_rows = lax.dynamic_slice_in_dim(keep, chip * single, single, 0)
    give = lax.dynamic_slice_in_dim(keep, (1 - chip) * single, single, 0)
    arriving = partner(give, 2)
    cols = held(basis_cols)
    send = projected_pieces(own_rows, arriving, cols, members, slabs)
    got = lax.all_to_all(send.reshape(members * slabs, single, half), ("ens", "space"), 0, 0)
    projected_half = got.reshape(slabs * rows, half)

    part = pieces[:, rows_out : rows_out + rows, :].reshape(slabs, 2, members // 2, single, quarter)
    part = part.transpose(2, 1, 0, 3, 4).reshape(slabs * rows, quarter)
    far = partner(part, 2)
    near = partner(jnp.stack([part, far]), 1)
    basis, kept = assembled(member, part, far, near, control)
    block = gradient_block(slab, basis, projected_half, rows_out)
    other = partner(block, 1)
    return updated(core, kept, block, other)


def solution(mesh):
    return jax.shard_map(
        on_device,
        mesh=mesh,
        in_specs=(
            P("ens", None, None, "space", None),
            P("ens"),
            P("ens", "space", None),
            P("space", None),
            P("space", None),
            P(),
            P("space", None),
        ),
        out_specs=P("space", None),
        check_vma=False,
    )
```

```python
import jax
import jax.numpy as jnp
from jax import lax
from jax.experimental import pallas as pl
from jax.experimental.pallas import tpu as pltpu
from jax.sharding import PartitionSpec as P


DEPTH = 1.0
GRAVITY = 1.0
CORIOLIS = 0.5
FRICTION = 0.1
TIME_STEP = 0.3
STEP_SIZE = 1.0
EPSILON = 1e-06

F32 = jnp.float32
BF16 = jnp.bfloat16
TILE = 8
LANES = 128
MIB = 1 << 20


VMEM = pl.BlockSpec(memory_space=pltpu.VMEM)
SMEM = pl.BlockSpec(memory_space=pltpu.SMEM)
HBM = pl.BlockSpec(memory_space=pltpu.HBM)


def limit(mib):
    return pltpu.CompilerParams(vmem_limit_bytes=mib * MIB)


def tile_rows(shape):
    return lax.broadcasted_iota(jnp.int32, shape, 0)


def split_lanes(field):
    return jnp.stack([field[:, k : k + LANES] for k in range(0, field.shape[1], LANES)])


def join_lanes(field):
    return jnp.concatenate([field[k] for k in range(field.shape[0])], axis=1)


def shift_cols(field, step):
    turned = pltpu.roll(field, (-step) % LANES, 2)
    lane = lax.broadcasted_iota(jnp.int32, field.shape, 2)
    outside = jnp.zeros_like(turned[:1])
    if step > 0:
        beside = jnp.concatenate([turned[1:], outside], axis=0)
        return jnp.where(lane >= LANES - step, beside, turned)
    beside = jnp.concatenate([outside, turned[:-1]], axis=0)
    return jnp.where(lane < -step, beside, turned)


def dx(field):
    return shift_cols(field, 1) - shift_cols(field, -1)


def fetch(source, target, sem):
    copy = pltpu.make_async_copy(source, target, sem)
    copy.start()
    return copy


def pack_edges(index_ref, states_ref, targets_ref, sea_ref, up_ref, down_ref, last, first, seen, sea, sems):
    count, _, _, rows, cols = states_ref.shape
    states = []
    for s in range(count):
        slot = index_ref[s]
        for side, (buffer, row) in enumerate(((last, rows - TILE), (first, 0))):
            source = states_ref.at[s, slot, :, pl.ds(row, TILE), :]
            states.append(fetch(source, buffer.at[s], sems.at[side, s]))
    others = [
        fetch(targets_ref.at[:, pl.ds(rows - TILE, TILE), :], seen.at[0], sems.at[0, count]),
        fetch(targets_ref.at[:, pl.ds(0, TILE), :], seen.at[1], sems.at[1, count]),
        fetch(sea_ref.at[pl.ds(rows - TILE, TILE), :], sea.at[0], sems.at[0, count + 1]),
        fetch(sea_ref.at[pl.ds(0, TILE), :], sea.at[1], sems.at[1, count + 1]),
    ]
    row = tile_rows((TILE, cols))
    for s in range(count):
        states[2 * s].wait()
        height, east, north = (last[s, f].astype(F32) for f in range(3))
        height, north = pltpu.roll(height, 3, 0), pltpu.roll(north, 6, 0)
        up_ref[s] = jnp.where(row < 3, height, jnp.where(row < 6, north, east)).astype(BF16)
        states[2 * s + 1].wait()
        height, east, north = (first[s, f].astype(F32) for f in range(3))
        east, north = pltpu.roll(east, 6, 0), pltpu.roll(north, 3, 0)
        down_ref[s] = jnp.where(row < 3, height, jnp.where(row < 6, north, east)).astype(BF16)
    for copy in others:
        copy.wait()
    targets_up = jnp.zeros((TILE, cols), F32)
    targets_down = jnp.zeros((TILE, cols), F32)
    for s in range(count):
        targets_up = jnp.where(row == s, seen[0, s].astype(F32)[TILE - 1 :, :], targets_up)
        targets_down = jnp.where(row == s, seen[1, s].astype(F32)[:1, :], targets_down)
    up_ref[count] = targets_up.astype(BF16)
    down_ref[count] = targets_down.astype(BF16)
    up_ref[count + 1] = sea[0].astype(F32).astype(BF16)
    down_ref[count + 1] = sea[1].astype(F32).astype(BF16)


def edge_messages(section_index, checkpoints, targets, sea_mask):
    count, _, fields, _, cols = checkpoints.shape
    edges = jax.ShapeDtypeStruct((count + 2, TILE, cols), BF16)
    return pl.pallas_call(
        pack_edges,
        name="pack_edges",
        out_shape=(edges, edges),
        in_specs=[SMEM] + [HBM] * 3,
        out_specs=(VMEM, VMEM),
        scratch_shapes=[
            pltpu.VMEM((count, fields, TILE, cols), BF16),
            pltpu.VMEM((count, fields, TILE, cols), BF16),
            pltpu.VMEM((2, count, TILE, cols), BF16),
            pltpu.VMEM((2, TILE, cols), jnp.int32),
            pltpu.SemaphoreType.DMA((2, count + 2)),
        ],
        compiler_params=limit(12),
    )(*map(in_hbm, (section_index, checkpoints, targets, sea_mask)))


def pack_pieces(member_ref, basis_ref, control_ref, out_ref, basis, own, sems):
    rows, width = basis_ref.shape
    rows_out = control_ref.shape[0]
    slabs, _, quarter = out_ref.shape
    at = pl.multiple_of(member_ref[0] * quarter, quarter)
    copies = [
        fetch(control_ref.at[:, pl.ds(at, quarter)], own, sems.at[0]),
        fetch(basis_ref, basis, sems.at[1]),
    ]
    for copy in copies:
        copy.wait()
    part = own[...].astype(BF16)
    part_basis = basis[:, pl.ds(at, quarter)]
    row = tile_rows((TILE, width))
    first = basis[:TILE, :].astype(F32)
    last = pltpu.roll(basis[rows - TILE :, :].astype(F32), 4, 0)
    both = jnp.where(row < 2, first, last)
    tiles = []
    for q in range(0, width // quarter, 2):
        here = both[:, q * quarter : (q + 1) * quarter]
        below = pltpu.roll(both[:, (q + 1) * quarter : (q + 2) * quarter], 4, 0)
        tiles.append(jnp.where(row[:, :quarter] < 4, here, below))
    edges = jnp.concatenate(tiles, axis=0).astype(BF16)
    for k in range(slabs):
        out_ref[k, :rows_out] = part
        out_ref[k, rows_out : rows_out + rows] = part_basis
        out_ref[k, rows_out + rows :] = edges


def pieces_for(member, basis_rows, control, slabs, quarter):
    rows, width = basis_rows.shape
    rows_out = control.shape[0]
    edges = 4 * width // quarter
    return pl.pallas_call(
        pack_pieces,
        name="pack_pieces",
        out_shape=jax.ShapeDtypeStruct((slabs, rows_out + rows + edges, quarter), BF16),
        in_specs=[SMEM, HBM, HBM],
        out_specs=VMEM,
        scratch_shapes=[
            pltpu.VMEM((rows, width), BF16),
            pltpu.VMEM((rows_out, quarter), F32),
            pltpu.SemaphoreType.DMA((2,)),
        ],
        compiler_params=limit(10),
    )(member.reshape(1), in_hbm(basis_rows), in_hbm(control))


def in_hbm(array):
    return pltpu.with_memory_space_constraint(array, pltpu.HBM)


def hold(source_ref, out_ref, sem):
    copy = pltpu.make_async_copy(source_ref, out_ref, sem)
    copy.start()
    copy.wait()


def held(array):
    size = array.size * array.dtype.itemsize
    return pl.pallas_call(
        hold,
        name="hold",
        out_shape=jax.ShapeDtypeStruct(array.shape, array.dtype),
        in_specs=[HBM],
        out_specs=VMEM,
        scratch_shapes=[pltpu.SemaphoreType.DMA],
        compiler_params=limit(size // MIB + 2),
    )(in_hbm(array))


PAIRS = 5


class Rows:
    def __init__(self, ref):
        self.ref = ref

    def put(self, tile, value):
        self.ref[:, TILE * (tile + 1) : TILE * (tile + 2), :] = value

    def put_at(self, start, value):
        self.ref[:, start : start + value.shape[1], :] = value

    def get(self, tile, step=0):
        start = TILE * (tile + 1) + step
        return self.ref[:, start : start + TILE, :]


class Ring(Rows):
    def put(self, tile, value):
        super().put(tile, value)
        rows = self.ref.shape[1]
        if tile == 0:
            self.ref[:, rows - TILE :, :] = value
        if TILE * (tile + 3) == rows:
            self.ref[:, :TILE, :] = value


def rows_of(tile):
    return slice(TILE * tile, TILE * (tile + 1))


def clear(*refs):
    for ref in refs:
        ref[...] = jnp.zeros_like(ref)


def add_state(tiles, state, mask, live, padded, plain, sums):
    heights, easts, norths, seens = state
    fluxes, mid_fluxes, weights, rights, misfits = (Rows(ref) for ref in padded)
    lefts, partial = plain
    push_left, push_right, gy, same, two_x, two_y, up, down = sums
    half = 0.5 * TIME_STEP
    keep = 1.0 - TIME_STEP * FRICTION
    turn = TIME_STEP * CORIOLIS / keep
    slope = half * GRAVITY / keep

    for tile in range(tiles):
        fluxes.put(tile, (DEPTH + heights.get(tile)) * norths.get(tile))

    for tile in range(tiles):
        here = rows_of(tile)
        height = heights.get(tile)
        east = easts.get(tile)
        north = norths.get(tile)
        flux = dx((DEPTH + height) * east) + (fluxes.get(tile, 1) - fluxes.get(tile, -1))
        sea = mask[:, here, :]
        height_mid = sea * (height - half * flux)
        weight = DEPTH * sea + height_mid
        east_mid = east + turn * north - slope * dx(height)
        north_mid = north - turn * east - slope * (heights.get(tile, 1) - heights.get(tile, -1))
        right = shift_cols(weight, 1)
        left = shift_cols(weight, -1)
        scaled = half * keep * weight
        mid_fluxes.put(tile, scaled * north_mid)
        weights.put(tile, weight)
        rights.put(tile, right)
        lefts[:, here, :] = left
        same[:, here, :] += weight * weight
        two_x[:, here, :] += left * right
        partial[:, here, :] = (
            height + height_mid - 2.0 * seens.get(tile) - dx(scaled * east_mid)
        )

    for tile in range(tiles):
        here = rows_of(tile)
        change = mid_fluxes.get(tile, 1) - mid_fluxes.get(tile, -1)
        misfit = live[:, here, :] * (partial[:, here, :] - change)
        misfits.put(tile, misfit)
        push_left[:, here, :] += lefts[:, here, :] * misfit
        push_right[:, here, :] += rights.get(tile) * misfit

    for tile in range(tiles):
        here = rows_of(tile)
        weight = weights.get(tile)
        gy[:, here, :] += weight * (misfits.get(tile, 1) - misfits.get(tile, -1))
        two_y[:, here, :] += weight * weights.get(tile, 2)
        up[:, here, :] += weight * rights.get(tile, 1)
        down[:, here, :] += weight * rights.get(tile, -1)


def inner_states(index_ref, states_ref, targets_ref, sea_ref, basis_ref, push_ref, pairs_ref, rows_ref, sems, sea, held_states, held_targets, mask, live, *scratch):
    count = states_ref.shape[0]
    rows = sea_ref.shape[0]
    tiles = rows // TILE
    plain, padded = scratch[:2], scratch[2:]

    def copies_of(k):
        return (
            pltpu.make_async_copy(states_ref.at[k, index_ref[k]], held_states.at[k], sems.at[0, k]),
            pltpu.make_async_copy(targets_ref.at[k], held_targets.at[k], sems.at[1, k]),
        )

    others = (
        pltpu.make_async_copy(sea_ref, sea, sems.at[0, count]),
        pltpu.make_async_copy(basis_ref, rows_ref, sems.at[1, count]),
    )
    for copy in others:
        copy.start()
    for k in range(count):
        for copy in copies_of(k):
            copy.start()
    clear(push_ref, pairs_ref, *padded)
    for copy in others:
        copy.wait()
    for tile in range(tiles):
        mask[:, rows_of(tile), :] = split_lanes(sea[rows_of(tile), :].astype(F32))
    row = lax.broadcasted_iota(jnp.int32, live.shape, 1)
    live[...] = jnp.where((row >= 2) & (row < rows - 2), mask[...], 0.0)

    @pl.loop(0, count)
    def _(s):
        for copy in copies_of(s):
            copy.wait()
        state = [Rows(ref) for ref in padded[:4]]
        for tile in range(tiles):
            for field in range(3):
                value = held_states[s, field, rows_of(tile), :].astype(F32)
                state[field].put(tile, split_lanes(value))
            state[3].put(tile, split_lanes(held_targets[s, rows_of(tile), :].astype(F32)))
        sums = [push_ref.at[k] for k in range(3)] + [pairs_ref.at[k] for k in range(PAIRS)]
        add_state(tiles, state, mask, live, padded[4:], plain, sums)


def inner_pass(section_index, checkpoints, targets, sea_mask, basis_rows):
    count, _, fields, rows, cols = checkpoints.shape
    width = basis_rows.shape[1]
    lanes = cols // LANES
    padded = pltpu.VMEM((lanes, rows + 2 * TILE, LANES), F32)
    plain = pltpu.VMEM((lanes, rows, LANES), F32)
    outs = (
        jax.ShapeDtypeStruct((3, lanes, rows, LANES), F32),
        jax.ShapeDtypeStruct((PAIRS, lanes, rows, LANES), F32),
        jax.ShapeDtypeStruct((rows, width), BF16),
    )
    return pl.pallas_call(
        inner_states,
        name="inner_states",
        out_shape=outs,
        in_specs=[SMEM] + [HBM] * 4,
        out_specs=(VMEM,) * 3,
        scratch_shapes=[
            pltpu.SemaphoreType.DMA((2, count + 1)),
            pltpu.VMEM((rows, cols), jnp.int32),
            pltpu.VMEM((count, fields, rows, cols), BF16),
            pltpu.VMEM((count, rows, cols), BF16),
        ]
        + [plain] * 4
        + [padded] * 9,
        compiler_params=limit(24),
    )(*map(in_hbm, (section_index, checkpoints, targets, sea_mask, basis_rows)))


def seam_states(index_ref, states_ref, targets_ref, sea_ref, before_ref, after_ref, push_in_ref, pairs_in_ref, push_ref, pairs_ref, mask_ref, sems, sea, ends, seen_ends, seen_edge, mask, live, lefts, partial, sums_ref, *padded):
    count = states_ref.shape[0]
    rows, cols = sea_ref.shape
    row = tile_rows((TILE, cols))
    top = row < 4

    def copies_of(k):
        for side, start in enumerate((rows - TILE, 0)):
            here = pl.ds(start, TILE)
            yield pltpu.make_async_copy(
                states_ref.at[k, index_ref[k], :, here, :], ends.at[k, side], sems.at[side, k]
            )
            yield pltpu.make_async_copy(
                targets_ref.at[k, here, :], seen_ends.at[k, side], sems.at[2 + side, k]
            )

    fetched = pltpu.make_async_copy(sea_ref, sea, sems.at[0, count])
    fetched.start()
    for k in range(count):
        for copy in copies_of(k):
            copy.start()
    clear(sums_ref, *padded)
    seen_edge[0] = split_lanes(before_ref[count].astype(F32))
    seen_edge[1] = split_lanes(after_ref[count].astype(F32))
    after = jnp.where(row < 2, after_ref[count + 1].astype(F32), 0.0)
    before = jnp.where(row >= 6, before_ref[count + 1].astype(F32), 0.0)
    beyond = after + before
    fetched.wait()
    turned = pltpu.roll(beyond, 4, 0)
    last = pltpu.roll(sea[rows - TILE :, :].astype(F32), 4, 0)
    first = pltpu.roll(sea[:TILE, :].astype(F32), 4, 0)
    mask[:, :TILE, :] = split_lanes(jnp.where(top, last, turned))
    mask[:, TILE:, :] = split_lanes(jnp.where(top, turned, first))
    for tile in range(rows // TILE):
        mask_ref[:, rows_of(tile), :] = split_lanes(
            sea[rows_of(tile), :].astype(F32)
        ).astype(BF16)
    mask_ref[:, rows:, :] = split_lanes(beyond).astype(BF16)
    place = lax.broadcasted_iota(jnp.int32, live.shape, 1)
    counts = ((place >= 2) & (place < 5)) | ((place >= 11) & (place < 14))
    live[...] = jnp.where(counts, mask[...], 0.0)

    @pl.loop(0, count)
    def _(s):
        state = [Rows(ref) for ref in padded[:4]]
        after = split_lanes(after_ref[s].astype(F32))
        before = split_lanes(before_ref[s].astype(F32))
        for copy in copies_of(s):
            copy.wait()
        state[0].put_at(12, after)
        state[0].put_at(17, before)
        state[1].put_at(12, before)
        state[1].put_at(6, after)
        state[2].put_at(14, before)
        state[2].put_at(9, after)
        state[3].put_at(12, seen_edge[1, :, pl.ds(s, 1), :])
        state[3].put_at(19, seen_edge[0, :, pl.ds(s, 1), :])
        for field in range(3):
            state[field].put_at(4, split_lanes(ends[s, 0, field].astype(F32)))
            state[field].put_at(20, split_lanes(ends[s, 1, field].astype(F32)))
        state[3].put_at(4, split_lanes(seen_ends[s, 0].astype(F32)))
        state[3].put_at(20, split_lanes(seen_ends[s, 1].astype(F32)))
        sums = [sums_ref.at[k] for k in range(3 + PAIRS)]
        add_state(2, state, mask, live, padded[4:], (lefts, partial), sums)

    place = lax.broadcasted_iota(jnp.int32, (lefts.shape[0], TILE, LANES), 1)
    top = place < 4
    final = rows // TILE - 1

    def ring(inner, outer, out, bounds):
        ending = pltpu.roll(outer[:, :TILE, :], 4, 1)
        opening = pltpu.roll(outer[:, TILE:, :], 4, 1)
        for tile in range(1, final):
            out[:, rows_of(tile), :] = inner[:, rows_of(tile), :]
        head = inner[:, :TILE, :]
        tail = inner[:, rows_of(final), :]
        if bounds is None:
            head = head + jnp.where(top, opening, 0.0)
            tail = tail + jnp.where(top, 0.0, ending)
        else:
            head = jnp.where(place < bounds[0], opening, head)
            tail = jnp.where(place > bounds[1], ending, tail)
        out[:, :TILE, :] = head
        out[:, rows_of(final), :] = tail
        out[:, rows:, :] = jnp.where(top, ending, opening)

    for k in range(3):
        ring(push_in_ref[k], sums_ref[k], push_ref.at[k], None)
    for k in range(PAIRS):
        bounds = (2, 5) if k == PAIRS - 1 else (1, 4)
        ring(pairs_in_ref[k], sums_ref[3 + k], pairs_ref.at[k], bounds)


def seam_pass(section_index, checkpoints, before, after, targets, sea_mask, push, pairs):
    count, _, fields, rows, cols = checkpoints.shape
    lanes = cols // LANES
    ring = rows + TILE
    plain = pltpu.VMEM((lanes, 2 * TILE, LANES), F32)
    padded = pltpu.VMEM((lanes, 4 * TILE, LANES), F32)
    outs = (
        jax.ShapeDtypeStruct((3, lanes, ring, LANES), F32),
        jax.ShapeDtypeStruct((PAIRS, lanes, ring, LANES), F32),
        jax.ShapeDtypeStruct((lanes, ring, LANES), BF16),
    )

    return pl.pallas_call(
        seam_states,
        name="seam_states",
        out_shape=outs,
        in_specs=[SMEM] + [HBM] * 3 + [VMEM] * 4,
        out_specs=(VMEM,) * 3,
        scratch_shapes=[
            pltpu.SemaphoreType.DMA((4, count + 1)),
            pltpu.VMEM((rows, cols), jnp.int32),
            pltpu.VMEM((count, 2, fields, TILE, cols), BF16),
            pltpu.VMEM((count, 2, TILE, cols), BF16),
            pltpu.VMEM((2, lanes, TILE, LANES), F32),
        ]
        + [plain] * 4
        + [pltpu.VMEM((3 + PAIRS, lanes, 2 * TILE, LANES), F32)]
        + [padded] * 9,
        compiler_params=limit(24),
    )(
        *map(in_hbm, (section_index, checkpoints, targets, sea_mask)),
        before,
        after,
        push,
        pairs,
    )


def make_coeffs(slab_ref, basis_ref, pieces_ref, out_ref):
    slabs, _, quarter = pieces_ref.shape
    rows, width = basis_ref.shape
    rows_out = width // slabs
    slab = slab_ref[0]

    def edge_of(k):
        parts = []
        for q in range(width // quarter):
            start = rows_out + rows + TILE * (q // 2)
            part = pieces_ref[k, start : start + TILE, :].astype(F32)
            parts.append(pltpu.roll(part, 4, 0) if q % 2 else part)
        return jnp.concatenate(parts, axis=1)

    after = edge_of(jnp.minimum(slab + 1, slabs - 1))
    before = pltpu.roll(edge_of(jnp.maximum(slab - 1, 0)), 4, 0)
    row = tile_rows((TILE, width))
    use_after = (row < 2) & (slab < slabs - 1)
    use_before = (row >= 6) & (slab > 0)
    edge = jnp.where(use_after, after, jnp.where(use_before, before, 0.0))
    basis = jnp.concatenate([basis_ref[...].astype(F32), edge], axis=0).astype(BF16)
    part = pieces_ref[:, :rows_out, :].reshape(width, quarter)
    out_ref[...] = jnp.dot(basis, part, preferred_element_type=F32).astype(BF16)


def coeffs_part(slab, basis_rows, pieces):
    return pl.pallas_call(
        make_coeffs,
        name="make_coeffs",
        out_shape=jax.ShapeDtypeStruct((basis_rows.shape[0] + TILE, pieces.shape[2]), BF16),
        in_specs=[SMEM, VMEM, VMEM],
        out_specs=VMEM,
        compiler_params=limit(12),
    )(slab.reshape(1), basis_rows, pieces)


def apply_potential(member_ref, own_ref, near_ref, far_ref, both_ref, cols_ref, push_ref, pairs_ref, mask_ref, keep_ref, give_ref, coeffs, total, field, east, part, gy, *rings):
    member = member_ref[0]
    quarter = own_ref.shape[1]
    for bits, ref in enumerate((own_ref, near_ref, far_ref, both_ref)):
        at = pl.multiple_of((member ^ bits) * quarter, quarter)
        coeffs[:, pl.ds(at, quarter)] = ref[...]
    field[...] = lax.dot_general(
        coeffs[...], cols_ref[...], (((1,), (1,)), ((), ())), preferred_element_type=F32
    )
    same, two_x, two_y, up, down = (pairs_ref.at[k] for k in range(PAIRS))
    potential, masks, right_xs, right_ys, norths, two_norths, gx = (
        Ring(ref) for ref in rings[:7]
    )
    back_up_x, back_up_y, back_down_x, back_down_y = (Ring(ref) for ref in rings[7:])
    tiles = field.shape[0] // TILE
    own_tiles = tiles - 1
    unit = -4.0 / TIME_STEP**2

    for tile in range(tiles):
        potential.put(tile, split_lanes(field[rows_of(tile), :]))
        masks.put(tile, mask_ref[:, rows_of(tile), :].astype(F32))

    for tile in range(tiles):
        here = rows_of(tile)
        sx = potential.get(tile, -1) - potential.get(tile, 1)
        sy = dx(potential.get(tile))
        east[:, here, :] = sx
        right_x = shift_cols(sx, 1)
        right_xs.put(tile, right_x)
        right_ys.put(tile, shift_cols(sy, 1))
        norths.put(tile, sy)
        two_norths.put(tile, two_y[:, here, :] * sy)
        up_here = up[:, here, :]
        down_here = down[:, here, :]
        back_up_x.put(tile, shift_cols(up_here * sx, -1))
        back_up_y.put(tile, shift_cols(up_here * sy, -1))
        back_down_x.put(tile, shift_cols(down_here * sx, -1))
        back_down_y.put(tile, shift_cols(down_here * sy, -1))
        beside = masks.get(tile) * two_x[:, here, :]
        part[:, here, :] = shift_cols(
            beside * right_x + unit * push_ref[0, :, here, :], 1
        ) + shift_cols(beside * shift_cols(sx, -1) - unit * push_ref[1, :, here, :], -1)

    for tile in range(tiles):
        here = rows_of(tile)
        mask = masks.get(tile)
        same_x = same[:, here, :] * east[:, here, :]
        up_here = up[:, here, :]
        down_here = down[:, here, :]
        ahead = up_here * right_ys.get(tile, 1) - same_x - down_here * right_ys.get(tile, -1)
        behind = same_x + back_down_y.get(tile, 1) - back_up_y.get(tile, -1)
        gx.put(
            tile,
            part[:, here, :] + shift_cols(mask, 1) * ahead - shift_cols(mask, -1) * behind,
        )
        if tile < own_tiles:
            same_y = same[:, here, :] * norths.get(tile)
            ahead = (
                up_here * right_xs.get(tile, 1)
                - back_down_x.get(tile, 1)
                + two_y[:, here, :] * norths.get(tile, 2)
                - same_y
            )
            behind = (
                down_here * right_xs.get(tile, -1)
                - back_up_x.get(tile, -1)
                + same_y
                - two_norths.get(tile, -2)
            )
            gy[:, here, :] = (
                unit * push_ref[2, :, here, :]
                + masks.get(tile, 1) * ahead
                - masks.get(tile, -1) * behind
            )

    scale = -(TIME_STEP**4) / 64.0
    for tile in range(own_tiles):
        here = rows_of(tile)
        total[here, :] = join_lanes(
            scale * (gx.get(tile, 1) - gx.get(tile, -1) - dx(gy[:, here, :]))
        )
    pair = keep_ref.shape[0]
    core = member % 2
    keep_ref[...] = total[pl.ds(pl.multiple_of(core * pair, pair), pair), :]
    give_ref[...] = total[pl.ds(pl.multiple_of((1 - core) * pair, pair), pair), :]


def gradient_halves(member, parts, basis_cols, push, pairs, mask):
    lanes, ring, _ = mask.shape
    cols, width = basis_cols.shape
    pair = (ring - TILE) // 2
    half = jax.ShapeDtypeStruct((pair, cols), F32)
    return pl.pallas_call(
        apply_potential,
        name="apply_potential",
        out_shape=(half, half),
        in_specs=[SMEM] + [VMEM] * 8,
        out_specs=(VMEM, VMEM),
        scratch_shapes=[
            pltpu.VMEM((ring, width), BF16),
            pltpu.VMEM((2 * pair, cols), F32),
            pltpu.VMEM((ring, cols), F32),
        ]
        + [pltpu.VMEM((lanes, ring, LANES), F32)] * 3
        + [pltpu.VMEM((lanes, ring + 2 * TILE, LANES), F32)] * 11,
        compiler_params=limit(24),
    )(member.reshape(1), *parts, basis_cols, push, pairs, mask)


def project(own_ref, other_ref, cols_ref, out_ref):
    total = (own_ref[...] + other_ref[...]).astype(BF16)
    projected = jnp.dot(total, cols_ref[...], preferred_element_type=F32).astype(BF16)
    half = out_ref.shape[3]
    for core in range(2):
        part = projected[:, core * half : (core + 1) * half]
        for chip in range(out_ref.shape[0] // 2):
            for k in range(out_ref.shape[1]):
                out_ref[2 * chip + core, k] = part


def projected_pieces(own, other, basis_cols, members, slabs):
    single = own.shape[0]
    half = basis_cols.shape[1] // 2
    return pl.pallas_call(
        project,
        name="project",
        out_shape=jax.ShapeDtypeStruct((members, slabs, single, half), BF16),
        in_specs=[VMEM] * 3,
        out_specs=VMEM,
        compiler_params=limit(16),
    )(own, other, basis_cols)


def assemble(member_ref, own_ref, far_ref, near_ref, control_ref, basis_ref, kept_ref, sem):
    copy = pltpu.make_async_copy(control_ref, kept_ref, sem)
    copy.start()
    member = member_ref[0]
    quarter = own_ref.shape[1]
    parts = (own_ref[...], near_ref[0], far_ref[...], near_ref[1])
    for bits, part in enumerate(parts):
        at = pl.multiple_of((member ^ bits) * quarter, quarter)
        basis_ref[pl.ds(at, quarter), :] = part.astype(F32).T.astype(BF16)
    copy.wait()


def assembled(member, own, far, near, control):
    rows, _ = own.shape
    width = control.shape[1]
    return pl.pallas_call(
        assemble,
        name="assemble",
        out_shape=(
            jax.ShapeDtypeStruct((width, rows), BF16),
            jax.ShapeDtypeStruct(control.shape, F32),
        ),
        in_specs=[SMEM, VMEM, VMEM, VMEM, HBM],
        out_specs=(VMEM, VMEM),
        scratch_shapes=[pltpu.SemaphoreType.DMA],
        compiler_params=limit(24),
    )(member.reshape(1), own, far, near, in_hbm(control))


def gradient(slab_ref, basis_ref, projected_ref, out_ref):
    rows_out = out_ref.shape[0] - TILE
    width = basis_ref.shape[0]
    half = out_ref.shape[1]
    projected = projected_ref[...]
    block = width // 4
    squares = jnp.zeros((TILE, half), F32)
    for k in range(4):
        part = jnp.dot(
            basis_ref[k * block : (k + 1) * block, :], projected, preferred_element_type=F32
        )
        squares += jnp.sum((part * part).reshape(block // TILE, TILE, half), axis=0)
    at = pl.multiple_of(slab_ref[0] * rows_out, rows_out)
    out_ref[:rows_out] = jnp.dot(
        basis_ref[pl.ds(at, rows_out), :], projected, preferred_element_type=F32
    )
    out_ref[rows_out:] = squares


def gradient_block(slab, basis, projected, rows_out):
    half = projected.shape[1]
    return pl.pallas_call(
        gradient,
        name="gradient",
        out_shape=jax.ShapeDtypeStruct((rows_out + TILE, half), F32),
        in_specs=[SMEM, VMEM, VMEM],
        out_specs=VMEM,
        compiler_params=limit(24),
    )(slab.reshape(1), basis, projected)


def update(core_ref, control_ref, own_ref, other_ref, out_ref):
    rows_out, width = control_ref.shape
    half = width // 2
    total = jnp.sum(own_ref[rows_out:] + other_ref[rows_out:])
    scale = STEP_SIZE * lax.rsqrt(total / (width * width) + EPSILON)
    for turn, ref in enumerate((own_ref, other_ref)):
        at = pl.multiple_of((core_ref[0] ^ turn) * half, half)
        out_ref[:, pl.ds(at, half)] = control_ref[:, pl.ds(at, half)] - ref[:rows_out] * scale


def updated(core, control, own, other):
    return pl.pallas_call(
        update,
        name="update",
        out_shape=jax.ShapeDtypeStruct(control.shape, F32),
        in_specs=[SMEM, VMEM, VMEM, VMEM],
        out_specs=VMEM,
        compiler_params=limit(8),
    )(core.reshape(1), control, own, other)


def partner(value, bit):
    count = lax.axis_size("ens")
    return lax.ppermute(value, "ens", [(i, i ^ bit) for i in range(count)])


def on_device(checkpoints, section_index, targets, sea_mask, basis_rows, basis_cols, control):
    members = lax.axis_size("ens")
    slabs = lax.axis_size("space")
    member = lax.axis_index("ens").astype(jnp.int32)
    slab = lax.axis_index("space").astype(jnp.int32)
    core = member & 1
    chip = member >> 1
    rows_out, width = control.shape
    rows = basis_rows.shape[0]
    quarter = width // members
    half = width // 2
    single = rows // 4

    pieces = pieces_for(member, basis_rows, control, slabs, quarter)
    pieces = lax.all_to_all(pieces, "space", 0, 0)
    up, down = edge_messages(section_index, checkpoints, targets, sea_mask)
    before = lax.ppermute(up, "space", [(i, i + 1) for i in range(slabs - 1)])
    after = lax.ppermute(down, "space", [(i + 1, i) for i in range(slabs - 1)])
    push, pairs, near_rows = inner_pass(section_index, checkpoints, targets, sea_mask, basis_rows)
    own = coeffs_part(slab, near_rows, pieces)
    parts = [own]
    for bits in (1, 2, 3):
        parts.append(partner(own, bits))
    push, pairs, mask = seam_pass(
        section_index, checkpoints, before, after, targets, sea_mask, push, pairs
    )
    keep, give = gradient_halves(member, parts, basis_cols, push, pairs, mask)

    keep = keep + partner(give, 1)
    own_rows = lax.dynamic_slice_in_dim(keep, chip * single, single, 0)
    give = lax.dynamic_slice_in_dim(keep, (1 - chip) * single, single, 0)
    arriving = partner(give, 2)
    cols = held(basis_cols)
    send = projected_pieces(own_rows, arriving, cols, members, slabs)
    got = lax.all_to_all(send.reshape(members * slabs, single, half), ("ens", "space"), 0, 0)
    projected_half = got.reshape(slabs * rows, half)

    part = pieces[:, rows_out : rows_out + rows, :].reshape(slabs, 2, members // 2, single, quarter)
    part = part.transpose(2, 1, 0, 3, 4).reshape(slabs * rows, quarter)
    far = partner(part, 2)
    near = partner(jnp.stack([part, far]), 1)
    basis, kept = assembled(member, part, far, near, control)
    block = gradient_block(slab, basis, projected_half, rows_out)
    other = partner(block, 1)
    return updated(core, kept, block, other)


def solution(mesh):
    return jax.shard_map(
        on_device,
        mesh=mesh,
        in_specs=(
            P("ens", None, None, "space", None),
            P("ens"),
            P("ens", "space", None),
            P("space", None),
            P("space", None),
            P(),
            P("space", None),
        ),
        out_specs=P("space", None),
        check_vma=False,
    )
```

```python
import jax
import jax.numpy as jnp
from jax import lax
from jax.experimental import pallas as pl
from jax.experimental.pallas import tpu as pltpu
from jax.sharding import PartitionSpec as P


DEPTH = 1.0
GRAVITY = 1.0
CORIOLIS = 0.5
FRICTION = 0.1
TIME_STEP = 0.3
STEP_SIZE = 1.0
EPSILON = 1e-06

F32 = jnp.float32
BF16 = jnp.bfloat16
TILE = 8
LANES = 128
MIB = 1 << 20


VMEM = pl.BlockSpec(memory_space=pltpu.VMEM)
SMEM = pl.BlockSpec(memory_space=pltpu.SMEM)
HBM = pl.BlockSpec(memory_space=pltpu.HBM)


def limit(mib):
    return pltpu.CompilerParams(vmem_limit_bytes=mib * MIB)


def tile_rows(shape):
    return lax.broadcasted_iota(jnp.int32, shape, 0)


def split_lanes(field):
    return jnp.stack([field[:, k : k + LANES] for k in range(0, field.shape[1], LANES)])


def join_lanes(field):
    return jnp.concatenate([field[k] for k in range(field.shape[0])], axis=1)


def shift_cols(field, step):
    turned = pltpu.roll(field, (-step) % LANES, 2)
    lane = lax.broadcasted_iota(jnp.int32, field.shape, 2)
    outside = jnp.zeros_like(turned[:1])
    if step > 0:
        beside = jnp.concatenate([turned[1:], outside], axis=0)
        return jnp.where(lane >= LANES - step, beside, turned)
    beside = jnp.concatenate([outside, turned[:-1]], axis=0)
    return jnp.where(lane < -step, beside, turned)


def dx(field):
    return shift_cols(field, 1) - shift_cols(field, -1)


def fetch(source, target, sem):
    copy = pltpu.make_async_copy(source, target, sem)
    copy.start()
    return copy


def pack_edges(index_ref, states_ref, targets_ref, sea_ref, up_ref, down_ref, last, first, seen, sea, sems):
    count, _, _, rows, cols = states_ref.shape
    states = []
    for s in range(count):
        slot = index_ref[s]
        for side, (buffer, row) in enumerate(((last, rows - TILE), (first, 0))):
            source = states_ref.at[s, slot, :, pl.ds(row, TILE), :]
            states.append(fetch(source, buffer.at[s], sems.at[side, s]))
    others = [
        fetch(targets_ref.at[:, pl.ds(rows - TILE, TILE), :], seen.at[0], sems.at[0, count]),
        fetch(targets_ref.at[:, pl.ds(0, TILE), :], seen.at[1], sems.at[1, count]),
        fetch(sea_ref.at[pl.ds(rows - TILE, TILE), :], sea.at[0], sems.at[0, count + 1]),
        fetch(sea_ref.at[pl.ds(0, TILE), :], sea.at[1], sems.at[1, count + 1]),
    ]
    row = tile_rows((TILE, cols))
    for s in range(count):
        states[2 * s].wait()
        height, east, north = (last[s, f].astype(F32) for f in range(3))
        height, north = pltpu.roll(height, 3, 0), pltpu.roll(north, 6, 0)
        up_ref[s] = jnp.where(row < 3, height, jnp.where(row < 6, north, east)).astype(BF16)
        states[2 * s + 1].wait()
        height, east, north = (first[s, f].astype(F32) for f in range(3))
        east, north = pltpu.roll(east, 6, 0), pltpu.roll(north, 3, 0)
        down_ref[s] = jnp.where(row < 3, height, jnp.where(row < 6, north, east)).astype(BF16)
    for copy in others:
        copy.wait()
    targets_up = jnp.zeros((TILE, cols), F32)
    targets_down = jnp.zeros((TILE, cols), F32)
    for s in range(count):
        targets_up = jnp.where(row == s, seen[0, s].astype(F32)[TILE - 1 :, :], targets_up)
        targets_down = jnp.where(row == s, seen[1, s].astype(F32)[:1, :], targets_down)
    up_ref[count] = targets_up.astype(BF16)
    down_ref[count] = targets_down.astype(BF16)
    up_ref[count + 1] = sea[0].astype(F32).astype(BF16)
    down_ref[count + 1] = sea[1].astype(F32).astype(BF16)


def edge_messages(section_index, checkpoints, targets, sea_mask):
    count, _, fields, _, cols = checkpoints.shape
    edges = jax.ShapeDtypeStruct((count + 2, TILE, cols), BF16)
    return pl.pallas_call(
        pack_edges,
        name="pack_edges",
        out_shape=(edges, edges),
        in_specs=[SMEM] + [HBM] * 3,
        out_specs=(VMEM, VMEM),
        scratch_shapes=[
            pltpu.VMEM((count, fields, TILE, cols), BF16),
            pltpu.VMEM((count, fields, TILE, cols), BF16),
            pltpu.VMEM((2, count, TILE, cols), BF16),
            pltpu.VMEM((2, TILE, cols), jnp.int32),
            pltpu.SemaphoreType.DMA((2, count + 2)),
        ],
        compiler_params=limit(12),
    )(*map(in_hbm, (section_index, checkpoints, targets, sea_mask)))


def pack_pieces(member_ref, basis_ref, control_ref, out_ref, basis, own, sems):
    rows, width = basis_ref.shape
    rows_out = control_ref.shape[0]
    slabs, _, quarter = out_ref.shape
    at = pl.multiple_of(member_ref[0] * quarter, quarter)
    copies = [
        fetch(control_ref.at[:, pl.ds(at, quarter)], own, sems.at[0]),
        fetch(basis_ref, basis, sems.at[1]),
    ]
    for copy in copies:
        copy.wait()
    part = own[...].astype(BF16)
    part_basis = basis[:, pl.ds(at, quarter)]
    row = tile_rows((TILE, width))
    first = basis[:TILE, :].astype(F32)
    last = pltpu.roll(basis[rows - TILE :, :].astype(F32), 4, 0)
    both = jnp.where(row < 2, first, last)
    tiles = []
    for q in range(0, width // quarter, 2):
        here = both[:, q * quarter : (q + 1) * quarter]
        below = pltpu.roll(both[:, (q + 1) * quarter : (q + 2) * quarter], 4, 0)
        tiles.append(jnp.where(row[:, :quarter] < 4, here, below))
    edges = jnp.concatenate(tiles, axis=0).astype(BF16)
    for k in range(slabs):
        out_ref[k, :rows_out] = part
        out_ref[k, rows_out : rows_out + rows] = part_basis
        out_ref[k, rows_out + rows :] = edges


def pieces_for(member, basis_rows, control, slabs, quarter):
    rows, width = basis_rows.shape
    rows_out = control.shape[0]
    edges = 4 * width // quarter
    return pl.pallas_call(
        pack_pieces,
        name="pack_pieces",
        out_shape=jax.ShapeDtypeStruct((slabs, rows_out + rows + edges, quarter), BF16),
        in_specs=[SMEM, HBM, HBM],
        out_specs=VMEM,
        scratch_shapes=[
            pltpu.VMEM((rows, width), BF16),
            pltpu.VMEM((rows_out, quarter), F32),
            pltpu.SemaphoreType.DMA((2,)),
        ],
        compiler_params=limit(10),
    )(member.reshape(1), in_hbm(basis_rows), in_hbm(control))


def in_hbm(array):
    return pltpu.with_memory_space_constraint(array, pltpu.HBM)


def hold(source_ref, out_ref, sem):
    copy = pltpu.make_async_copy(source_ref, out_ref, sem)
    copy.start()
    copy.wait()


def held(array):
    size = array.size * array.dtype.itemsize
    return pl.pallas_call(
        hold,
        name="hold",
        out_shape=jax.ShapeDtypeStruct(array.shape, array.dtype),
        in_specs=[HBM],
        out_specs=VMEM,
        scratch_shapes=[pltpu.SemaphoreType.DMA],
        compiler_params=limit(size // MIB + 2),
    )(in_hbm(array))


PAIRS = 5


class Rows:
    def __init__(self, ref):
        self.ref = ref

    def put(self, tile, value):
        self.ref[:, TILE * (tile + 1) : TILE * (tile + 2), :] = value

    def put_at(self, start, value):
        self.ref[:, start : start + value.shape[1], :] = value

    def get(self, tile, step=0):
        start = TILE * (tile + 1) + step
        return self.ref[:, start : start + TILE, :]


class Ring(Rows):
    def put(self, tile, value):
        super().put(tile, value)
        rows = self.ref.shape[1]
        if tile == 0:
            self.ref[:, rows - TILE :, :] = value
        if TILE * (tile + 3) == rows:
            self.ref[:, :TILE, :] = value


def rows_of(tile):
    return slice(TILE * tile, TILE * (tile + 1))


def clear(*refs):
    for ref in refs:
        ref[...] = jnp.zeros_like(ref)


def add_state(tiles, state, mask, live, padded, plain, sums):
    heights, easts, norths, seens = state
    fluxes, mid_fluxes, weights, rights, misfits = (Rows(ref) for ref in padded)
    lefts, partial = plain
    push_left, push_right, gy, same, two_x, two_y, up, down = sums
    half = 0.5 * TIME_STEP
    keep = 1.0 - TIME_STEP * FRICTION
    turn = TIME_STEP * CORIOLIS / keep
    slope = half * GRAVITY / keep

    for tile in range(tiles):
        fluxes.put(tile, (DEPTH + heights.get(tile)) * norths.get(tile))

    for tile in range(tiles):
        here = rows_of(tile)
        height = heights.get(tile)
        east = easts.get(tile)
        north = norths.get(tile)
        flux = dx((DEPTH + height) * east) + (fluxes.get(tile, 1) - fluxes.get(tile, -1))
        sea = mask[:, here, :]
        height_mid = sea * (height - half * flux)
        weight = DEPTH * sea + height_mid
        east_mid = east + turn * north - slope * dx(height)
        north_mid = north - turn * east - slope * (heights.get(tile, 1) - heights.get(tile, -1))
        right = shift_cols(weight, 1)
        left = shift_cols(weight, -1)
        scaled = half * keep * weight
        mid_fluxes.put(tile, scaled * north_mid)
        weights.put(tile, weight)
        rights.put(tile, right)
        lefts[:, here, :] = left
        same[:, here, :] += weight * weight
        two_x[:, here, :] += left * right
        partial[:, here, :] = (
            height + height_mid - 2.0 * seens.get(tile) - dx(scaled * east_mid)
        )

    for tile in range(tiles):
        here = rows_of(tile)
        change = mid_fluxes.get(tile, 1) - mid_fluxes.get(tile, -1)
        misfit = live[:, here, :] * (partial[:, here, :] - change)
        misfits.put(tile, misfit)
        push_left[:, here, :] += lefts[:, here, :] * misfit
        push_right[:, here, :] += rights.get(tile) * misfit

    for tile in range(tiles):
        here = rows_of(tile)
        weight = weights.get(tile)
        gy[:, here, :] += weight * (misfits.get(tile, 1) - misfits.get(tile, -1))
        two_y[:, here, :] += weight * weights.get(tile, 2)
        up[:, here, :] += weight * rights.get(tile, 1)
        down[:, here, :] += weight * rights.get(tile, -1)


def inner_states(index_ref, states_ref, targets_ref, sea_ref, basis_ref, push_ref, pairs_ref, rows_ref, sems, sea, held_states, held_targets, mask, live, *scratch):
    count = states_ref.shape[0]
    rows = sea_ref.shape[0]
    tiles = rows // TILE
    plain, padded = scratch[:2], scratch[2:]

    def copies_of(k):
        return (
            pltpu.make_async_copy(states_ref.at[k, index_ref[k]], held_states.at[k], sems.at[0, k]),
            pltpu.make_async_copy(targets_ref.at[k], held_targets.at[k], sems.at[1, k]),
        )

    others = (
        pltpu.make_async_copy(sea_ref, sea, sems.at[0, count]),
        pltpu.make_async_copy(basis_ref, rows_ref, sems.at[1, count]),
    )
    for copy in others:
        copy.start()
    for k in range(count):
        for copy in copies_of(k):
            copy.start()
    clear(push_ref, pairs_ref, *padded)
    for copy in others:
        copy.wait()
    for tile in range(tiles):
        mask[:, rows_of(tile), :] = split_lanes(sea[rows_of(tile), :].astype(F32))
    row = lax.broadcasted_iota(jnp.int32, live.shape, 1)
    live[...] = jnp.where((row >= 2) & (row < rows - 2), mask[...], 0.0)

    @pl.loop(0, count)
    def _(s):
        for copy in copies_of(s):
            copy.wait()
        state = [Rows(ref) for ref in padded[:4]]
        for tile in range(tiles):
            for field in range(3):
                value = held_states[s, field, rows_of(tile), :].astype(F32)
                state[field].put(tile, split_lanes(value))
            state[3].put(tile, split_lanes(held_targets[s, rows_of(tile), :].astype(F32)))
        sums = [push_ref.at[k] for k in range(3)] + [pairs_ref.at[k] for k in range(PAIRS)]
        add_state(tiles, state, mask, live, padded[4:], plain, sums)


def inner_pass(section_index, checkpoints, targets, sea_mask, basis_rows):
    count, _, fields, rows, cols = checkpoints.shape
    width = basis_rows.shape[1]
    lanes = cols // LANES
    padded = pltpu.VMEM((lanes, rows + 2 * TILE, LANES), F32)
    plain = pltpu.VMEM((lanes, rows, LANES), F32)
    outs = (
        jax.ShapeDtypeStruct((3, lanes, rows, LANES), F32),
        jax.ShapeDtypeStruct((PAIRS, lanes, rows, LANES), F32),
        jax.ShapeDtypeStruct((rows, width), BF16),
    )
    return pl.pallas_call(
        inner_states,
        name="inner_states",
        out_shape=outs,
        in_specs=[SMEM] + [HBM] * 4,
        out_specs=(VMEM,) * 3,
        scratch_shapes=[
            pltpu.SemaphoreType.DMA((2, count + 1)),
            pltpu.VMEM((rows, cols), jnp.int32),
            pltpu.VMEM((count, fields, rows, cols), BF16),
            pltpu.VMEM((count, rows, cols), BF16),
        ]
        + [plain] * 4
        + [padded] * 9,
        compiler_params=limit(24),
    )(*map(in_hbm, (section_index, checkpoints, targets, sea_mask, basis_rows)))


def seam_first(index_ref, states_ref, targets_ref, sea_ref, before_ref, sums_ref, sea_out, ends_out, seen_out, sems, ends, seen_ends, seen_edge, mask, live, lefts, partial, *padded):
    count = states_ref.shape[0]
    rows, cols = sea_ref.shape
    top = tile_rows((TILE, cols)) < 4

    def copies_of(k, side, row, ends, seen_ends):
        here = pl.ds(row, TILE)
        return (
            pltpu.make_async_copy(
                states_ref.at[k, index_ref[k], :, here, :], ends.at[k], sems.at[side, k]
            ),
            pltpu.make_async_copy(targets_ref.at[k, here, :], seen_ends.at[k], sems.at[2 + side, k]),
        )

    own_ends = (0, 0, ends, seen_ends)
    next_ends = (1, rows - TILE, ends_out, seen_out)
    fetched = fetch(sea_ref, sea_out, sems.at[0, count])
    for which in (own_ends, next_ends):
        for k in range(count):
            for copy in copies_of(k, *which):
                copy.start()
    clear(sums_ref, *padded)
    seen_edge[...] = split_lanes(before_ref[count].astype(F32))
    fetched.wait()
    beyond = pltpu.roll(before_ref[count + 1].astype(F32), 4, 0)
    row = tile_rows((TILE, cols))
    beyond = jnp.where(row >= 2, beyond, 0.0)
    own = pltpu.roll(sea_out[:TILE, :].astype(F32), 4, 0)
    mask[...] = split_lanes(jnp.where(top, beyond, own))
    place = lax.broadcasted_iota(jnp.int32, live.shape, 1)
    live[...] = jnp.where((place >= 3) & (place < 6), mask[...], 0.0)
    sums = [sums_ref.at[k] for k in range(3 + PAIRS)]
    state = [Rows(ref) for ref in padded[:4]]

    @pl.loop(0, count)
    def _(s):
        before = split_lanes(before_ref[s].astype(F32))
        state[0].put_at(9, before)
        state[1].put_at(4, before)
        state[2].put_at(6, before)
        state[3].put_at(11, seen_edge[:, pl.ds(s, 1), :])
        for copy in copies_of(s, *own_ends):
            copy.wait()
        for field in range(3):
            state[field].put_at(12, split_lanes(ends[s, field].astype(F32)))
        state[3].put_at(12, split_lanes(seen_ends[s].astype(F32)))
        add_state(1, state, mask, live, padded[4:], (lefts, partial), sums)

    for k in range(count):
        for copy in copies_of(k, *next_ends):
            copy.wait()


def seam_last(sea, ends, seen_ends, before_ref, after_ref, first_ref, push_in_ref, pairs_in_ref, push_ref, pairs_ref, mask_ref, seen_edge, mask, live, lefts, partial, sums_ref, *padded):
    count = ends.shape[0]
    rows, cols = sea.shape
    row = tile_rows((TILE, cols))
    top = row < 4
    clear(sums_ref, *padded)
    seen_edge[...] = split_lanes(after_ref[count].astype(F32))
    after = jnp.where(row < 2, after_ref[count + 1].astype(F32), 0.0)
    before = jnp.where(row >= 6, before_ref[count + 1].astype(F32), 0.0)
    own = pltpu.roll(sea[rows - TILE :, :].astype(F32), 4, 0)
    mask[...] = split_lanes(jnp.where(top, own, pltpu.roll(after, 4, 0)))
    for tile in range(rows // TILE):
        mask_ref[:, rows_of(tile), :] = split_lanes(
            sea[rows_of(tile), :].astype(F32)
        ).astype(BF16)
    mask_ref[:, rows:, :] = split_lanes(after + before).astype(BF16)
    place = lax.broadcasted_iota(jnp.int32, live.shape, 1)
    live[...] = jnp.where((place >= 2) & (place < 5), mask[...], 0.0)
    sums = [sums_ref.at[k] for k in range(3 + PAIRS)]
    state = [Rows(ref) for ref in padded[:4]]

    @pl.loop(0, count)
    def _(s):
        after = split_lanes(after_ref[s].astype(F32))
        state[0].put_at(12, after)
        state[1].put_at(6, after)
        state[2].put_at(9, after)
        state[3].put_at(12, seen_edge[:, pl.ds(s, 1), :])
        for field in range(3):
            state[field].put_at(4, split_lanes(ends[s, field].astype(F32)))
        state[3].put_at(4, split_lanes(seen_ends[s].astype(F32)))
        add_state(1, state, mask, live, padded[4:], (lefts, partial), sums)

    place = lax.broadcasted_iota(jnp.int32, lefts.shape, 1)
    top = place < 4
    final = rows // TILE - 1

    def ring(inner, ending, opening, out, bounds):
        ending = pltpu.roll(ending, 4, 1)
        opening = pltpu.roll(opening, 4, 1)
        for tile in range(1, final):
            out[:, rows_of(tile), :] = inner[:, rows_of(tile), :]
        head = inner[:, :TILE, :]
        tail = inner[:, rows_of(final), :]
        if bounds is None:
            head = head + jnp.where(top, opening, 0.0)
            tail = tail + jnp.where(top, 0.0, ending)
        else:
            head = jnp.where(place < bounds[0], opening, head)
            tail = jnp.where(place > bounds[1], ending, tail)
        out[:, :TILE, :] = head
        out[:, rows_of(final), :] = tail
        out[:, rows:, :] = jnp.where(top, ending, opening)

    for k in range(3):
        ring(push_in_ref[k], sums_ref[k], first_ref[k], push_ref.at[k], None)
    for k in range(PAIRS):
        bounds = (2, 5) if k == PAIRS - 1 else (1, 4)
        ring(pairs_in_ref[k], sums_ref[3 + k], first_ref[3 + k], pairs_ref.at[k], bounds)


def seam_first_pass(section_index, checkpoints, before, targets, sea_mask):
    count, _, fields, _, cols = checkpoints.shape
    lanes = cols // LANES
    tile = pltpu.VMEM((lanes, TILE, LANES), F32)
    padded = pltpu.VMEM((lanes, 3 * TILE, LANES), F32)
    ends = (count, fields, TILE, cols)
    seen = (count, TILE, cols)
    return pl.pallas_call(
        seam_first,
        name="seam_first",
        out_shape=(
            jax.ShapeDtypeStruct((3 + PAIRS, lanes, TILE, LANES), F32),
            jax.ShapeDtypeStruct(sea_mask.shape, jnp.int32),
            jax.ShapeDtypeStruct(ends, BF16),
            jax.ShapeDtypeStruct(seen, BF16),
        ),
        in_specs=[SMEM] + [HBM] * 3 + [VMEM],
        out_specs=(VMEM,) * 4,
        scratch_shapes=[
            pltpu.SemaphoreType.DMA((4, count + 1)),
            pltpu.VMEM(ends, BF16),
            pltpu.VMEM(seen, BF16),
        ]
        + [tile] * 5
        + [padded] * 9,
        compiler_params=limit(14),
    )(*map(in_hbm, (section_index, checkpoints, targets, sea_mask)), before)


def seam_last_pass(sea, ends, seen, before, after, first, push, pairs):
    rows, cols = sea.shape
    lanes = cols // LANES
    ring = rows + TILE
    tile = pltpu.VMEM((lanes, TILE, LANES), F32)
    padded = pltpu.VMEM((lanes, 3 * TILE, LANES), F32)
    return pl.pallas_call(
        seam_last,
        name="seam_last",
        out_shape=(
            jax.ShapeDtypeStruct((3, lanes, ring, LANES), F32),
            jax.ShapeDtypeStruct((PAIRS, lanes, ring, LANES), F32),
            jax.ShapeDtypeStruct((lanes, ring, LANES), BF16),
        ),
        in_specs=[VMEM] * 8,
        out_specs=(VMEM,) * 3,
        scratch_shapes=[tile] * 5
        + [pltpu.VMEM((3 + PAIRS, lanes, TILE, LANES), F32)]
        + [padded] * 9,
        compiler_params=limit(20),
    )(sea, ends, seen, before, after, first, push, pairs)


def make_coeffs(slab_ref, basis_ref, pieces_ref, out_ref):
    slabs, _, quarter = pieces_ref.shape
    rows, width = basis_ref.shape
    rows_out = width // slabs
    slab = slab_ref[0]

    def edge_of(k):
        parts = []
        for q in range(width // quarter):
            start = rows_out + rows + TILE * (q // 2)
            part = pieces_ref[k, start : start + TILE, :].astype(F32)
            parts.append(pltpu.roll(part, 4, 0) if q % 2 else part)
        return jnp.concatenate(parts, axis=1)

    after = edge_of(jnp.minimum(slab + 1, slabs - 1))
    before = pltpu.roll(edge_of(jnp.maximum(slab - 1, 0)), 4, 0)
    row = tile_rows((TILE, width))
    use_after = (row < 2) & (slab < slabs - 1)
    use_before = (row >= 6) & (slab > 0)
    edge = jnp.where(use_after, after, jnp.where(use_before, before, 0.0))
    basis = jnp.concatenate([basis_ref[...].astype(F32), edge], axis=0).astype(BF16)
    part = pieces_ref[:, :rows_out, :].reshape(width, quarter)
    out_ref[...] = jnp.dot(basis, part, preferred_element_type=F32).astype(BF16)


def coeffs_part(slab, basis_rows, pieces):
    return pl.pallas_call(
        make_coeffs,
        name="make_coeffs",
        out_shape=jax.ShapeDtypeStruct((basis_rows.shape[0] + TILE, pieces.shape[2]), BF16),
        in_specs=[SMEM, VMEM, VMEM],
        out_specs=VMEM,
        compiler_params=limit(12),
    )(slab.reshape(1), basis_rows, pieces)


def apply_potential(member_ref, own_ref, near_ref, far_ref, both_ref, cols_ref, push_ref, pairs_ref, mask_ref, keep_ref, give_ref, coeffs, total, field, east, part, gy, *rings):
    member = member_ref[0]
    quarter = own_ref.shape[1]
    for bits, ref in enumerate((own_ref, near_ref, far_ref, both_ref)):
        at = pl.multiple_of((member ^ bits) * quarter, quarter)
        coeffs[:, pl.ds(at, quarter)] = ref[...]
    field[...] = lax.dot_general(
        coeffs[...], cols_ref[...], (((1,), (1,)), ((), ())), preferred_element_type=F32
    )
    same, two_x, two_y, up, down = (pairs_ref.at[k] for k in range(PAIRS))
    potential, masks, right_xs, right_ys, norths, two_norths, gx = (
        Ring(ref) for ref in rings[:7]
    )
    back_up_x, back_up_y, back_down_x, back_down_y = (Ring(ref) for ref in rings[7:])
    tiles = field.shape[0] // TILE
    own_tiles = tiles - 1
    unit = -4.0 / TIME_STEP**2

    for tile in range(tiles):
        potential.put(tile, split_lanes(field[rows_of(tile), :]))
        masks.put(tile, mask_ref[:, rows_of(tile), :].astype(F32))

    for tile in range(tiles):
        here = rows_of(tile)
        sx = potential.get(tile, -1) - potential.get(tile, 1)
        sy = dx(potential.get(tile))
        east[:, here, :] = sx
        right_x = shift_cols(sx, 1)
        right_xs.put(tile, right_x)
        right_ys.put(tile, shift_cols(sy, 1))
        norths.put(tile, sy)
        two_norths.put(tile, two_y[:, here, :] * sy)
        up_here = up[:, here, :]
        down_here = down[:, here, :]
        back_up_x.put(tile, shift_cols(up_here * sx, -1))
        back_up_y.put(tile, shift_cols(up_here * sy, -1))
        back_down_x.put(tile, shift_cols(down_here * sx, -1))
        back_down_y.put(tile, shift_cols(down_here * sy, -1))
        beside = masks.get(tile) * two_x[:, here, :]
        part[:, here, :] = shift_cols(
            beside * right_x + unit * push_ref[0, :, here, :], 1
        ) + shift_cols(beside * shift_cols(sx, -1) - unit * push_ref[1, :, here, :], -1)

    for tile in range(tiles):
        here = rows_of(tile)
        mask = masks.get(tile)
        same_x = same[:, here, :] * east[:, here, :]
        up_here = up[:, here, :]
        down_here = down[:, here, :]
        ahead = up_here * right_ys.get(tile, 1) - same_x - down_here * right_ys.get(tile, -1)
        behind = same_x + back_down_y.get(tile, 1) - back_up_y.get(tile, -1)
        gx.put(
            tile,
            part[:, here, :] + shift_cols(mask, 1) * ahead - shift_cols(mask, -1) * behind,
        )
        if tile < own_tiles:
            same_y = same[:, here, :] * norths.get(tile)
            ahead = (
                up_here * right_xs.get(tile, 1)
                - back_down_x.get(tile, 1)
                + two_y[:, here, :] * norths.get(tile, 2)
                - same_y
            )
            behind = (
                down_here * right_xs.get(tile, -1)
                - back_up_x.get(tile, -1)
                + same_y
                - two_norths.get(tile, -2)
            )
            gy[:, here, :] = (
                unit * push_ref[2, :, here, :]
                + masks.get(tile, 1) * ahead
                - masks.get(tile, -1) * behind
            )

    scale = -(TIME_STEP**4) / 64.0
    for tile in range(own_tiles):
        here = rows_of(tile)
        total[here, :] = join_lanes(
            scale * (gx.get(tile, 1) - gx.get(tile, -1) - dx(gy[:, here, :]))
        )
    pair = keep_ref.shape[0]
    core = member % 2
    keep_ref[...] = total[pl.ds(pl.multiple_of(core * pair, pair), pair), :]
    give_ref[...] = total[pl.ds(pl.multiple_of((1 - core) * pair, pair), pair), :]


def gradient_halves(member, parts, basis_cols, push, pairs, mask):
    lanes, ring, _ = mask.shape
    cols, width = basis_cols.shape
    pair = (ring - TILE) // 2
    half = jax.ShapeDtypeStruct((pair, cols), F32)
    return pl.pallas_call(
        apply_potential,
        name="apply_potential",
        out_shape=(half, half),
        in_specs=[SMEM] + [VMEM] * 8,
        out_specs=(VMEM, VMEM),
        scratch_shapes=[
            pltpu.VMEM((ring, width), BF16),
            pltpu.VMEM((2 * pair, cols), F32),
            pltpu.VMEM((ring, cols), F32),
        ]
        + [pltpu.VMEM((lanes, ring, LANES), F32)] * 3
        + [pltpu.VMEM((lanes, ring + 2 * TILE, LANES), F32)] * 11,
        compiler_params=limit(24),
    )(member.reshape(1), *parts, basis_cols, push, pairs, mask)


def project(own_ref, other_ref, cols_ref, out_ref):
    total = (own_ref[...] + other_ref[...]).astype(BF16)
    projected = jnp.dot(total, cols_ref[...], preferred_element_type=F32).astype(BF16)
    half = out_ref.shape[3]
    for core in range(2):
        part = projected[:, core * half : (core + 1) * half]
        for chip in range(out_ref.shape[1] // 2):
            for k in range(out_ref.shape[0]):
                out_ref[k, 2 * chip + core] = part


def projected_pieces(own, other, basis_cols, members, slabs):
    single = own.shape[0]
    half = basis_cols.shape[1] // 2
    return pl.pallas_call(
        project,
        name="project",
        out_shape=jax.ShapeDtypeStruct((slabs, members, single, half), BF16),
        in_specs=[VMEM] * 3,
        out_specs=VMEM,
        compiler_params=limit(16),
    )(own, other, basis_cols)


def assemble(member_ref, own_ref, far_ref, near_ref, control_ref, basis_ref, kept_ref, sem):
    copy = pltpu.make_async_copy(control_ref, kept_ref, sem)
    copy.start()
    member = member_ref[0]
    quarter = own_ref.shape[1]
    parts = (own_ref[...], near_ref[0], far_ref[...], near_ref[1])
    for bits, part in enumerate(parts):
        at = pl.multiple_of((member ^ bits) * quarter, quarter)
        basis_ref[pl.ds(at, quarter), :] = part.astype(F32).T.astype(BF16)
    copy.wait()


def assembled(member, own, far, near, control):
    rows, _ = own.shape
    width = control.shape[1]
    return pl.pallas_call(
        assemble,
        name="assemble",
        out_shape=(
            jax.ShapeDtypeStruct((width, rows), BF16),
            jax.ShapeDtypeStruct(control.shape, F32),
        ),
        in_specs=[SMEM, VMEM, VMEM, VMEM, HBM],
        out_specs=(VMEM, VMEM),
        scratch_shapes=[pltpu.SemaphoreType.DMA],
        compiler_params=limit(24),
    )(member.reshape(1), own, far, near, in_hbm(control))


def gradient(slab_ref, basis_ref, projected_ref, out_ref):
    rows_out = out_ref.shape[0] - TILE
    width = basis_ref.shape[0]
    half = out_ref.shape[1]
    projected = projected_ref[...]
    block = width // 4
    squares = jnp.zeros((TILE, half), F32)
    for k in range(4):
        part = jnp.dot(
            basis_ref[k * block : (k + 1) * block, :], projected, preferred_element_type=F32
        )
        squares += jnp.sum((part * part).reshape(block // TILE, TILE, half), axis=0)
    at = pl.multiple_of(slab_ref[0] * rows_out, rows_out)
    out_ref[:rows_out] = jnp.dot(
        basis_ref[pl.ds(at, rows_out), :], projected, preferred_element_type=F32
    )
    out_ref[rows_out:] = squares


def gradient_block(slab, basis, projected, rows_out):
    half = projected.shape[1]
    return pl.pallas_call(
        gradient,
        name="gradient",
        out_shape=jax.ShapeDtypeStruct((rows_out + TILE, half), F32),
        in_specs=[SMEM, VMEM, VMEM],
        out_specs=VMEM,
        compiler_params=limit(24),
    )(slab.reshape(1), basis, projected)


def update(core_ref, control_ref, own_ref, other_ref, out_ref):
    rows_out, width = control_ref.shape
    half = width // 2
    total = jnp.sum(own_ref[rows_out:] + other_ref[rows_out:])
    scale = STEP_SIZE * lax.rsqrt(total / (width * width) + EPSILON)
    for turn, ref in enumerate((own_ref, other_ref)):
        at = pl.multiple_of((core_ref[0] ^ turn) * half, half)
        out_ref[:, pl.ds(at, half)] = control_ref[:, pl.ds(at, half)] - ref[:rows_out] * scale


def updated(core, control, own, other):
    return pl.pallas_call(
        update,
        name="update",
        out_shape=jax.ShapeDtypeStruct(control.shape, F32),
        in_specs=[SMEM, VMEM, VMEM, VMEM],
        out_specs=VMEM,
        compiler_params=limit(8),
    )(core.reshape(1), control, own, other)


def partner(value, bit):
    count = lax.axis_size("ens")
    return lax.ppermute(value, "ens", [(i, i ^ bit) for i in range(count)])


def on_device(checkpoints, section_index, targets, sea_mask, basis_rows, basis_cols, control):
    members = lax.axis_size("ens")
    slabs = lax.axis_size("space")
    member = lax.axis_index("ens").astype(jnp.int32)
    slab = lax.axis_index("space").astype(jnp.int32)
    core = member & 1
    chip = member >> 1
    rows_out, width = control.shape
    rows = basis_rows.shape[0]
    quarter = width // members
    half = width // 2
    single = rows // 4

    pieces = pieces_for(member, basis_rows, control, slabs, quarter)
    pieces = lax.all_to_all(pieces, "space", 0, 0)
    up, down = edge_messages(section_index, checkpoints, targets, sea_mask)
    before = lax.ppermute(up, "space", [(i, i + 1) for i in range(slabs - 1)])
    after = lax.ppermute(down, "space", [(i + 1, i) for i in range(slabs - 1)])
    push, pairs, near_rows = inner_pass(section_index, checkpoints, targets, sea_mask, basis_rows)
    own = coeffs_part(slab, near_rows, pieces)
    parts = [own]
    for bits in (1, 2, 3):
        parts.append(partner(own, bits))
    first, sea, ends, seen = seam_first_pass(section_index, checkpoints, before, targets, sea_mask)
    push, pairs, mask = seam_last_pass(sea, ends, seen, before, after, first, push, pairs)
    keep, give = gradient_halves(member, parts, basis_cols, push, pairs, mask)

    keep = keep + partner(give, 1)
    own_rows = lax.dynamic_slice_in_dim(keep, chip * single, single, 0)
    give = lax.dynamic_slice_in_dim(keep, (1 - chip) * single, single, 0)
    arriving = partner(give, 2)
    cols = held(basis_cols)
    send = projected_pieces(own_rows, arriving, cols, members, slabs)
    got = lax.all_to_all(send.reshape(members * slabs, single, half), ("space", "ens"), 0, 0)
    projected_half = got.reshape(slabs * rows, half)

    part = pieces[:, rows_out : rows_out + rows, :].reshape(slabs, 2, members // 2, single, quarter)
    part = part.transpose(0, 2, 1, 3, 4).reshape(slabs * rows, quarter)
    far = partner(part, 2)
    near = partner(jnp.stack([part, far]), 1)
    basis, kept = assembled(member, part, far, near, control)
    block = gradient_block(slab, basis, projected_half, rows_out)
    other = partner(block, 1)
    return updated(core, kept, block, other)


def solution(mesh):
    return jax.shard_map(
        on_device,
        mesh=mesh,
        in_specs=(
            P("ens", None, None, "space", None),
            P("ens"),
            P("ens", "space", None),
            P("space", None),
            P("space", None),
            P(),
            P("space", None),
        ),
        out_specs=P("space", None),
        check_vma=False,
    )
```

```python
import jax
import jax.numpy as jnp
from jax import lax
from jax.experimental import pallas as pl
from jax.experimental.pallas import tpu as pltpu
from jax.sharding import PartitionSpec as P


DEPTH = 1.0
GRAVITY = 1.0
CORIOLIS = 0.5
FRICTION = 0.1
TIME_STEP = 0.3
STEP_SIZE = 1.0
EPSILON = 1e-06

F32 = jnp.float32
BF16 = jnp.bfloat16
TILE = 8
LANES = 128
MIB = 1 << 20


VMEM = pl.BlockSpec(memory_space=pltpu.VMEM)
SMEM = pl.BlockSpec(memory_space=pltpu.SMEM)
HBM = pl.BlockSpec(memory_space=pltpu.HBM)


def limit(mib):
    return pltpu.CompilerParams(vmem_limit_bytes=mib * MIB)


def tile_rows(shape):
    return lax.broadcasted_iota(jnp.int32, shape, 0)


def split_lanes(field):
    return jnp.stack([field[:, k : k + LANES] for k in range(0, field.shape[1], LANES)])


def join_lanes(field):
    return jnp.concatenate([field[k] for k in range(field.shape[0])], axis=1)


def shift_cols(field, step):
    turned = pltpu.roll(field, (-step) % LANES, 2)
    lane = lax.broadcasted_iota(jnp.int32, field.shape, 2)
    outside = jnp.zeros_like(turned[:1])
    if step > 0:
        beside = jnp.concatenate([turned[1:], outside], axis=0)
        return jnp.where(lane >= LANES - step, beside, turned)
    beside = jnp.concatenate([outside, turned[:-1]], axis=0)
    return jnp.where(lane < -step, beside, turned)


def dx(field):
    return shift_cols(field, 1) - shift_cols(field, -1)


def fetch(source, target, sem):
    copy = pltpu.make_async_copy(source, target, sem)
    copy.start()
    return copy


def pack_edges(index_ref, states_ref, targets_ref, sea_ref, up_ref, down_ref, last, first, seen, sea, sems):
    count, _, _, rows, cols = states_ref.shape
    states = []
    for s in range(count):
        slot = index_ref[s]
        for side, (buffer, row) in enumerate(((last, rows - TILE), (first, 0))):
            source = states_ref.at[s, slot, :, pl.ds(row, TILE), :]
            states.append(fetch(source, buffer.at[s], sems.at[side, s]))
    others = [
        fetch(targets_ref.at[:, pl.ds(rows - TILE, TILE), :], seen.at[0], sems.at[0, count]),
        fetch(targets_ref.at[:, pl.ds(0, TILE), :], seen.at[1], sems.at[1, count]),
        fetch(sea_ref.at[pl.ds(rows - TILE, TILE), :], sea.at[0], sems.at[0, count + 1]),
        fetch(sea_ref.at[pl.ds(0, TILE), :], sea.at[1], sems.at[1, count + 1]),
    ]
    row = tile_rows((TILE, cols))
    for s in range(count):
        states[2 * s].wait()
        height, east, north = (last[s, f].astype(F32) for f in range(3))
        height, north = pltpu.roll(height, 3, 0), pltpu.roll(north, 6, 0)
        up_ref[s] = jnp.where(row < 3, height, jnp.where(row < 6, north, east)).astype(BF16)
        states[2 * s + 1].wait()
        height, east, north = (first[s, f].astype(F32) for f in range(3))
        east, north = pltpu.roll(east, 6, 0), pltpu.roll(north, 3, 0)
        down_ref[s] = jnp.where(row < 3, height, jnp.where(row < 6, north, east)).astype(BF16)
    for copy in others:
        copy.wait()
    targets_up = jnp.zeros((TILE, cols), F32)
    targets_down = jnp.zeros((TILE, cols), F32)
    for s in range(count):
        targets_up = jnp.where(row == s, seen[0, s].astype(F32)[TILE - 1 :, :], targets_up)
        targets_down = jnp.where(row == s, seen[1, s].astype(F32)[:1, :], targets_down)
    up_ref[count] = targets_up.astype(BF16)
    down_ref[count] = targets_down.astype(BF16)
    up_ref[count + 1] = sea[0].astype(F32).astype(BF16)
    down_ref[count + 1] = sea[1].astype(F32).astype(BF16)


def edge_messages(section_index, checkpoints, targets, sea_mask):
    count, _, fields, _, cols = checkpoints.shape
    edges = jax.ShapeDtypeStruct((count + 2, TILE, cols), BF16)
    return pl.pallas_call(
        pack_edges,
        name="pack_edges",
        out_shape=(edges, edges),
        in_specs=[SMEM] + [HBM] * 3,
        out_specs=(VMEM, VMEM),
        scratch_shapes=[
            pltpu.VMEM((count, fields, TILE, cols), BF16),
            pltpu.VMEM((count, fields, TILE, cols), BF16),
            pltpu.VMEM((2, count, TILE, cols), BF16),
            pltpu.VMEM((2, TILE, cols), jnp.int32),
            pltpu.SemaphoreType.DMA((2, count + 2)),
        ],
        compiler_params=limit(12),
    )(*map(in_hbm, (section_index, checkpoints, targets, sea_mask)))


def pack_pieces(member_ref, basis_ref, control_ref, out_ref, basis, own, sems):
    rows, width = basis_ref.shape
    rows_out = control_ref.shape[0]
    slabs, _, quarter = out_ref.shape
    at = pl.multiple_of(member_ref[0] * quarter, quarter)
    copies = [
        fetch(control_ref.at[:, pl.ds(at, quarter)], own, sems.at[0]),
        fetch(basis_ref, basis, sems.at[1]),
    ]
    for copy in copies:
        copy.wait()
    part = own[...].astype(BF16)
    part_basis = basis[:, pl.ds(at, quarter)]
    row = tile_rows((TILE, width))
    first = basis[:TILE, :].astype(F32)
    last = pltpu.roll(basis[rows - TILE :, :].astype(F32), 4, 0)
    both = jnp.where(row < 2, first, last)
    tiles = []
    for q in range(0, width // quarter, 2):
        here = both[:, q * quarter : (q + 1) * quarter]
        below = pltpu.roll(both[:, (q + 1) * quarter : (q + 2) * quarter], 4, 0)
        tiles.append(jnp.where(row[:, :quarter] < 4, here, below))
    edges = jnp.concatenate(tiles, axis=0).astype(BF16)
    for k in range(slabs):
        out_ref[k, :rows_out] = part
        out_ref[k, rows_out : rows_out + rows] = part_basis
        out_ref[k, rows_out + rows :] = edges


def pieces_for(member, basis_rows, control, slabs, quarter):
    rows, width = basis_rows.shape
    rows_out = control.shape[0]
    edges = 4 * width // quarter
    return pl.pallas_call(
        pack_pieces,
        name="pack_pieces",
        out_shape=jax.ShapeDtypeStruct((slabs, rows_out + rows + edges, quarter), BF16),
        in_specs=[SMEM, HBM, HBM],
        out_specs=VMEM,
        scratch_shapes=[
            pltpu.VMEM((rows, width), BF16),
            pltpu.VMEM((rows_out, quarter), F32),
            pltpu.SemaphoreType.DMA((2,)),
        ],
        compiler_params=limit(10),
    )(member.reshape(1), in_hbm(basis_rows), in_hbm(control))


def in_hbm(array):
    return pltpu.with_memory_space_constraint(array, pltpu.HBM)


def hold(source_ref, out_ref, sem):
    copy = pltpu.make_async_copy(source_ref, out_ref, sem)
    copy.start()
    copy.wait()


def held(array):
    size = array.size * array.dtype.itemsize
    return pl.pallas_call(
        hold,
        name="hold",
        out_shape=jax.ShapeDtypeStruct(array.shape, array.dtype),
        in_specs=[HBM],
        out_specs=VMEM,
        scratch_shapes=[pltpu.SemaphoreType.DMA],
        compiler_params=limit(size // MIB + 2),
    )(in_hbm(array))


PAIRS = 5


class Rows:
    def __init__(self, ref):
        self.ref = ref

    def put(self, tile, value):
        self.ref[:, TILE * (tile + 1) : TILE * (tile + 2), :] = value

    def put_at(self, start, value):
        self.ref[:, start : start + value.shape[1], :] = value

    def get(self, tile, step=0):
        start = TILE * (tile + 1) + step
        return self.ref[:, start : start + TILE, :]


class Ring(Rows):
    def put(self, tile, value):
        super().put(tile, value)
        rows = self.ref.shape[1]
        if tile == 0:
            self.ref[:, rows - TILE :, :] = value
        if TILE * (tile + 3) == rows:
            self.ref[:, :TILE, :] = value


def rows_of(tile):
    return slice(TILE * tile, TILE * (tile + 1))


def clear(*refs):
    for ref in refs:
        ref[...] = jnp.zeros_like(ref)


def add_state(tiles, state, mask, live, padded, plain, sums):
    heights, easts, norths, seens = state
    fluxes, mid_fluxes, weights, rights, misfits = (Rows(ref) for ref in padded)
    lefts, partial = plain
    push_left, push_right, gy, same, two_x, two_y, up, down = sums
    half = 0.5 * TIME_STEP
    keep = 1.0 - TIME_STEP * FRICTION
    turn = TIME_STEP * CORIOLIS / keep
    slope = half * GRAVITY / keep

    for tile in range(tiles):
        fluxes.put(tile, (DEPTH + heights.get(tile)) * norths.get(tile))

    for tile in range(tiles):
        here = rows_of(tile)
        height = heights.get(tile)
        east = easts.get(tile)
        north = norths.get(tile)
        flux = dx((DEPTH + height) * east) + (fluxes.get(tile, 1) - fluxes.get(tile, -1))
        sea = mask[:, here, :]
        height_mid = sea * (height - half * flux)
        weight = DEPTH * sea + height_mid
        east_mid = east + turn * north - slope * dx(height)
        north_mid = north - turn * east - slope * (heights.get(tile, 1) - heights.get(tile, -1))
        right = shift_cols(weight, 1)
        left = shift_cols(weight, -1)
        scaled = half * keep * weight
        mid_fluxes.put(tile, scaled * north_mid)
        weights.put(tile, weight)
        rights.put(tile, right)
        lefts[:, here, :] = left
        same[:, here, :] += weight * weight
        two_x[:, here, :] += left * right
        partial[:, here, :] = (
            height + height_mid - 2.0 * seens.get(tile) - dx(scaled * east_mid)
        )

    for tile in range(tiles):
        here = rows_of(tile)
        change = mid_fluxes.get(tile, 1) - mid_fluxes.get(tile, -1)
        misfit = live[:, here, :] * (partial[:, here, :] - change)
        misfits.put(tile, misfit)
        push_left[:, here, :] += lefts[:, here, :] * misfit
        push_right[:, here, :] += rights.get(tile) * misfit

    for tile in range(tiles):
        here = rows_of(tile)
        weight = weights.get(tile)
        gy[:, here, :] += weight * (misfits.get(tile, 1) - misfits.get(tile, -1))
        two_y[:, here, :] += weight * weights.get(tile, 2)
        up[:, here, :] += weight * rights.get(tile, 1)
        down[:, here, :] += weight * rights.get(tile, -1)


def inner_states(index_ref, states_ref, targets_ref, sea_ref, basis_ref, push_ref, pairs_ref, rows_ref, sems, sea, held_states, held_targets, mask, live, *scratch):
    count = states_ref.shape[0]
    rows = sea_ref.shape[0]
    tiles = rows // TILE
    plain, padded = scratch[:2], scratch[2:]

    def copies_of(k):
        return (
            pltpu.make_async_copy(states_ref.at[k, index_ref[k]], held_states.at[k], sems.at[0, k]),
            pltpu.make_async_copy(targets_ref.at[k], held_targets.at[k], sems.at[1, k]),
        )

    others = (
        pltpu.make_async_copy(sea_ref, sea, sems.at[0, count]),
        pltpu.make_async_copy(basis_ref, rows_ref, sems.at[1, count]),
    )
    for copy in others:
        copy.start()
    for k in range(count):
        for copy in copies_of(k):
            copy.start()
    clear(push_ref, pairs_ref, *padded)
    for copy in others:
        copy.wait()
    for tile in range(tiles):
        mask[:, rows_of(tile), :] = split_lanes(sea[rows_of(tile), :].astype(F32))
    row = lax.broadcasted_iota(jnp.int32, live.shape, 1)
    live[...] = jnp.where((row >= 2) & (row < rows - 2), mask[...], 0.0)

    @pl.loop(0, count)
    def _(s):
        for copy in copies_of(s):
            copy.wait()
        state = [Rows(ref) for ref in padded[:4]]
        for tile in range(tiles):
            for field in range(3):
                value = held_states[s, field, rows_of(tile), :].astype(F32)
                state[field].put(tile, split_lanes(value))
            state[3].put(tile, split_lanes(held_targets[s, rows_of(tile), :].astype(F32)))
        sums = [push_ref.at[k] for k in range(3)] + [pairs_ref.at[k] for k in range(PAIRS)]
        add_state(tiles, state, mask, live, padded[4:], plain, sums)


def inner_pass(section_index, checkpoints, targets, sea_mask, basis_rows):
    count, _, fields, rows, cols = checkpoints.shape
    width = basis_rows.shape[1]
    lanes = cols // LANES
    padded = pltpu.VMEM((lanes, rows + 2 * TILE, LANES), F32)
    plain = pltpu.VMEM((lanes, rows, LANES), F32)
    outs = (
        jax.ShapeDtypeStruct((3, lanes, rows, LANES), F32),
        jax.ShapeDtypeStruct((PAIRS, lanes, rows, LANES), F32),
        jax.ShapeDtypeStruct((rows, width), BF16),
    )
    return pl.pallas_call(
        inner_states,
        name="inner_states",
        out_shape=outs,
        in_specs=[SMEM] + [HBM] * 4,
        out_specs=(VMEM,) * 3,
        scratch_shapes=[
            pltpu.SemaphoreType.DMA((2, count + 1)),
            pltpu.VMEM((rows, cols), jnp.int32),
            pltpu.VMEM((count, fields, rows, cols), BF16),
            pltpu.VMEM((count, rows, cols), BF16),
        ]
        + [plain] * 4
        + [padded] * 9,
        compiler_params=limit(24),
    )(*map(in_hbm, (section_index, checkpoints, targets, sea_mask, basis_rows)))


def end_copies(index_ref, states_ref, targets_ref, row, ends_out, seen_out, sems):
    here = pl.ds(row, TILE)
    count = states_ref.shape[0]
    copies = [fetch(targets_ref.at[:, here, :], seen_out, sems.at[count])]
    for k in range(count):
        source = states_ref.at[k, index_ref[k], :, here, :]
        copies.append(fetch(source, ends_out.at[k], sems.at[k]))
    return copies


def fetch_ends(index_ref, states_ref, targets_ref, sea_ref, sea_out, ends_out, seen_out, sems):
    count = states_ref.shape[0]
    copies = [fetch(sea_ref, sea_out, sems.at[count + 1])]
    copies += end_copies(index_ref, states_ref, targets_ref, 0, ends_out, seen_out, sems)
    for copy in copies:
        copy.wait()


def end_shapes(checkpoints):
    count, _, fields, _, cols = checkpoints.shape
    return (
        jax.ShapeDtypeStruct((count, fields, TILE, cols), BF16),
        jax.ShapeDtypeStruct((count, TILE, cols), BF16),
    )


def fetched_ends(section_index, checkpoints, targets, sea_mask):
    count = checkpoints.shape[0]
    return pl.pallas_call(
        fetch_ends,
        name="fetch_ends",
        out_shape=(jax.ShapeDtypeStruct(sea_mask.shape, jnp.int32),) + end_shapes(checkpoints),
        in_specs=[SMEM] + [HBM] * 3,
        out_specs=(VMEM,) * 3,
        scratch_shapes=[pltpu.SemaphoreType.DMA((count + 2,))],
        compiler_params=limit(6),
    )(*map(in_hbm, (section_index, checkpoints, targets, sea_mask)))


def seam_first(index_ref, states_ref, targets_ref, sea, ends, seen_ends, before_ref, sums_ref, ends_out, seen_out, sems, seen_edge, mask, live, lefts, partial, *padded):
    count = ends.shape[0]
    rows, cols = sea.shape
    top = tile_rows((TILE, cols)) < 4
    copies = end_copies(
        index_ref, states_ref, targets_ref, rows - TILE, ends_out, seen_out, sems
    )
    clear(sums_ref, *padded)
    seen_edge[...] = split_lanes(before_ref[count].astype(F32))
    beyond = pltpu.roll(before_ref[count + 1].astype(F32), 4, 0)
    row = tile_rows((TILE, cols))
    beyond = jnp.where(row >= 2, beyond, 0.0)
    own = pltpu.roll(sea[:TILE, :].astype(F32), 4, 0)
    mask[...] = split_lanes(jnp.where(top, beyond, own))
    place = lax.broadcasted_iota(jnp.int32, live.shape, 1)
    live[...] = jnp.where((place >= 3) & (place < 6), mask[...], 0.0)
    sums = [sums_ref.at[k] for k in range(3 + PAIRS)]
    state = [Rows(ref) for ref in padded[:4]]

    @pl.loop(0, count)
    def _(s):
        before = split_lanes(before_ref[s].astype(F32))
        state[0].put_at(9, before)
        state[1].put_at(4, before)
        state[2].put_at(6, before)
        state[3].put_at(11, seen_edge[:, pl.ds(s, 1), :])
        for field in range(3):
            state[field].put_at(12, split_lanes(ends[s, field].astype(F32)))
        state[3].put_at(12, split_lanes(seen_ends[s].astype(F32)))
        add_state(1, state, mask, live, padded[4:], (lefts, partial), sums)

    for copy in copies:
        copy.wait()


def seam_last(sea, ends, seen_ends, before_ref, after_ref, first_ref, push_in_ref, pairs_in_ref, push_ref, pairs_ref, mask_ref, seen_edge, mask, live, lefts, partial, sums_ref, *padded):
    count = ends.shape[0]
    rows, cols = sea.shape
    row = tile_rows((TILE, cols))
    top = row < 4
    clear(sums_ref, *padded)
    seen_edge[...] = split_lanes(after_ref[count].astype(F32))
    after = jnp.where(row < 2, after_ref[count + 1].astype(F32), 0.0)
    before = jnp.where(row >= 6, before_ref[count + 1].astype(F32), 0.0)
    own = pltpu.roll(sea[rows - TILE :, :].astype(F32), 4, 0)
    mask[...] = split_lanes(jnp.where(top, own, pltpu.roll(after, 4, 0)))
    for tile in range(rows // TILE):
        mask_ref[:, rows_of(tile), :] = split_lanes(
            sea[rows_of(tile), :].astype(F32)
        ).astype(BF16)
    mask_ref[:, rows:, :] = split_lanes(after + before).astype(BF16)
    place = lax.broadcasted_iota(jnp.int32, live.shape, 1)
    live[...] = jnp.where((place >= 2) & (place < 5), mask[...], 0.0)
    sums = [sums_ref.at[k] for k in range(3 + PAIRS)]
    state = [Rows(ref) for ref in padded[:4]]

    @pl.loop(0, count)
    def _(s):
        after = split_lanes(after_ref[s].astype(F32))
        state[0].put_at(12, after)
        state[1].put_at(6, after)
        state[2].put_at(9, after)
        state[3].put_at(12, seen_edge[:, pl.ds(s, 1), :])
        for field in range(3):
            state[field].put_at(4, split_lanes(ends[s, field].astype(F32)))
        state[3].put_at(4, split_lanes(seen_ends[s].astype(F32)))
        add_state(1, state, mask, live, padded[4:], (lefts, partial), sums)

    place = lax.broadcasted_iota(jnp.int32, lefts.shape, 1)
    top = place < 4
    final = rows // TILE - 1

    def ring(inner, ending, opening, out, bounds):
        ending = pltpu.roll(ending, 4, 1)
        opening = pltpu.roll(opening, 4, 1)
        for tile in range(1, final):
            out[:, rows_of(tile), :] = inner[:, rows_of(tile), :]
        head = inner[:, :TILE, :]
        tail = inner[:, rows_of(final), :]
        if bounds is None:
            head = head + jnp.where(top, opening, 0.0)
            tail = tail + jnp.where(top, 0.0, ending)
        else:
            head = jnp.where(place < bounds[0], opening, head)
            tail = jnp.where(place > bounds[1], ending, tail)
        out[:, :TILE, :] = head
        out[:, rows_of(final), :] = tail
        out[:, rows:, :] = jnp.where(top, ending, opening)

    for k in range(3):
        ring(push_in_ref[k], sums_ref[k], first_ref[k], push_ref.at[k], None)
    for k in range(PAIRS):
        bounds = (2, 5) if k == PAIRS - 1 else (1, 4)
        ring(pairs_in_ref[k], sums_ref[3 + k], first_ref[3 + k], pairs_ref.at[k], bounds)


def seam_first_pass(section_index, checkpoints, targets, sea, ends, seen, before):
    count = checkpoints.shape[0]
    lanes = sea.shape[1] // LANES
    tile = pltpu.VMEM((lanes, TILE, LANES), F32)
    padded = pltpu.VMEM((lanes, 3 * TILE, LANES), F32)
    sums = jax.ShapeDtypeStruct((3 + PAIRS, lanes, TILE, LANES), F32)
    return pl.pallas_call(
        seam_first,
        name="seam_first",
        out_shape=(sums,) + end_shapes(checkpoints),
        in_specs=[SMEM] + [HBM] * 2 + [VMEM] * 4,
        out_specs=(VMEM,) * 3,
        scratch_shapes=[pltpu.SemaphoreType.DMA((count + 1,))] + [tile] * 5 + [padded] * 9,
        compiler_params=limit(12),
    )(*map(in_hbm, (section_index, checkpoints, targets)), sea, ends, seen, before)


def seam_last_pass(sea, ends, seen, before, after, first, push, pairs):
    rows, cols = sea.shape
    lanes = cols // LANES
    ring = rows + TILE
    tile = pltpu.VMEM((lanes, TILE, LANES), F32)
    padded = pltpu.VMEM((lanes, 3 * TILE, LANES), F32)
    return pl.pallas_call(
        seam_last,
        name="seam_last",
        out_shape=(
            jax.ShapeDtypeStruct((3, lanes, ring, LANES), F32),
            jax.ShapeDtypeStruct((PAIRS, lanes, ring, LANES), F32),
            jax.ShapeDtypeStruct((lanes, ring, LANES), BF16),
        ),
        in_specs=[VMEM] * 8,
        out_specs=(VMEM,) * 3,
        scratch_shapes=[tile] * 5
        + [pltpu.VMEM((3 + PAIRS, lanes, TILE, LANES), F32)]
        + [padded] * 9,
        compiler_params=limit(20),
    )(sea, ends, seen, before, after, first, push, pairs)


def make_coeffs(slab_ref, basis_ref, pieces_ref, out_ref):
    slabs, _, quarter = pieces_ref.shape
    rows, width = basis_ref.shape
    rows_out = width // slabs
    slab = slab_ref[0]

    def edge_of(k):
        parts = []
        for q in range(width // quarter):
            start = rows_out + rows + TILE * (q // 2)
            part = pieces_ref[k, start : start + TILE, :].astype(F32)
            parts.append(pltpu.roll(part, 4, 0) if q % 2 else part)
        return jnp.concatenate(parts, axis=1)

    after = edge_of(jnp.minimum(slab + 1, slabs - 1))
    before = pltpu.roll(edge_of(jnp.maximum(slab - 1, 0)), 4, 0)
    row = tile_rows((TILE, width))
    use_after = (row < 2) & (slab < slabs - 1)
    use_before = (row >= 6) & (slab > 0)
    edge = jnp.where(use_after, after, jnp.where(use_before, before, 0.0))
    basis = jnp.concatenate([basis_ref[...].astype(F32), edge], axis=0).astype(BF16)
    part = pieces_ref[:, :rows_out, :].reshape(width, quarter)
    out_ref[...] = jnp.dot(basis, part, preferred_element_type=F32).astype(BF16)


def coeffs_part(slab, basis_rows, pieces):
    return pl.pallas_call(
        make_coeffs,
        name="make_coeffs",
        out_shape=jax.ShapeDtypeStruct((basis_rows.shape[0] + TILE, pieces.shape[2]), BF16),
        in_specs=[SMEM, VMEM, VMEM],
        out_specs=VMEM,
        compiler_params=limit(12),
    )(slab.reshape(1), basis_rows, pieces)


def apply_potential(member_ref, own_ref, near_ref, far_ref, both_ref, cols_ref, push_ref, pairs_ref, mask_ref, keep_ref, give_ref, coeffs, total, field, east, part, gy, *rings):
    member = member_ref[0]
    quarter = own_ref.shape[1]
    for bits, ref in enumerate((own_ref, near_ref, far_ref, both_ref)):
        at = pl.multiple_of((member ^ bits) * quarter, quarter)
        coeffs[:, pl.ds(at, quarter)] = ref[...]
    field[...] = lax.dot_general(
        coeffs[...], cols_ref[...], (((1,), (1,)), ((), ())), preferred_element_type=F32
    )
    same, two_x, two_y, up, down = (pairs_ref.at[k] for k in range(PAIRS))
    potential, masks, right_xs, right_ys, norths, two_norths, gx = (
        Ring(ref) for ref in rings[:7]
    )
    back_up_x, back_up_y, back_down_x, back_down_y = (Ring(ref) for ref in rings[7:])
    tiles = field.shape[0] // TILE
    own_tiles = tiles - 1
    unit = -4.0 / TIME_STEP**2

    for tile in range(tiles):
        potential.put(tile, split_lanes(field[rows_of(tile), :]))
        masks.put(tile, mask_ref[:, rows_of(tile), :].astype(F32))

    for tile in range(tiles):
        here = rows_of(tile)
        sx = potential.get(tile, -1) - potential.get(tile, 1)
        sy = dx(potential.get(tile))
        east[:, here, :] = sx
        right_x = shift_cols(sx, 1)
        right_xs.put(tile, right_x)
        right_ys.put(tile, shift_cols(sy, 1))
        norths.put(tile, sy)
        two_norths.put(tile, two_y[:, here, :] * sy)
        up_here = up[:, here, :]
        down_here = down[:, here, :]
        back_up_x.put(tile, shift_cols(up_here * sx, -1))
        back_up_y.put(tile, shift_cols(up_here * sy, -1))
        back_down_x.put(tile, shift_cols(down_here * sx, -1))
        back_down_y.put(tile, shift_cols(down_here * sy, -1))
        beside = masks.get(tile) * two_x[:, here, :]
        part[:, here, :] = shift_cols(
            beside * right_x + unit * push_ref[0, :, here, :], 1
        ) + shift_cols(beside * shift_cols(sx, -1) - unit * push_ref[1, :, here, :], -1)

    for tile in range(tiles):
        here = rows_of(tile)
        mask = masks.get(tile)
        same_x = same[:, here, :] * east[:, here, :]
        up_here = up[:, here, :]
        down_here = down[:, here, :]
        ahead = up_here * right_ys.get(tile, 1) - same_x - down_here * right_ys.get(tile, -1)
        behind = same_x + back_down_y.get(tile, 1) - back_up_y.get(tile, -1)
        gx.put(
            tile,
            part[:, here, :] + shift_cols(mask, 1) * ahead - shift_cols(mask, -1) * behind,
        )
        if tile < own_tiles:
            same_y = same[:, here, :] * norths.get(tile)
            ahead = (
                up_here * right_xs.get(tile, 1)
                - back_down_x.get(tile, 1)
                + two_y[:, here, :] * norths.get(tile, 2)
                - same_y
            )
            behind = (
                down_here * right_xs.get(tile, -1)
                - back_up_x.get(tile, -1)
                + same_y
                - two_norths.get(tile, -2)
            )
            gy[:, here, :] = (
                unit * push_ref[2, :, here, :]
                + masks.get(tile, 1) * ahead
                - masks.get(tile, -1) * behind
            )

    scale = -(TIME_STEP**4) / 64.0
    for tile in range(own_tiles):
        here = rows_of(tile)
        total[here, :] = join_lanes(
            scale * (gx.get(tile, 1) - gx.get(tile, -1) - dx(gy[:, here, :]))
        )
    pair = keep_ref.shape[0]
    core = member % 2
    keep_ref[...] = total[pl.ds(pl.multiple_of(core * pair, pair), pair), :]
    give_ref[...] = total[pl.ds(pl.multiple_of((1 - core) * pair, pair), pair), :]


def gradient_halves(member, parts, basis_cols, push, pairs, mask):
    lanes, ring, _ = mask.shape
    cols, width = basis_cols.shape
    pair = (ring - TILE) // 2
    half = jax.ShapeDtypeStruct((pair, cols), F32)
    return pl.pallas_call(
        apply_potential,
        name="apply_potential",
        out_shape=(half, half),
        in_specs=[SMEM] + [VMEM] * 8,
        out_specs=(VMEM, VMEM),
        scratch_shapes=[
            pltpu.VMEM((ring, width), BF16),
            pltpu.VMEM((2 * pair, cols), F32),
            pltpu.VMEM((ring, cols), F32),
        ]
        + [pltpu.VMEM((lanes, ring, LANES), F32)] * 3
        + [pltpu.VMEM((lanes, ring + 2 * TILE, LANES), F32)] * 11,
        compiler_params=limit(24),
    )(member.reshape(1), *parts, basis_cols, push, pairs, mask)


def project(own_ref, other_ref, cols_ref, out_ref):
    total = (own_ref[...] + other_ref[...]).astype(BF16)
    projected = jnp.dot(total, cols_ref[...], preferred_element_type=F32).astype(BF16)
    half = out_ref.shape[3]
    for core in range(2):
        part = projected[:, core * half : (core + 1) * half]
        for chip in range(out_ref.shape[1] // 2):
            for k in range(out_ref.shape[0]):
                out_ref[k, 2 * chip + core] = part


def projected_pieces(own, other, basis_cols, members, slabs):
    single = own.shape[0]
    half = basis_cols.shape[1] // 2
    return pl.pallas_call(
        project,
        name="project",
        out_shape=jax.ShapeDtypeStruct((slabs, members, single, half), BF16),
        in_specs=[VMEM] * 3,
        out_specs=VMEM,
        compiler_params=limit(16),
    )(own, other, basis_cols)


def assemble(member_ref, own_ref, far_ref, near_ref, control_ref, basis_ref, kept_ref, sem):
    copy = pltpu.make_async_copy(control_ref, kept_ref, sem)
    copy.start()
    member = member_ref[0]
    quarter = own_ref.shape[1]
    parts = (own_ref[...], near_ref[0], far_ref[...], near_ref[1])
    for bits, part in enumerate(parts):
        at = pl.multiple_of((member ^ bits) * quarter, quarter)
        basis_ref[pl.ds(at, quarter), :] = part.astype(F32).T.astype(BF16)
    copy.wait()


def assembled(member, own, far, near, control):
    rows, _ = own.shape
    width = control.shape[1]
    return pl.pallas_call(
        assemble,
        name="assemble",
        out_shape=(
            jax.ShapeDtypeStruct((width, rows), BF16),
            jax.ShapeDtypeStruct(control.shape, F32),
        ),
        in_specs=[SMEM, VMEM, VMEM, VMEM, HBM],
        out_specs=(VMEM, VMEM),
        scratch_shapes=[pltpu.SemaphoreType.DMA],
        compiler_params=limit(24),
    )(member.reshape(1), own, far, near, in_hbm(control))


def gradient(slab_ref, basis_ref, projected_ref, out_ref):
    rows_out = out_ref.shape[0] - TILE
    width = basis_ref.shape[0]
    half = out_ref.shape[1]
    projected = projected_ref[...]
    block = width // 4
    squares = jnp.zeros((TILE, half), F32)
    for k in range(4):
        part = jnp.dot(
            basis_ref[k * block : (k + 1) * block, :], projected, preferred_element_type=F32
        )
        squares += jnp.sum((part * part).reshape(block // TILE, TILE, half), axis=0)
    at = pl.multiple_of(slab_ref[0] * rows_out, rows_out)
    out_ref[:rows_out] = jnp.dot(
        basis_ref[pl.ds(at, rows_out), :], projected, preferred_element_type=F32
    )
    out_ref[rows_out:] = squares


def gradient_block(slab, basis, projected, rows_out):
    half = projected.shape[1]
    return pl.pallas_call(
        gradient,
        name="gradient",
        out_shape=jax.ShapeDtypeStruct((rows_out + TILE, half), F32),
        in_specs=[SMEM, VMEM, VMEM],
        out_specs=VMEM,
        compiler_params=limit(24),
    )(slab.reshape(1), basis, projected)


def update(core_ref, control_ref, own_ref, other_ref, out_ref):
    rows_out, width = control_ref.shape
    half = width // 2
    total = jnp.sum(own_ref[rows_out:] + other_ref[rows_out:])
    scale = STEP_SIZE * lax.rsqrt(total / (width * width) + EPSILON)
    for turn, ref in enumerate((own_ref, other_ref)):
        at = pl.multiple_of((core_ref[0] ^ turn) * half, half)
        out_ref[:, pl.ds(at, half)] = control_ref[:, pl.ds(at, half)] - ref[:rows_out] * scale


def updated(core, control, own, other):
    return pl.pallas_call(
        update,
        name="update",
        out_shape=jax.ShapeDtypeStruct(control.shape, F32),
        in_specs=[SMEM, VMEM, VMEM, VMEM],
        out_specs=VMEM,
        compiler_params=limit(8),
    )(core.reshape(1), control, own, other)


def partner(value, bit):
    count = lax.axis_size("ens")
    return lax.ppermute(value, "ens", [(i, i ^ bit) for i in range(count)])


def on_device(checkpoints, section_index, targets, sea_mask, basis_rows, basis_cols, control):
    members = lax.axis_size("ens")
    slabs = lax.axis_size("space")
    member = lax.axis_index("ens").astype(jnp.int32)
    slab = lax.axis_index("space").astype(jnp.int32)
    core = member & 1
    chip = member >> 1
    rows_out, width = control.shape
    rows = basis_rows.shape[0]
    quarter = width // members
    half = width // 2
    single = rows // 4

    pieces = pieces_for(member, basis_rows, control, slabs, quarter)
    pieces = lax.all_to_all(pieces, "space", 0, 0)
    up, down = edge_messages(section_index, checkpoints, targets, sea_mask)
    before = lax.ppermute(up, "space", [(i, i + 1) for i in range(slabs - 1)])
    after = lax.ppermute(down, "space", [(i + 1, i) for i in range(slabs - 1)])
    push, pairs, near_rows = inner_pass(section_index, checkpoints, targets, sea_mask, basis_rows)
    own = coeffs_part(slab, near_rows, pieces)
    parts = [own]
    for bits in (1, 2, 3):
        parts.append(partner(own, bits))
    sea, ends, seen = fetched_ends(section_index, checkpoints, targets, sea_mask)
    first, ends, seen = seam_first_pass(
        section_index, checkpoints, targets, sea, ends, seen, before
    )
    push, pairs, mask = seam_last_pass(sea, ends, seen, before, after, first, push, pairs)
    keep, give = gradient_halves(member, parts, basis_cols, push, pairs, mask)

    keep = keep + partner(give, 1)
    own_rows = lax.dynamic_slice_in_dim(keep, chip * single, single, 0)
    give = lax.dynamic_slice_in_dim(keep, (1 - chip) * single, single, 0)
    arriving = partner(give, 2)
    cols = held(basis_cols)
    send = projected_pieces(own_rows, arriving, cols, members, slabs)
    got = lax.all_to_all(send.reshape(members * slabs, single, half), ("space", "ens"), 0, 0)
    projected_half = got.reshape(slabs * rows, half)

    part = pieces[:, rows_out : rows_out + rows, :].reshape(slabs, 2, members // 2, single, quarter)
    part = part.transpose(0, 2, 1, 3, 4).reshape(slabs * rows, quarter)
    far = partner(part, 2)
    near = partner(jnp.stack([part, far]), 1)
    basis, kept = assembled(member, part, far, near, control)
    block = gradient_block(slab, basis, projected_half, rows_out)
    other = partner(block, 1)
    return updated(core, kept, block, other)


def solution(mesh):
    return jax.shard_map(
        on_device,
        mesh=mesh,
        in_specs=(
            P("ens", None, None, "space", None),
            P("ens"),
            P("ens", "space", None),
            P("space", None),
            P("space", None),
            P(),
            P("space", None),
        ),
        out_specs=P("space", None),
        check_vma=False,
    )
```

```python
import jax
import jax.numpy as jnp
from jax import lax
from jax.experimental import pallas as pl
from jax.experimental.pallas import tpu as pltpu
from jax.sharding import PartitionSpec as P


DEPTH = 1.0
GRAVITY = 1.0
CORIOLIS = 0.5
FRICTION = 0.1
TIME_STEP = 0.3
STEP_SIZE = 1.0
EPSILON = 1e-06

F32 = jnp.float32
BF16 = jnp.bfloat16
TILE = 8
LANES = 128
MIB = 1 << 20


VMEM = pl.BlockSpec(memory_space=pltpu.VMEM)
SMEM = pl.BlockSpec(memory_space=pltpu.SMEM)
HBM = pl.BlockSpec(memory_space=pltpu.HBM)


def limit(mib):
    return pltpu.CompilerParams(vmem_limit_bytes=mib * MIB)


def tile_rows(shape):
    return lax.broadcasted_iota(jnp.int32, shape, 0)


def split_lanes(field):
    return jnp.stack([field[:, k : k + LANES] for k in range(0, field.shape[1], LANES)])


def join_lanes(field):
    return jnp.concatenate([field[k] for k in range(field.shape[0])], axis=1)


def shift_cols(field, step):
    turned = pltpu.roll(field, (-step) % LANES, 2)
    lane = lax.broadcasted_iota(jnp.int32, field.shape, 2)
    outside = jnp.zeros_like(turned[:1])
    if step > 0:
        beside = jnp.concatenate([turned[1:], outside], axis=0)
        return jnp.where(lane >= LANES - step, beside, turned)
    beside = jnp.concatenate([outside, turned[:-1]], axis=0)
    return jnp.where(lane < -step, beside, turned)


def dx(field):
    return shift_cols(field, 1) - shift_cols(field, -1)


def fetch(source, target, sem):
    copy = pltpu.make_async_copy(source, target, sem)
    copy.start()
    return copy


def pack_edges(index_ref, states_ref, targets_ref, sea_ref, up_ref, down_ref, last, first, seen, sea, sems):
    count, _, _, rows, cols = states_ref.shape
    states = []
    for s in range(count):
        slot = index_ref[s]
        for side, (buffer, row) in enumerate(((last, rows - TILE), (first, 0))):
            source = states_ref.at[s, slot, :, pl.ds(row, TILE), :]
            states.append(fetch(source, buffer.at[s], sems.at[side, s]))
    others = [
        fetch(targets_ref.at[:, pl.ds(rows - TILE, TILE), :], seen.at[0], sems.at[0, count]),
        fetch(targets_ref.at[:, pl.ds(0, TILE), :], seen.at[1], sems.at[1, count]),
        fetch(sea_ref.at[pl.ds(rows - TILE, TILE), :], sea.at[0], sems.at[0, count + 1]),
        fetch(sea_ref.at[pl.ds(0, TILE), :], sea.at[1], sems.at[1, count + 1]),
    ]
    row = tile_rows((TILE, cols))
    for s in range(count):
        states[2 * s].wait()
        height, east, north = (last[s, f].astype(F32) for f in range(3))
        height, north = pltpu.roll(height, 3, 0), pltpu.roll(north, 6, 0)
        up_ref[s] = jnp.where(row < 3, height, jnp.where(row < 6, north, east)).astype(BF16)
        states[2 * s + 1].wait()
        height, east, north = (first[s, f].astype(F32) for f in range(3))
        east, north = pltpu.roll(east, 6, 0), pltpu.roll(north, 3, 0)
        down_ref[s] = jnp.where(row < 3, height, jnp.where(row < 6, north, east)).astype(BF16)
    for copy in others:
        copy.wait()
    targets_up = jnp.zeros((TILE, cols), F32)
    targets_down = jnp.zeros((TILE, cols), F32)
    for s in range(count):
        targets_up = jnp.where(row == s, seen[0, s].astype(F32)[TILE - 1 :, :], targets_up)
        targets_down = jnp.where(row == s, seen[1, s].astype(F32)[:1, :], targets_down)
    up_ref[count] = targets_up.astype(BF16)
    down_ref[count] = targets_down.astype(BF16)
    up_ref[count + 1] = sea[0].astype(F32).astype(BF16)
    down_ref[count + 1] = sea[1].astype(F32).astype(BF16)


def edge_messages(section_index, checkpoints, targets, sea_mask):
    count, _, fields, _, cols = checkpoints.shape
    edges = jax.ShapeDtypeStruct((count + 2, TILE, cols), BF16)
    return pl.pallas_call(
        pack_edges,
        name="pack_edges",
        out_shape=(edges, edges),
        in_specs=[SMEM] + [HBM] * 3,
        out_specs=(VMEM, VMEM),
        scratch_shapes=[
            pltpu.VMEM((count, fields, TILE, cols), BF16),
            pltpu.VMEM((count, fields, TILE, cols), BF16),
            pltpu.VMEM((2, count, TILE, cols), BF16),
            pltpu.VMEM((2, TILE, cols), jnp.int32),
            pltpu.SemaphoreType.DMA((2, count + 2)),
        ],
        compiler_params=limit(12),
    )(*map(in_hbm, (section_index, checkpoints, targets, sea_mask)))


def pack_pieces(member_ref, basis_ref, control_ref, out_ref, basis, own, sems):
    rows, width = basis_ref.shape
    rows_out = control_ref.shape[0]
    slabs, _, quarter = out_ref.shape
    at = pl.multiple_of(member_ref[0] * quarter, quarter)
    copies = [
        fetch(control_ref.at[:, pl.ds(at, quarter)], own, sems.at[0]),
        fetch(basis_ref, basis, sems.at[1]),
    ]
    for copy in copies:
        copy.wait()
    part = own[...].astype(BF16)
    part_basis = basis[:, pl.ds(at, quarter)]
    row = tile_rows((TILE, width))
    first = basis[:TILE, :].astype(F32)
    last = pltpu.roll(basis[rows - TILE :, :].astype(F32), 4, 0)
    both = jnp.where(row < 2, first, last)
    tiles = []
    for q in range(0, width // quarter, 2):
        here = both[:, q * quarter : (q + 1) * quarter]
        below = pltpu.roll(both[:, (q + 1) * quarter : (q + 2) * quarter], 4, 0)
        tiles.append(jnp.where(row[:, :quarter] < 4, here, below))
    edges = jnp.concatenate(tiles, axis=0).astype(BF16)
    for k in range(slabs):
        out_ref[k, :rows_out] = part
        out_ref[k, rows_out : rows_out + rows] = part_basis
        out_ref[k, rows_out + rows :] = edges


def pieces_for(member, basis_rows, control, slabs, quarter):
    rows, width = basis_rows.shape
    rows_out = control.shape[0]
    edges = 4 * width // quarter
    return pl.pallas_call(
        pack_pieces,
        name="pack_pieces",
        out_shape=jax.ShapeDtypeStruct((slabs, rows_out + rows + edges, quarter), BF16),
        in_specs=[SMEM, HBM, HBM],
        out_specs=VMEM,
        scratch_shapes=[
            pltpu.VMEM((rows, width), BF16),
            pltpu.VMEM((rows_out, quarter), F32),
            pltpu.SemaphoreType.DMA((2,)),
        ],
        compiler_params=limit(10),
    )(member.reshape(1), in_hbm(basis_rows), in_hbm(control))


def in_hbm(array):
    return pltpu.with_memory_space_constraint(array, pltpu.HBM)


def hold(source_ref, out_ref, sem):
    copy = pltpu.make_async_copy(source_ref, out_ref, sem)
    copy.start()
    copy.wait()


def held(array):
    size = array.size * array.dtype.itemsize
    return pl.pallas_call(
        hold,
        name="hold",
        out_shape=jax.ShapeDtypeStruct(array.shape, array.dtype),
        in_specs=[HBM],
        out_specs=VMEM,
        scratch_shapes=[pltpu.SemaphoreType.DMA],
        compiler_params=limit(size // MIB + 2),
    )(in_hbm(array))


PAIRS = 5


class Rows:
    def __init__(self, ref):
        self.ref = ref

    def put(self, tile, value):
        self.ref[:, TILE * (tile + 1) : TILE * (tile + 2), :] = value

    def put_at(self, start, value):
        self.ref[:, start : start + value.shape[1], :] = value

    def get(self, tile, step=0):
        start = TILE * (tile + 1) + step
        return self.ref[:, start : start + TILE, :]


class Ring(Rows):
    def put(self, tile, value):
        super().put(tile, value)
        rows = self.ref.shape[1]
        if tile == 0:
            self.ref[:, rows - TILE :, :] = value
        if TILE * (tile + 3) == rows:
            self.ref[:, :TILE, :] = value


def rows_of(tile):
    return slice(TILE * tile, TILE * (tile + 1))


def clear(*refs):
    for ref in refs:
        ref[...] = jnp.zeros_like(ref)


def add_state(tiles, state, mask, live, padded, plain, sums):
    heights, easts, norths, seens = state
    fluxes, mid_fluxes, weights, rights, misfits = (Rows(ref) for ref in padded)
    lefts, partial = plain
    push_left, push_right, gy, same, two_x, two_y, up, down = sums
    half = 0.5 * TIME_STEP
    keep = 1.0 - TIME_STEP * FRICTION
    turn = TIME_STEP * CORIOLIS / keep
    slope = half * GRAVITY / keep

    for tile in range(tiles):
        fluxes.put(tile, (DEPTH + heights.get(tile)) * norths.get(tile))

    for tile in range(tiles):
        here = rows_of(tile)
        height = heights.get(tile)
        east = easts.get(tile)
        north = norths.get(tile)
        flux = dx((DEPTH + height) * east) + (fluxes.get(tile, 1) - fluxes.get(tile, -1))
        sea = mask[:, here, :]
        height_mid = sea * (height - half * flux)
        weight = DEPTH * sea + height_mid
        east_mid = east + turn * north - slope * dx(height)
        north_mid = north - turn * east - slope * (heights.get(tile, 1) - heights.get(tile, -1))
        right = shift_cols(weight, 1)
        left = shift_cols(weight, -1)
        scaled = half * keep * weight
        mid_fluxes.put(tile, scaled * north_mid)
        weights.put(tile, weight)
        rights.put(tile, right)
        lefts[:, here, :] = left
        same[:, here, :] += weight * weight
        two_x[:, here, :] += left * right
        partial[:, here, :] = (
            height + height_mid - 2.0 * seens.get(tile) - dx(scaled * east_mid)
        )

    for tile in range(tiles):
        here = rows_of(tile)
        change = mid_fluxes.get(tile, 1) - mid_fluxes.get(tile, -1)
        misfit = live[:, here, :] * (partial[:, here, :] - change)
        misfits.put(tile, misfit)
        push_left[:, here, :] += lefts[:, here, :] * misfit
        push_right[:, here, :] += rights.get(tile) * misfit

    for tile in range(tiles):
        here = rows_of(tile)
        weight = weights.get(tile)
        gy[:, here, :] += weight * (misfits.get(tile, 1) - misfits.get(tile, -1))
        two_y[:, here, :] += weight * weights.get(tile, 2)
        up[:, here, :] += weight * rights.get(tile, 1)
        down[:, here, :] += weight * rights.get(tile, -1)


def inner_states(index_ref, states_ref, targets_ref, sea_ref, basis_ref, push_ref, pairs_ref, rows_ref, sems, sea, held_states, held_targets, mask, live, *scratch):
    count = states_ref.shape[0]
    rows = sea_ref.shape[0]
    tiles = rows // TILE
    plain, padded = scratch[:2], scratch[2:]

    def copies_of(k):
        return (
            pltpu.make_async_copy(states_ref.at[k, index_ref[k]], held_states.at[k], sems.at[0, k]),
            pltpu.make_async_copy(targets_ref.at[k], held_targets.at[k], sems.at[1, k]),
        )

    others = (
        pltpu.make_async_copy(sea_ref, sea, sems.at[0, count]),
        pltpu.make_async_copy(basis_ref, rows_ref, sems.at[1, count]),
    )
    for copy in others:
        copy.start()
    for k in range(count):
        for copy in copies_of(k):
            copy.start()
    clear(push_ref, pairs_ref, *padded)
    for copy in others:
        copy.wait()
    for tile in range(tiles):
        mask[:, rows_of(tile), :] = split_lanes(sea[rows_of(tile), :].astype(F32))
    row = lax.broadcasted_iota(jnp.int32, live.shape, 1)
    live[...] = jnp.where((row >= 2) & (row < rows - 2), mask[...], 0.0)

    @pl.loop(0, count)
    def _(s):
        for copy in copies_of(s):
            copy.wait()
        state = [Rows(ref) for ref in padded[:4]]
        for tile in range(tiles):
            for field in range(3):
                value = held_states[s, field, rows_of(tile), :].astype(F32)
                state[field].put(tile, split_lanes(value))
            state[3].put(tile, split_lanes(held_targets[s, rows_of(tile), :].astype(F32)))
        sums = [push_ref.at[k] for k in range(3)] + [pairs_ref.at[k] for k in range(PAIRS)]
        add_state(tiles, state, mask, live, padded[4:], plain, sums)


def inner_pass(section_index, checkpoints, targets, sea_mask, basis_rows):
    count, _, fields, rows, cols = checkpoints.shape
    width = basis_rows.shape[1]
    lanes = cols // LANES
    padded = pltpu.VMEM((lanes, rows + 2 * TILE, LANES), F32)
    plain = pltpu.VMEM((lanes, rows, LANES), F32)
    outs = (
        jax.ShapeDtypeStruct((3, lanes, rows, LANES), F32),
        jax.ShapeDtypeStruct((PAIRS, lanes, rows, LANES), F32),
        jax.ShapeDtypeStruct((rows, width), BF16),
    )
    return pl.pallas_call(
        inner_states,
        name="inner_states",
        out_shape=outs,
        in_specs=[SMEM] + [HBM] * 4,
        out_specs=(VMEM,) * 3,
        scratch_shapes=[
            pltpu.SemaphoreType.DMA((2, count + 1)),
            pltpu.VMEM((rows, cols), jnp.int32),
            pltpu.VMEM((count, fields, rows, cols), BF16),
            pltpu.VMEM((count, rows, cols), BF16),
        ]
        + [plain] * 4
        + [padded] * 9,
        compiler_params=limit(24),
    )(*map(in_hbm, (section_index, checkpoints, targets, sea_mask, basis_rows)))


def end_copies(index_ref, states_ref, targets_ref, row, ends_out, seen_out, sems):
    here = pl.ds(row, TILE)
    count = states_ref.shape[0]
    copies = [fetch(targets_ref.at[:, here, :], seen_out, sems.at[count])]
    for k in range(count):
        source = states_ref.at[k, index_ref[k], :, here, :]
        copies.append(fetch(source, ends_out.at[k], sems.at[k]))
    return copies


def fetch_ends(index_ref, states_ref, targets_ref, sea_ref, sea_out, ends_out, seen_out, sems):
    count = states_ref.shape[0]
    copies = [fetch(sea_ref, sea_out, sems.at[count + 1])]
    copies += end_copies(index_ref, states_ref, targets_ref, 0, ends_out, seen_out, sems)
    for copy in copies:
        copy.wait()


def end_shapes(checkpoints):
    count, _, fields, _, cols = checkpoints.shape
    return (
        jax.ShapeDtypeStruct((count, fields, TILE, cols), BF16),
        jax.ShapeDtypeStruct((count, TILE, cols), BF16),
    )


def fetched_ends(section_index, checkpoints, targets, sea_mask):
    count = checkpoints.shape[0]
    return pl.pallas_call(
        fetch_ends,
        name="fetch_ends",
        out_shape=(jax.ShapeDtypeStruct(sea_mask.shape, jnp.int32),) + end_shapes(checkpoints),
        in_specs=[SMEM] + [HBM] * 3,
        out_specs=(VMEM,) * 3,
        scratch_shapes=[pltpu.SemaphoreType.DMA((count + 2,))],
        compiler_params=limit(6),
    )(*map(in_hbm, (section_index, checkpoints, targets, sea_mask)))


def seam_first(index_ref, states_ref, targets_ref, sea, ends, seen_ends, before_ref, sums_ref, ends_out, seen_out, sems, seen_edge, mask, live, lefts, partial, *padded):
    count = ends.shape[0]
    rows, cols = sea.shape
    top = tile_rows((TILE, cols)) < 4
    copies = end_copies(
        index_ref, states_ref, targets_ref, rows - TILE, ends_out, seen_out, sems
    )
    clear(sums_ref, *padded)
    seen_edge[...] = split_lanes(before_ref[count].astype(F32))
    beyond = pltpu.roll(before_ref[count + 1].astype(F32), 4, 0)
    row = tile_rows((TILE, cols))
    beyond = jnp.where(row >= 2, beyond, 0.0)
    own = pltpu.roll(sea[:TILE, :].astype(F32), 4, 0)
    mask[...] = split_lanes(jnp.where(top, beyond, own))
    place = lax.broadcasted_iota(jnp.int32, live.shape, 1)
    live[...] = jnp.where((place >= 3) & (place < 6), mask[...], 0.0)
    sums = [sums_ref.at[k] for k in range(3 + PAIRS)]
    state = [Rows(ref) for ref in padded[:4]]

    @pl.loop(0, count)
    def _(s):
        before = split_lanes(before_ref[s].astype(F32))
        state[0].put_at(9, before)
        state[1].put_at(4, before)
        state[2].put_at(6, before)
        state[3].put_at(11, seen_edge[:, pl.ds(s, 1), :])
        for field in range(3):
            state[field].put_at(12, split_lanes(ends[s, field].astype(F32)))
        state[3].put_at(12, split_lanes(seen_ends[s].astype(F32)))
        add_state(1, state, mask, live, padded[4:], (lefts, partial), sums)

    for copy in copies:
        copy.wait()


def seam_last(sea, ends, seen_ends, before_ref, after_ref, first_ref, push_in_ref, pairs_in_ref, push_ref, pairs_ref, mask_ref, seen_edge, mask, live, lefts, partial, sums_ref, *padded):
    count = ends.shape[0]
    rows, cols = sea.shape
    row = tile_rows((TILE, cols))
    top = row < 4
    clear(sums_ref, *padded)
    seen_edge[...] = split_lanes(after_ref[count].astype(F32))
    after = jnp.where(row < 2, after_ref[count + 1].astype(F32), 0.0)
    before = jnp.where(row >= 6, before_ref[count + 1].astype(F32), 0.0)
    own = pltpu.roll(sea[rows - TILE :, :].astype(F32), 4, 0)
    mask[...] = split_lanes(jnp.where(top, own, pltpu.roll(after, 4, 0)))
    for tile in range(rows // TILE):
        mask_ref[:, rows_of(tile), :] = split_lanes(
            sea[rows_of(tile), :].astype(F32)
        ).astype(BF16)
    mask_ref[:, rows:, :] = split_lanes(after + before).astype(BF16)
    place = lax.broadcasted_iota(jnp.int32, live.shape, 1)
    live[...] = jnp.where((place >= 2) & (place < 5), mask[...], 0.0)
    sums = [sums_ref.at[k] for k in range(3 + PAIRS)]
    state = [Rows(ref) for ref in padded[:4]]

    @pl.loop(0, count)
    def _(s):
        after = split_lanes(after_ref[s].astype(F32))
        state[0].put_at(12, after)
        state[1].put_at(6, after)
        state[2].put_at(9, after)
        state[3].put_at(12, seen_edge[:, pl.ds(s, 1), :])
        for field in range(3):
            state[field].put_at(4, split_lanes(ends[s, field].astype(F32)))
        state[3].put_at(4, split_lanes(seen_ends[s].astype(F32)))
        add_state(1, state, mask, live, padded[4:], (lefts, partial), sums)

    place = lax.broadcasted_iota(jnp.int32, lefts.shape, 1)
    top = place < 4
    final = rows // TILE - 1

    def ring(inner, ending, opening, out, bounds):
        ending = pltpu.roll(ending, 4, 1)
        opening = pltpu.roll(opening, 4, 1)
        for tile in range(1, final):
            out[:, rows_of(tile), :] = inner[:, rows_of(tile), :]
        head = inner[:, :TILE, :]
        tail = inner[:, rows_of(final), :]
        if bounds is None:
            head = head + jnp.where(top, opening, 0.0)
            tail = tail + jnp.where(top, 0.0, ending)
        else:
            head = jnp.where(place < bounds[0], opening, head)
            tail = jnp.where(place > bounds[1], ending, tail)
        out[:, :TILE, :] = head
        out[:, rows_of(final), :] = tail
        out[:, rows:, :] = jnp.where(top, ending, opening)

    for k in range(3):
        ring(push_in_ref[k], sums_ref[k], first_ref[k], push_ref.at[k], None)
    for k in range(PAIRS):
        bounds = (2, 5) if k == PAIRS - 1 else (1, 4)
        ring(pairs_in_ref[k], sums_ref[3 + k], first_ref[3 + k], pairs_ref.at[k], bounds)


def seam_first_pass(section_index, checkpoints, targets, sea, ends, seen, before):
    count = checkpoints.shape[0]
    lanes = sea.shape[1] // LANES
    tile = pltpu.VMEM((lanes, TILE, LANES), F32)
    padded = pltpu.VMEM((lanes, 3 * TILE, LANES), F32)
    sums = jax.ShapeDtypeStruct((3 + PAIRS, lanes, TILE, LANES), F32)
    return pl.pallas_call(
        seam_first,
        name="seam_first",
        out_shape=(sums,) + end_shapes(checkpoints),
        in_specs=[SMEM] + [HBM] * 2 + [VMEM] * 4,
        out_specs=(VMEM,) * 3,
        scratch_shapes=[pltpu.SemaphoreType.DMA((count + 1,))] + [tile] * 5 + [padded] * 9,
        compiler_params=limit(12),
    )(*map(in_hbm, (section_index, checkpoints, targets)), sea, ends, seen, before)


def seam_last_pass(sea, ends, seen, before, after, first, push, pairs):
    rows, cols = sea.shape
    lanes = cols // LANES
    ring = rows + TILE
    tile = pltpu.VMEM((lanes, TILE, LANES), F32)
    padded = pltpu.VMEM((lanes, 3 * TILE, LANES), F32)
    return pl.pallas_call(
        seam_last,
        name="seam_last",
        out_shape=(
            jax.ShapeDtypeStruct((3, lanes, ring, LANES), F32),
            jax.ShapeDtypeStruct((PAIRS, lanes, ring, LANES), F32),
            jax.ShapeDtypeStruct((lanes, ring, LANES), BF16),
        ),
        in_specs=[VMEM] * 8,
        out_specs=(VMEM,) * 3,
        scratch_shapes=[tile] * 5
        + [pltpu.VMEM((3 + PAIRS, lanes, TILE, LANES), F32)]
        + [padded] * 9,
        compiler_params=limit(20),
    )(sea, ends, seen, before, after, first, push, pairs)


def make_coeffs(slab_ref, basis_ref, pieces_ref, out_ref):
    slabs, _, quarter = pieces_ref.shape
    rows, width = basis_ref.shape
    rows_out = width // slabs
    slab = slab_ref[0]

    def edge_of(k):
        parts = []
        for q in range(width // quarter):
            start = rows_out + rows + TILE * (q // 2)
            part = pieces_ref[k, start : start + TILE, :].astype(F32)
            parts.append(pltpu.roll(part, 4, 0) if q % 2 else part)
        return jnp.concatenate(parts, axis=1)

    after = edge_of(jnp.minimum(slab + 1, slabs - 1))
    before = pltpu.roll(edge_of(jnp.maximum(slab - 1, 0)), 4, 0)
    row = tile_rows((TILE, width))
    use_after = (row < 2) & (slab < slabs - 1)
    use_before = (row >= 6) & (slab > 0)
    edge = jnp.where(use_after, after, jnp.where(use_before, before, 0.0))
    basis = jnp.concatenate([basis_ref[...].astype(F32), edge], axis=0).astype(BF16)
    part = pieces_ref[:, :rows_out, :].reshape(width, quarter)
    out_ref[...] = jnp.dot(basis, part, preferred_element_type=F32).astype(BF16)


def coeffs_part(slab, basis_rows, pieces):
    return pl.pallas_call(
        make_coeffs,
        name="make_coeffs",
        out_shape=jax.ShapeDtypeStruct((basis_rows.shape[0] + TILE, pieces.shape[2]), BF16),
        in_specs=[SMEM, VMEM, VMEM],
        out_specs=VMEM,
        compiler_params=limit(12),
    )(slab.reshape(1), basis_rows, pieces)


def apply_potential(member_ref, own_ref, near_ref, far_ref, both_ref, cols_ref, push_ref, pairs_ref, mask_ref, keep_ref, give_ref, coeffs, total, field, east, part, gy, *rings):
    member = member_ref[0]
    quarter = own_ref.shape[1]
    for bits, ref in enumerate((own_ref, near_ref, far_ref, both_ref)):
        at = pl.multiple_of((member ^ bits) * quarter, quarter)
        coeffs[:, pl.ds(at, quarter)] = ref[...]
    field[...] = lax.dot_general(
        coeffs[...], cols_ref[...], (((1,), (1,)), ((), ())), preferred_element_type=F32
    )
    same, two_x, two_y, up, down = (pairs_ref.at[k] for k in range(PAIRS))
    potential, masks, right_xs, right_ys, norths, two_norths, gx = (
        Ring(ref) for ref in rings[:7]
    )
    back_up_x, back_up_y, back_down_x, back_down_y = (Ring(ref) for ref in rings[7:])
    tiles = field.shape[0] // TILE
    own_tiles = tiles - 1
    unit = -4.0 / TIME_STEP**2

    for tile in range(tiles):
        potential.put(tile, split_lanes(field[rows_of(tile), :]))
        masks.put(tile, mask_ref[:, rows_of(tile), :].astype(F32))

    for tile in range(tiles):
        here = rows_of(tile)
        sx = potential.get(tile, -1) - potential.get(tile, 1)
        sy = dx(potential.get(tile))
        east[:, here, :] = sx
        right_x = shift_cols(sx, 1)
        right_xs.put(tile, right_x)
        right_ys.put(tile, shift_cols(sy, 1))
        norths.put(tile, sy)
        two_norths.put(tile, two_y[:, here, :] * sy)
        up_here = up[:, here, :]
        down_here = down[:, here, :]
        back_up_x.put(tile, shift_cols(up_here * sx, -1))
        back_up_y.put(tile, shift_cols(up_here * sy, -1))
        back_down_x.put(tile, shift_cols(down_here * sx, -1))
        back_down_y.put(tile, shift_cols(down_here * sy, -1))
        beside = masks.get(tile) * two_x[:, here, :]
        part[:, here, :] = shift_cols(
            beside * right_x + unit * push_ref[0, :, here, :], 1
        ) + shift_cols(beside * shift_cols(sx, -1) - unit * push_ref[1, :, here, :], -1)

    for tile in range(tiles):
        here = rows_of(tile)
        mask = masks.get(tile)
        same_x = same[:, here, :] * east[:, here, :]
        up_here = up[:, here, :]
        down_here = down[:, here, :]
        ahead = up_here * right_ys.get(tile, 1) - same_x - down_here * right_ys.get(tile, -1)
        behind = same_x + back_down_y.get(tile, 1) - back_up_y.get(tile, -1)
        gx.put(
            tile,
            part[:, here, :] + shift_cols(mask, 1) * ahead - shift_cols(mask, -1) * behind,
        )
        if tile < own_tiles:
            same_y = same[:, here, :] * norths.get(tile)
            ahead = (
                up_here * right_xs.get(tile, 1)
                - back_down_x.get(tile, 1)
                + two_y[:, here, :] * norths.get(tile, 2)
                - same_y
            )
            behind = (
                down_here * right_xs.get(tile, -1)
                - back_up_x.get(tile, -1)
                + same_y
                - two_norths.get(tile, -2)
            )
            gy[:, here, :] = (
                unit * push_ref[2, :, here, :]
                + masks.get(tile, 1) * ahead
                - masks.get(tile, -1) * behind
            )

    scale = -(TIME_STEP**4) / 64.0
    for tile in range(own_tiles):
        here = rows_of(tile)
        total[here, :] = join_lanes(
            scale * (gx.get(tile, 1) - gx.get(tile, -1) - dx(gy[:, here, :]))
        )
    pair = keep_ref.shape[0]
    core = member % 2
    keep_ref[...] = total[pl.ds(pl.multiple_of(core * pair, pair), pair), :]
    give_ref[...] = total[pl.ds(pl.multiple_of((1 - core) * pair, pair), pair), :]


def gradient_halves(member, parts, basis_cols, push, pairs, mask):
    lanes, ring, _ = mask.shape
    cols, width = basis_cols.shape
    pair = (ring - TILE) // 2
    half = jax.ShapeDtypeStruct((pair, cols), F32)
    return pl.pallas_call(
        apply_potential,
        name="apply_potential",
        out_shape=(half, half),
        in_specs=[SMEM] + [VMEM] * 8,
        out_specs=(VMEM, VMEM),
        scratch_shapes=[
            pltpu.VMEM((ring, width), BF16),
            pltpu.VMEM((2 * pair, cols), F32),
            pltpu.VMEM((ring, cols), F32),
        ]
        + [pltpu.VMEM((lanes, ring, LANES), F32)] * 3
        + [pltpu.VMEM((lanes, ring + 2 * TILE, LANES), F32)] * 11,
        compiler_params=limit(24),
    )(member.reshape(1), *parts, basis_cols, push, pairs, mask)


def project(own_ref, other_ref, cols_ref, out_ref):
    total = (own_ref[...] + other_ref[...]).astype(BF16)
    projected = jnp.dot(total, cols_ref[...], preferred_element_type=F32).astype(BF16)
    half = out_ref.shape[3]
    for core in range(2):
        part = projected[:, core * half : (core + 1) * half]
        for chip in range(out_ref.shape[1] // 2):
            for k in range(out_ref.shape[0]):
                out_ref[k, 2 * chip + core] = part


def projected_pieces(own, other, basis_cols, members, slabs):
    single = own.shape[0]
    half = basis_cols.shape[1] // 2
    return pl.pallas_call(
        project,
        name="project",
        out_shape=jax.ShapeDtypeStruct((slabs, members, single, half), BF16),
        in_specs=[VMEM] * 3,
        out_specs=VMEM,
        compiler_params=limit(16),
    )(own, other, basis_cols)


def assemble(member_ref, own_ref, far_ref, near_ref, both_ref, control_ref, basis_ref, kept_ref, sem):
    copy = pltpu.make_async_copy(control_ref, kept_ref, sem)
    copy.start()
    member = member_ref[0]
    quarter = own_ref.shape[1]
    parts = (own_ref[...], near_ref[...], far_ref[...], both_ref[...])
    for bits, part in enumerate(parts):
        at = pl.multiple_of((member ^ bits) * quarter, quarter)
        basis_ref[pl.ds(at, quarter), :] = part.astype(F32).T.astype(BF16)
    copy.wait()


def assembled(member, own, far, near, both, control):
    rows, _ = own.shape
    width = control.shape[1]
    return pl.pallas_call(
        assemble,
        name="assemble",
        out_shape=(
            jax.ShapeDtypeStruct((width, rows), BF16),
            jax.ShapeDtypeStruct(control.shape, F32),
        ),
        in_specs=[SMEM, VMEM, VMEM, VMEM, VMEM, HBM],
        out_specs=(VMEM, VMEM),
        scratch_shapes=[pltpu.SemaphoreType.DMA],
        compiler_params=limit(24),
    )(member.reshape(1), own, far, near, both, in_hbm(control))


def gradient(slab_ref, basis_ref, projected_ref, out_ref):
    rows_out = out_ref.shape[0] - TILE
    width = basis_ref.shape[0]
    half = out_ref.shape[1]
    projected = projected_ref[...]
    block = width // 4
    squares = jnp.zeros((TILE, half), F32)
    for k in range(4):
        part = jnp.dot(
            basis_ref[k * block : (k + 1) * block, :], projected, preferred_element_type=F32
        )
        squares += jnp.sum((part * part).reshape(block // TILE, TILE, half), axis=0)
    at = pl.multiple_of(slab_ref[0] * rows_out, rows_out)
    out_ref[:rows_out] = jnp.dot(
        basis_ref[pl.ds(at, rows_out), :], projected, preferred_element_type=F32
    )
    out_ref[rows_out:] = squares


def gradient_block(slab, basis, projected, rows_out):
    half = projected.shape[1]
    return pl.pallas_call(
        gradient,
        name="gradient",
        out_shape=jax.ShapeDtypeStruct((rows_out + TILE, half), F32),
        in_specs=[SMEM, VMEM, VMEM],
        out_specs=VMEM,
        compiler_params=limit(24),
    )(slab.reshape(1), basis, projected)


def update(core_ref, control_ref, own_ref, other_ref, out_ref):
    rows_out, width = control_ref.shape
    half = width // 2
    total = jnp.sum(own_ref[rows_out:] + other_ref[rows_out:])
    scale = STEP_SIZE * lax.rsqrt(total / (width * width) + EPSILON)
    for turn, ref in enumerate((own_ref, other_ref)):
        at = pl.multiple_of((core_ref[0] ^ turn) * half, half)
        out_ref[:, pl.ds(at, half)] = control_ref[:, pl.ds(at, half)] - ref[:rows_out] * scale


def updated(core, control, own, other):
    return pl.pallas_call(
        update,
        name="update",
        out_shape=jax.ShapeDtypeStruct(control.shape, F32),
        in_specs=[SMEM, VMEM, VMEM, VMEM],
        out_specs=VMEM,
        compiler_params=limit(8),
    )(core.reshape(1), control, own, other)


def partner(value, bit):
    count = lax.axis_size("ens")
    return lax.ppermute(value, "ens", [(i, i ^ bit) for i in range(count)])


def on_device(checkpoints, section_index, targets, sea_mask, basis_rows, basis_cols, control):
    members = lax.axis_size("ens")
    slabs = lax.axis_size("space")
    member = lax.axis_index("ens").astype(jnp.int32)
    slab = lax.axis_index("space").astype(jnp.int32)
    core = member & 1
    chip = member >> 1
    rows_out, width = control.shape
    rows = basis_rows.shape[0]
    quarter = width // members
    half = width // 2
    single = rows // 4

    pieces = pieces_for(member, basis_rows, control, slabs, quarter)
    pieces = lax.all_to_all(pieces, "space", 0, 0)
    up, down = edge_messages(section_index, checkpoints, targets, sea_mask)
    before = lax.ppermute(up, "space", [(i, i + 1) for i in range(slabs - 1)])
    after = lax.ppermute(down, "space", [(i + 1, i) for i in range(slabs - 1)])
    push, pairs, near_rows = inner_pass(section_index, checkpoints, targets, sea_mask, basis_rows)
    own = coeffs_part(slab, near_rows, pieces)
    parts = [own]
    for bits in (1, 2, 3):
        parts.append(partner(own, bits))
    sea, ends, seen = fetched_ends(section_index, checkpoints, targets, sea_mask)
    first, ends, seen = seam_first_pass(
        section_index, checkpoints, targets, sea, ends, seen, before
    )
    push, pairs, mask = seam_last_pass(sea, ends, seen, before, after, first, push, pairs)
    keep, give = gradient_halves(member, parts, basis_cols, push, pairs, mask)

    keep = keep + partner(give, 1)
    own_rows = lax.dynamic_slice_in_dim(keep, chip * single, single, 0)
    give = lax.dynamic_slice_in_dim(keep, (1 - chip) * single, single, 0)
    arriving = partner(give, 2)
    cols = held(basis_cols)
    send = projected_pieces(own_rows, arriving, cols, members, slabs)
    got = lax.all_to_all(send.reshape(members * slabs, single, half), ("space", "ens"), 0, 0)
    projected_half = got.reshape(slabs * rows, half)

    part = pieces[:, rows_out : rows_out + rows, :].reshape(slabs, 2, members // 2, single, quarter)
    part = part.transpose(0, 2, 1, 3, 4).reshape(slabs * rows, quarter)
    far = partner(part, 2)
    near = partner(part, 1)
    both = partner(far, 1)
    basis, kept = assembled(member, part, far, near, both, control)
    block = gradient_block(slab, basis, projected_half, rows_out)
    other = partner(block, 1)
    return updated(core, kept, block, other)


def solution(mesh):
    return jax.shard_map(
        on_device,
        mesh=mesh,
        in_specs=(
            P("ens", None, None, "space", None),
            P("ens"),
            P("ens", "space", None),
            P("space", None),
            P("space", None),
            P(),
            P("space", None),
        ),
        out_specs=P("space", None),
        check_vma=False,
    )
```
